128 devices in a mesh: gx: 4 (over x), gy: 8 (over y_hi, z), gz: 4 (over y_lo, core).
Axes of the slice: x: 4, y: 4 (y_hi: 2, y_lo: 2; y = y_hi * 2 + y_lo), z: 4, core: 2. Of those that a mesh axis runs over, the one named last changes fastest.
Arguments:
- intensity: float32 [32, 64, 512], P('gx', 'gy', 'gz'), may hold values from -6 to 6
- cotangent: float32 [32, 64, 512], P('gx', 'gy', 'gz'), may hold values from -6 to 6
- departure_cells: int32 [2, 2, 3, 32, 64, 512], P(None, None, None, 'gx', 'gy', 'gz'), may hold values from -2 to 2
- departure_fracs: float32 [2, 2, 3, 32, 64, 512], P(None, None, None, 'gx', 'gy', 'gz'), may hold values from 0 to 1
Outputs:
- intensity_adjoint: float32 [32, 64, 512], P('gx', 'gy', 'gz')
- velocity_adjoint: float32 [3, 32, 64, 512], P(None, 'gx', 'gy', 'gz')
The draws below stay inside these ranges and needn't reach their ends.
All inputs are finite; a program needn't handle non-finite values.
Results may differ from the reference program's by a relative error of at most 0.00002.
Values sent between devices are 32-bit elements; how exact they have to be, the bound alone decides.
A program may use at most 128 MiB of HBM per device.

```python
import jax
import jax.numpy as jnp

MARGIN = 4
STEPS = 2
SECTIONS = 2
NX = 32
NY = 64
NZ = 512


def place_ends(entries, stream_key, least, largest):
    longest = entries.shape.index(max(entries.shape))
    spots = []
    for shift in (0, 1):
        where = [jax.random.randint(jax.random.fold_in(stream_key, axis), (), 0, length) for axis, length in enumerate(entries.shape)]
        where[longest] = (where[longest] + shift) % entries.shape[longest]
        spots.append(tuple(where))
    return entries.at[spots[0]].set(least).at[spots[1]].set(largest)


def shard_levels(rng, dims, pieces, least, largest):
    def one(position, blocks):
        heights = jax.random.uniform(jax.random.fold_in(jax.random.fold_in(rng, 6), position), (blocks,), jnp.float32, least / len(pieces), largest / len(pieces))
        return jnp.repeat(jnp.exp(heights), dims[position] // blocks).reshape((-1,) + (1,) * (len(dims) - position - 1))

    level = one(*pieces[0])
    for cut in pieces[1:]:
        level = level * one(*cut)
    return level


def bell_draw(stream_key, shape, scale, reach, pieces=(), held_as=jnp.bfloat16):
    array = scale * jax.random.normal(stream_key, shape, jnp.float32)
    if pieces:
        array = array * shard_levels(stream_key, shape, pieces, -0.22, 0.18)
    return jnp.clip(array, -reach, reach).astype(held_as)


def setup_inputs(seed: int = 0) -> dict:
    keys = jax.random.split(jax.random.key(seed), 5)
    return {
        "intensity": bell_draw(keys[0], (NX, NY, NZ), 1.0, 6.0, ((0, 4), (1, 8), (2, 4)), jnp.float32),
        "cotangent": bell_draw(keys[1], (NX, NY, NZ), 1.0, 6.0, ((0, 4), (1, 8), (2, 4)), jnp.float32),
        "departure_cells": place_ends(jax.random.randint(keys[2], (STEPS, SECTIONS, 3, NX, NY, NZ), -2, 3), jax.random.fold_in(keys[2], 1), -2, 2).astype(jnp.int32),
        "departure_fracs": jnp.clip(1.0 * jax.random.uniform(keys[3], (STEPS, SECTIONS, 3, NX, NY, NZ), jnp.float32) ** shard_levels(keys[3], (STEPS, SECTIONS, 3, NX, NY, NZ), ((3, 4), (4, 8), (5, 4)), -0.2, 0.2), 0.0, 1.0),
    }


def cubic_taps(fraction):
    fraction_squared = fraction * fraction
    fraction_cubed = fraction_squared * fraction
    weights = [0.5 * (2.0 * fraction_squared - fraction_cubed - fraction), 0.5 * (3.0 * fraction_cubed - 5.0 * fraction_squared + 2.0), 0.5 * (4.0 * fraction_squared - 3.0 * fraction_cubed + fraction), 0.5 * (fraction_cubed - fraction_squared)]
    slopes = [0.5 * (4.0 * fraction - 3.0 * fraction_squared - 1.0), 0.5 * (9.0 * fraction_squared - 10.0 * fraction), 0.5 * (8.0 * fraction - 9.0 * fraction_squared + 1.0), 0.5 * (3.0 * fraction_squared - 2.0 * fraction)]
    return (weights, slopes)

def shift_table(offsets, taps):
    layers = []
    for target in range(-3, 5):
        summed = jnp.zeros(offsets.shape, jnp.float32)
        for tap_index in range(4):
            summed = summed + jnp.where(offsets + (tap_index - 1) == target, taps[tap_index], 0.0)
        layers.append(summed)
    return jnp.stack(layers)

def build_tables(cell_part, fraction_part, with_slopes):
    weight_tables = []
    slope_tables = []
    for component in range(3):
        weights, slopes = cubic_taps(fraction_part[component])
        weight_tables.append(shift_table(cell_part[component], weights))
        if with_slopes:
            slope_tables.append(shift_table(cell_part[component], slopes))
    return (weight_tables, slope_tables)

def sample(padded, weight_tables, slope_tables, with_value):
    table_x, table_y, table_z = weight_tables
    with_slopes = len(slope_tables) > 0
    extent_x, extent_y, extent_z = table_x.shape[1:]
    offset_base = MARGIN - 3
    shape_out = (padded.shape[0],) + table_x.shape[1:]
    sampled = jnp.zeros(shape_out, jnp.float32)
    grad_x = jnp.zeros(shape_out, jnp.float32)
    grad_y = jnp.zeros(shape_out, jnp.float32)
    grad_z = jnp.zeros(shape_out, jnp.float32)
    for shift_x in range(8):
        for shift_y in range(8):
            slab_rows = padded[:, offset_base + shift_x:offset_base + shift_x + extent_x, offset_base + shift_y:offset_base + shift_y + extent_y, :]
            column = jnp.zeros(shape_out, jnp.float32)
            slope_column = jnp.zeros(shape_out, jnp.float32)
            for shift_z in range(8):
                window = slab_rows[:, :, :, offset_base + shift_z:offset_base + shift_z + extent_z]
                column = column + table_z[shift_z] * window
                if with_slopes:
                    slope_column = slope_column + slope_tables[2][shift_z] * window
            plane_weight = table_x[shift_x] * table_y[shift_y]
            if with_value:
                sampled = sampled + plane_weight * column
            if with_slopes:
                grad_x = grad_x + slope_tables[0][shift_x] * table_y[shift_y] * column
                grad_y = grad_y + table_x[shift_x] * slope_tables[1][shift_y] * column
                grad_z = grad_z + plane_weight * slope_column
    return (sampled, jnp.concatenate([grad_x, grad_y, grad_z]))

def periodic(field):
    return jnp.pad(field, ((0, 0), (MARGIN, MARGIN), (MARGIN, MARGIN), (MARGIN, MARGIN)), mode='wrap')

def spread(field, weight_tables):
    zeros_field = jnp.zeros(field.shape, jnp.float32)
    _, pullback = jax.vjp(lambda inner: sample(periodic(inner), weight_tables, [], True)[0], zeros_field)
    return pullback(field)[0]

def reference(intensity, cotangent, departure_cells, departure_fracs):
    early_dep = build_tables(departure_cells[0, 1], departure_fracs[0, 1], True)
    late_dep = build_tables(departure_cells[1, 1], departure_fracs[1, 1], True)
    early_mid = build_tables(departure_cells[0, 0], departure_fracs[0, 0], False)
    late_mid = build_tables(departure_cells[1, 0], departure_fracs[1, 0], False)
    image_mid, grad_early = sample(periodic(intensity[None]), early_dep[0], early_dep[1], True)
    _, grad_late = sample(periodic(image_mid), late_dep[0], late_dep[1], False)
    grad_late = cotangent[None] * grad_late
    adjoint_mid = spread(cotangent[None], late_dep[0])
    grad_early = adjoint_mid * grad_early
    intensity_adjoint = spread(adjoint_mid, early_dep[0])[0]
    velocity_adjoint = spread(grad_late, late_mid[0]) + spread(grad_early, early_mid[0])
    return (intensity_adjoint, velocity_adjoint)
```

```python
import functools

import jax
import jax.numpy as jnp
from jax import lax
from jax.experimental import pallas as pl
from jax.experimental.pallas import tpu as pltpu
from jax.sharding import PartitionSpec as P

MARGIN = 4
SHIFTS = 8
AXES = (("gx", 0), ("gy", 1), ("gz", 2))


def cubic_taps(fraction):
    fraction_squared = fraction * fraction
    fraction_cubed = fraction_squared * fraction
    weights = [
        0.5 * (2.0 * fraction_squared - fraction_cubed - fraction),
        0.5 * (3.0 * fraction_cubed - 5.0 * fraction_squared + 2.0),
        0.5 * (4.0 * fraction_squared - 3.0 * fraction_cubed + fraction),
        0.5 * (fraction_cubed - fraction_squared),
    ]
    slopes = [
        0.5 * (4.0 * fraction - 3.0 * fraction_squared - 1.0),
        0.5 * (9.0 * fraction_squared - 10.0 * fraction),
        0.5 * (8.0 * fraction - 9.0 * fraction_squared + 1.0),
        0.5 * (3.0 * fraction_squared - 2.0 * fraction),
    ]
    return (weights, slopes)


def build_tables(cells_ref, fracs_ref, step, section, weight_refs, slope_refs):
    for component in range(3):
        offsets = cells_ref[step, section, component]
        weights, slopes = cubic_taps(fracs_ref[step, section, component])
        for shift in range(SHIFTS):
            target = shift - 3
            summed = jnp.zeros(offsets.shape, jnp.float32)
            slope_sum = jnp.zeros(offsets.shape, jnp.float32)
            for tap_index in range(4):
                hit = offsets + (tap_index - 1) == target
                summed = summed + jnp.where(hit, weights[tap_index], 0.0)
                if slope_refs is not None:
                    slope_sum = slope_sum + jnp.where(hit, slopes[tap_index], 0.0)
            weight_refs[component][shift] = summed
            if slope_refs is not None:
                slope_refs[component][shift] = slope_sum


def roll_lanes(field, shift):
    shift = shift % field.shape[-1]
    if shift == 0:
        return field
    return pltpu.roll(field, shift, field.ndim - 1)


def sample_block(wrapped_ref, rolled_ref, window_ref, weight_refs, slope_refs, with_value):
    px, py, pz = wrapped_ref.shape
    nx, ny, nz = px - 2 * MARGIN, py - 2 * MARGIN, window_ref.shape[-1]
    field = wrapped_ref[...]
    for sz in range(SHIFTS):
        rolled_ref[...] = roll_lanes(field, 3 - sz)[:, :, :nz]
        for sy in range(SHIFTS):
            window_ref[sy, sz] = rolled_ref[:, sy + 1 : sy + 1 + ny, :]
    table_x, table_y, table_z = weight_refs
    shape = (nx, ny, nz)
    value = jnp.zeros(shape, jnp.float32)
    grad_x = jnp.zeros(shape, jnp.float32)
    grad_y = jnp.zeros(shape, jnp.float32)
    grad_z = jnp.zeros(shape, jnp.float32)
    for sy in range(SHIFTS):
        along_x = jnp.zeros(shape, jnp.float32)
        along_x_slope = jnp.zeros(shape, jnp.float32)
        along_x_zslope = jnp.zeros(shape, jnp.float32)
        for sx in range(SHIFTS):
            column = jnp.zeros(shape, jnp.float32)
            slope_column = jnp.zeros(shape, jnp.float32)
            for sz in range(SHIFTS):
                window = window_ref[sy, sz, sx + 1 : sx + 1 + nx]
                column = column + table_z[sz] * window
                if slope_refs is not None:
                    slope_column = slope_column + slope_refs[2][sz] * window
            along_x = along_x + table_x[sx] * column
            if slope_refs is not None:
                along_x_slope = along_x_slope + slope_refs[0][sx] * column
                along_x_zslope = along_x_zslope + table_x[sx] * slope_column
        weight_y = table_y[sy]
        if with_value:
            value = value + weight_y * along_x
        if slope_refs is not None:
            grad_x = grad_x + weight_y * along_x_slope
            grad_y = grad_y + slope_refs[1][sy] * along_x
            grad_z = grad_z + weight_y * along_x_zslope
    return value, (grad_x, grad_y, grad_z)


def spread_block(field, weight_refs, product_ref, staged_ref, pz):
    table_x, table_y, table_z = weight_refs
    nx, ny, nz = field.shape
    px, py = nx + 2 * MARGIN, ny + 2 * MARGIN
    for sy in range(SHIFTS):
        weighted = table_y[sy] * field
        for sx in range(SHIFTS):
            product_ref[sy, sx] = table_x[sx] * weighted
    total = jnp.zeros((px, py, pz), jnp.float32)
    for sz in range(SHIFTS):
        weight_z = table_z[sz]
        for sy in range(SHIFTS):
            rows = [None] * px
            for sx in range(SHIFTS):
                deposit = weight_z * product_ref[sy, sx]
                for x in range(nx):
                    slot = x + sx + 1
                    rows[slot] = deposit[x] if rows[slot] is None else rows[slot] + deposit[x]
            rows[0] = jnp.zeros((ny, nz), jnp.float32)
            for slot in range(px):
                staged_ref[sy, slot, 8 : 8 + ny, :] = rows[slot]
        summed = jnp.zeros((px, py, nz), jnp.float32)
        for sy in range(SHIFTS):
            summed = summed + staged_ref[sy, :, 7 - sy : 7 - sy + py, :]
        padded = jnp.concatenate([summed, jnp.zeros((px, py, pz - nz), jnp.float32)], axis=2)
        total = total + roll_lanes(padded, sz - 3)
    return total


def table_scratch(shape, count):
    return [pltpu.VMEM((SHIFTS,) + shape, jnp.float32) for _ in range(count)]


def clear_rims(staged_ref):
    staged_ref[...] = jnp.zeros(staged_ref.shape, jnp.float32)


def early_sample_kernel(wrapped_ref, cells_ref, fracs_ref, image_ref, grad_ref,
                        rolled_ref, window_ref, *tables):
    weights, slopes = tables[:3], tables[3:]
    build_tables(cells_ref, fracs_ref, 0, 1, weights, slopes)
    value, grads = sample_block(wrapped_ref, rolled_ref, window_ref, weights, slopes, True)
    image_ref[...] = value
    for component in range(3):
        grad_ref[component] = grads[component]


def late_spread_kernel(cot_ref, cells_ref, fracs_ref, out_ref, product_ref, staged_ref, *tables):
    build_tables(cells_ref, fracs_ref, 1, 1, tables, None)
    clear_rims(staged_ref)
    out_ref[...] = spread_block(cot_ref[...], tables, product_ref, staged_ref, out_ref.shape[-1])


def late_velocity_kernel(wrapped_ref, cot_ref, cells_ref, fracs_ref, out_ref,
                         rolled_ref, window_ref, product_ref, staged_ref, *tables):
    weights, slopes, mid = tables[:3], tables[3:6], tables[6:]
    build_tables(cells_ref, fracs_ref, 1, 1, weights, slopes)
    build_tables(cells_ref, fracs_ref, 1, 0, mid, None)
    _, grads = sample_block(wrapped_ref, rolled_ref, window_ref, weights, slopes, False)
    cot = cot_ref[...]
    clear_rims(staged_ref)
    for component in range(3):
        out_ref[component] = spread_block(cot * grads[component], mid, product_ref, staged_ref,
                                          out_ref.shape[-1])


def early_spread_kernel(adjoint_ref, grad_ref, cells_ref, fracs_ref, out_ref,
                        product_ref, staged_ref, *tables):
    dep, mid = tables[:3], tables[3:]
    build_tables(cells_ref, fracs_ref, 0, 1, dep, None)
    build_tables(cells_ref, fracs_ref, 0, 0, mid, None)
    adjoint = adjoint_ref[...]
    clear_rims(staged_ref)
    pz = out_ref.shape[-1]
    out_ref[0] = spread_block(adjoint, dep, product_ref, staged_ref, pz)
    for component in range(3):
        out_ref[1 + component] = spread_block(adjoint * grad_ref[component], mid, product_ref,
                                              staged_ref, pz)


def vmem_call(kernel, out_shapes, scratch, *args):
    return pl.pallas_call(
        kernel,
        out_shape=out_shapes,
        in_specs=[pl.BlockSpec(memory_space=pltpu.VMEM)] * len(args),
        out_specs=jax.tree.map(lambda _: pl.BlockSpec(memory_space=pltpu.VMEM), out_shapes),
        scratch_shapes=scratch,
        compiler_params=pltpu.CompilerParams(vmem_limit_bytes=48 * 1024 * 1024),
    )(*args)


def shift_from(piece, axis, upward):
    count = lax.axis_size(axis)
    if upward:
        pairs = [(i, (i + 1) % count) for i in range(count)]
    else:
        pairs = [((i + 1) % count, i) for i in range(count)]
    return lax.ppermute(piece, axis, pairs)


def widen(block, pz):
    for axis, dim in AXES[:2]:
        size = block.shape[dim]
        head = lax.slice_in_dim(block, 0, MARGIN, axis=dim)
        tail = lax.slice_in_dim(block, size - MARGIN, size, axis=dim)
        block = jnp.concatenate(
            [shift_from(tail, axis, True), block, shift_from(head, axis, False)], axis=dim
        )
    nz = block.shape[2]
    head = block[:, :, :MARGIN]
    tail = block[:, :, nz - MARGIN :]
    gap = jnp.zeros(block.shape[:2] + (pz - nz - 2 * MARGIN,), jnp.float32)
    return jnp.concatenate(
        [block, shift_from(head, "gz", False), gap, shift_from(tail, "gz", True)], axis=2
    )


def fold(wrapped, nz):
    pz = wrapped.shape[3]
    upper = wrapped[..., nz : nz + MARGIN]
    lower = wrapped[..., pz - MARGIN :]
    block = wrapped[..., :nz]
    from_below = shift_from(upper, "gz", True)
    from_above = shift_from(lower, "gz", False)
    block = block.at[..., :MARGIN].add(from_below)
    block = block.at[..., nz - MARGIN :].add(from_above)
    for axis, dim in (("gy", 2), ("gx", 1)):
        size = block.shape[dim] - 2 * MARGIN
        low = lax.slice_in_dim(block, 0, MARGIN, axis=dim)
        high = lax.slice_in_dim(block, size + MARGIN, size + 2 * MARGIN, axis=dim)
        block = lax.slice_in_dim(block, MARGIN, size + MARGIN, axis=dim)
        got_low = shift_from(high, axis, True)
        got_high = shift_from(low, axis, False)
        lead = (slice(None),) * dim
        block = block.at[lead + (slice(0, MARGIN),)].add(got_low)
        block = block.at[lead + (slice(size - MARGIN, size),)].add(got_high)
    return block


def body(intensity, cotangent, departure_cells, departure_fracs):
    cells = departure_cells
    fracs = departure_fracs
    nx, ny, nz = intensity.shape
    px, py, pz = nx + 2 * MARGIN, ny + 2 * MARGIN, nz + 128
    block = (nx, ny, nz)
    f32 = jnp.float32
    rolled = pltpu.VMEM((px, py, nz), f32)
    windows = pltpu.VMEM((SHIFTS, SHIFTS, px, ny, nz), f32)
    products = pltpu.VMEM((SHIFTS, SHIFTS) + block, f32)
    staged = pltpu.VMEM((SHIFTS, px, ny + 16, nz), f32)

    wrapped = widen(intensity, pz)
    image_mid, grad_raw = vmem_call(
        early_sample_kernel,
        (jax.ShapeDtypeStruct(block, f32), jax.ShapeDtypeStruct((3,) + block, f32)),
        [rolled, windows] + table_scratch(block, 6),
        wrapped, cells, fracs,
    )
    adjoint_padded = vmem_call(
        late_spread_kernel,
        jax.ShapeDtypeStruct((px, py, pz), f32),
        [products, staged] + table_scratch(block, 3),
        cotangent, cells, fracs,
    )
    wrapped_mid = widen(image_mid, pz)
    velocity_padded = vmem_call(
        late_velocity_kernel,
        jax.ShapeDtypeStruct((3, px, py, pz), f32),
        [rolled, windows, products, staged] + table_scratch(block, 9),
        wrapped_mid, cotangent, cells, fracs,
    )
    folded = fold(jnp.concatenate([adjoint_padded[None], velocity_padded]), nz)
    adjoint_mid = folded[0]
    velocity_late = folded[1:]
    early_padded = vmem_call(
        early_spread_kernel,
        jax.ShapeDtypeStruct((4, px, py, pz), f32),
        [products, staged] + table_scratch(block, 6),
        adjoint_mid, grad_raw, cells, fracs,
    )
    folded = fold(early_padded, nz)
    return (folded[0], velocity_late + folded[1:])


def solution(mesh):
    in_specs = (
        P("gx", "gy", "gz"),
        P("gx", "gy", "gz"),
        P(None, None, None, "gx", "gy", "gz"),
        P(None, None, None, "gx", "gy", "gz"),
    )
    out_specs = (P("gx", "gy", "gz"), P(None, "gx", "gy", "gz"))
    return jax.shard_map(body, mesh=mesh, in_specs=in_specs, out_specs=out_specs, check_vma=False)
```

```python
import functools

import jax
import jax.numpy as jnp
from jax import lax
from jax.experimental import pallas as pl
from jax.experimental.pallas import tpu as pltpu
from jax.sharding import PartitionSpec as P

MARGIN = 4
SHIFTS = 8
AXES = (("gx", 0), ("gy", 1), ("gz", 2))


def cubic_taps(fraction):
    fraction_squared = fraction * fraction
    fraction_cubed = fraction_squared * fraction
    weights = [
        0.5 * (2.0 * fraction_squared - fraction_cubed - fraction),
        0.5 * (3.0 * fraction_cubed - 5.0 * fraction_squared + 2.0),
        0.5 * (4.0 * fraction_squared - 3.0 * fraction_cubed + fraction),
        0.5 * (fraction_cubed - fraction_squared),
    ]
    slopes = [
        0.5 * (4.0 * fraction - 3.0 * fraction_squared - 1.0),
        0.5 * (9.0 * fraction_squared - 10.0 * fraction),
        0.5 * (8.0 * fraction - 9.0 * fraction_squared + 1.0),
        0.5 * (3.0 * fraction_squared - 2.0 * fraction),
    ]
    return (weights, slopes)


def build_tables(cells_ref, fracs_ref, step, section, weight_refs, slope_refs):
    for component in range(3):
        offsets = cells_ref[step, section, component]
        weights, slopes = cubic_taps(fracs_ref[step, section, component])
        for shift in range(SHIFTS):
            target = shift - 3
            summed = jnp.zeros(offsets.shape, jnp.float32)
            slope_sum = jnp.zeros(offsets.shape, jnp.float32)
            for tap_index in range(4):
                hit = offsets + (tap_index - 1) == target
                summed = summed + jnp.where(hit, weights[tap_index], 0.0)
                if slope_refs is not None:
                    slope_sum = slope_sum + jnp.where(hit, slopes[tap_index], 0.0)
            weight_refs[component][shift] = summed
            if slope_refs is not None:
                slope_refs[component][shift] = slope_sum


def roll_lanes(field, shift):
    shift = shift % field.shape[-1]
    if shift == 0:
        return field
    return pltpu.roll(field, shift, field.ndim - 1)


def sample_block(wrapped_ref, rolled_ref, window_ref, weight_refs, slope_refs, with_value):
    px, py, pz = wrapped_ref.shape
    nx, ny, nz = px - 2 * MARGIN, py - 2 * MARGIN, window_ref.shape[-1]
    field = wrapped_ref[...]
    for sz in range(SHIFTS):
        rolled_ref[...] = roll_lanes(field, 3 - sz)[:, :, :nz]
        for sy in range(SHIFTS):
            window_ref[sy, sz] = rolled_ref[:, sy + 1 : sy + 1 + ny, :]
    table_x, table_y, table_z = weight_refs
    shape = (nx, ny, nz)
    value = jnp.zeros(shape, jnp.float32)
    grad_x = jnp.zeros(shape, jnp.float32)
    grad_y = jnp.zeros(shape, jnp.float32)
    grad_z = jnp.zeros(shape, jnp.float32)
    for sy in range(SHIFTS):
        along_x = jnp.zeros(shape, jnp.float32)
        along_x_slope = jnp.zeros(shape, jnp.float32)
        along_x_zslope = jnp.zeros(shape, jnp.float32)
        for sx in range(SHIFTS):
            column = jnp.zeros(shape, jnp.float32)
            slope_column = jnp.zeros(shape, jnp.float32)
            for sz in range(SHIFTS):
                window = window_ref[sy, sz, sx + 1 : sx + 1 + nx]
                column = column + table_z[sz] * window
                if slope_refs is not None:
                    slope_column = slope_column + slope_refs[2][sz] * window
            along_x = along_x + table_x[sx] * column
            if slope_refs is not None:
                along_x_slope = along_x_slope + slope_refs[0][sx] * column
                along_x_zslope = along_x_zslope + table_x[sx] * slope_column
        weight_y = table_y[sy]
        if with_value:
            value = value + weight_y * along_x
        if slope_refs is not None:
            grad_x = grad_x + weight_y * along_x_slope
            grad_y = grad_y + slope_refs[1][sy] * along_x
            grad_z = grad_z + weight_y * along_x_zslope
    return value, (grad_x, grad_y, grad_z)


def spread_block(field, weight_refs, product_ref, staged_ref, pz):
    table_x, table_y, table_z = weight_refs
    nx, ny, nz = field.shape
    px, py = nx + 2 * MARGIN, ny + 2 * MARGIN
    for sy in range(SHIFTS):
        weighted = table_y[sy] * field
        for sx in range(SHIFTS):
            product_ref[sy, sx] = table_x[sx] * weighted
    total = jnp.zeros((px, py, pz), jnp.float32)
    for sz in range(SHIFTS):
        weight_z = table_z[sz]
        for sy in range(SHIFTS):
            rows = [None] * px
            for sx in range(SHIFTS):
                deposit = weight_z * product_ref[sy, sx]
                for x in range(nx):
                    slot = x + sx + 1
                    rows[slot] = deposit[x] if rows[slot] is None else rows[slot] + deposit[x]
            rows[0] = jnp.zeros((ny, nz), jnp.float32)
            for slot in range(px):
                staged_ref[sy, slot, 8 : 8 + ny, :] = rows[slot]
        summed = jnp.zeros((px, py, nz), jnp.float32)
        for sy in range(SHIFTS):
            summed = summed + staged_ref[sy, :, 7 - sy : 7 - sy + py, :]
        padded = jnp.concatenate([summed, jnp.zeros((px, py, pz - nz), jnp.float32)], axis=2)
        total = total + roll_lanes(padded, sz - 3)
    return total


def table_scratch(shape, count):
    return [pltpu.VMEM((SHIFTS,) + shape, jnp.float32) for _ in range(count)]


def clear_rims(staged_ref):
    staged_ref[...] = jnp.zeros(staged_ref.shape, jnp.float32)


def early_sample_kernel(wrapped_ref, cells_ref, fracs_ref, image_ref, grad_ref,
                        rolled_ref, window_ref, *tables):
    weights, slopes = tables[:3], tables[3:]
    build_tables(cells_ref, fracs_ref, 0, 1, weights, slopes)
    value, grads = sample_block(wrapped_ref, rolled_ref, window_ref, weights, slopes, True)
    image_ref[...] = value
    for component in range(3):
        grad_ref[component] = grads[component]


def late_spread_kernel(cot_ref, cells_ref, fracs_ref, out_ref, product_ref, staged_ref, *tables):
    build_tables(cells_ref, fracs_ref, 1, 1, tables, None)
    clear_rims(staged_ref)
    out_ref[...] = spread_block(cot_ref[...], tables, product_ref, staged_ref, out_ref.shape[-1])


def late_velocity_kernel(wrapped_ref, cot_ref, cells_ref, fracs_ref, out_ref,
                         rolled_ref, window_ref, product_ref, staged_ref, *tables):
    weights, slopes, mid = tables[:3], tables[3:6], tables[6:]
    build_tables(cells_ref, fracs_ref, 1, 1, weights, slopes)
    build_tables(cells_ref, fracs_ref, 1, 0, mid, None)
    _, grads = sample_block(wrapped_ref, rolled_ref, window_ref, weights, slopes, False)
    cot = cot_ref[...]
    clear_rims(staged_ref)
    for component in range(3):
        out_ref[component] = spread_block(cot * grads[component], mid, product_ref, staged_ref,
                                          out_ref.shape[-1])


def early_spread_kernel(adjoint_ref, grad_ref, cells_ref, fracs_ref, out_ref,
                        product_ref, staged_ref, *tables):
    dep, mid = tables[:3], tables[3:]
    build_tables(cells_ref, fracs_ref, 0, 1, dep, None)
    build_tables(cells_ref, fracs_ref, 0, 0, mid, None)
    adjoint = adjoint_ref[...]
    clear_rims(staged_ref)
    pz = out_ref.shape[-1]
    out_ref[0] = spread_block(adjoint, dep, product_ref, staged_ref, pz)
    for component in range(3):
        out_ref[1 + component] = spread_block(adjoint * grad_ref[component], mid, product_ref,
                                              staged_ref, pz)


def vmem_call(kernel, out_shapes, scratch, *args):
    return pl.pallas_call(
        kernel,
        out_shape=out_shapes,
        in_specs=[pl.BlockSpec(memory_space=pltpu.VMEM)] * len(args),
        out_specs=jax.tree.map(lambda _: pl.BlockSpec(memory_space=pltpu.VMEM), out_shapes),
        scratch_shapes=scratch,
        compiler_params=pltpu.CompilerParams(vmem_limit_bytes=48 * 1024 * 1024),
    )(*args)


def shift_from(piece, axis, upward):
    count = lax.axis_size(axis)
    if upward:
        pairs = [(i, (i + 1) % count) for i in range(count)]
    else:
        pairs = [((i + 1) % count, i) for i in range(count)]
    return lax.ppermute(piece, axis, pairs)


def widen(block, pz):
    for axis, dim in AXES[:2]:
        size = block.shape[dim]
        head = lax.slice_in_dim(block, 0, MARGIN, axis=dim)
        tail = lax.slice_in_dim(block, size - MARGIN, size, axis=dim)
        block = jnp.concatenate(
            [shift_from(tail, axis, True), block, shift_from(head, axis, False)], axis=dim
        )
    nz = block.shape[2]
    head = block[:, :, :MARGIN]
    tail = block[:, :, nz - MARGIN :]
    gap = jnp.zeros(block.shape[:2] + (pz - nz - 2 * MARGIN,), jnp.float32)
    return jnp.concatenate(
        [block, shift_from(head, "gz", False), gap, shift_from(tail, "gz", True)], axis=2
    )


def place_rim(rim, dim, start, size):
    widths = [(0, 0)] * rim.ndim
    widths[dim] = (start, size - start - rim.shape[dim])
    return jnp.pad(rim, widths)


def fold(wrapped, nz):
    pz = wrapped.shape[3]
    upper = wrapped[..., nz : nz + MARGIN]
    lower = wrapped[..., pz - MARGIN :]
    block = wrapped[..., :nz]
    from_below = shift_from(upper, "gz", True)
    from_above = shift_from(lower, "gz", False)
    block = block + place_rim(from_below, 3, 0, nz)
    block = block + place_rim(from_above, 3, nz - MARGIN, nz)
    for axis, dim in (("gy", 2), ("gx", 1)):
        size = block.shape[dim] - 2 * MARGIN
        low = lax.slice_in_dim(block, 0, MARGIN, axis=dim)
        high = lax.slice_in_dim(block, size + MARGIN, size + 2 * MARGIN, axis=dim)
        block = lax.slice_in_dim(block, MARGIN, size + MARGIN, axis=dim)
        got_low = shift_from(high, axis, True)
        got_high = shift_from(low, axis, False)
        block = block + place_rim(got_low, dim, 0, size)
        block = block + place_rim(got_high, dim, size - MARGIN, size)
    return block


def body(intensity, cotangent, departure_cells, departure_fracs):
    cells = departure_cells
    fracs = departure_fracs
    nx, ny, nz = intensity.shape
    px, py, pz = nx + 2 * MARGIN, ny + 2 * MARGIN, nz + 128
    block = (nx, ny, nz)
    f32 = jnp.float32
    rolled = pltpu.VMEM((px, py, nz), f32)
    windows = pltpu.VMEM((SHIFTS, SHIFTS, px, ny, nz), f32)
    products = pltpu.VMEM((SHIFTS, SHIFTS) + block, f32)
    staged = pltpu.VMEM((SHIFTS, px, ny + 16, nz), f32)

    wrapped = widen(intensity, pz)
    image_mid, grad_raw = vmem_call(
        early_sample_kernel,
        (jax.ShapeDtypeStruct(block, f32), jax.ShapeDtypeStruct((3,) + block, f32)),
        [rolled, windows] + table_scratch(block, 6),
        wrapped, cells, fracs,
    )
    adjoint_padded = vmem_call(
        late_spread_kernel,
        jax.ShapeDtypeStruct((px, py, pz), f32),
        [products, staged] + table_scratch(block, 3),
        cotangent, cells, fracs,
    )
    wrapped_mid = widen(image_mid, pz)
    velocity_padded = vmem_call(
        late_velocity_kernel,
        jax.ShapeDtypeStruct((3, px, py, pz), f32),
        [rolled, windows, products, staged] + table_scratch(block, 9),
        wrapped_mid, cotangent, cells, fracs,
    )
    folded = fold(jnp.concatenate([adjoint_padded[None], velocity_padded]), nz)
    adjoint_mid = folded[0]
    velocity_late = folded[1:]
    early_padded = vmem_call(
        early_spread_kernel,
        jax.ShapeDtypeStruct((4, px, py, pz), f32),
        [products, staged] + table_scratch(block, 6),
        adjoint_mid, grad_raw, cells, fracs,
    )
    folded = fold(early_padded, nz)
    return (folded[0], velocity_late + folded[1:])


def solution(mesh):
    in_specs = (
        P("gx", "gy", "gz"),
        P("gx", "gy", "gz"),
        P(None, None, None, "gx", "gy", "gz"),
        P(None, None, None, "gx", "gy", "gz"),
    )
    out_specs = (P("gx", "gy", "gz"), P(None, "gx", "gy", "gz"))
    return jax.shard_map(body, mesh=mesh, in_specs=in_specs, out_specs=out_specs, check_vma=False)
```

```python
import functools

import jax
import jax.numpy as jnp
from jax import lax
from jax.experimental import pallas as pl
from jax.experimental.pallas import tpu as pltpu
from jax.sharding import PartitionSpec as P

MARGIN = 4
SHIFTS = 8
AXES = (("gx", 0), ("gy", 1), ("gz", 2))


def cubic_taps(fraction):
    fraction_squared = fraction * fraction
    fraction_cubed = fraction_squared * fraction
    weights = [
        0.5 * (2.0 * fraction_squared - fraction_cubed - fraction),
        0.5 * (3.0 * fraction_cubed - 5.0 * fraction_squared + 2.0),
        0.5 * (4.0 * fraction_squared - 3.0 * fraction_cubed + fraction),
        0.5 * (fraction_cubed - fraction_squared),
    ]
    slopes = [
        0.5 * (4.0 * fraction - 3.0 * fraction_squared - 1.0),
        0.5 * (9.0 * fraction_squared - 10.0 * fraction),
        0.5 * (8.0 * fraction - 9.0 * fraction_squared + 1.0),
        0.5 * (3.0 * fraction_squared - 2.0 * fraction),
    ]
    return (weights, slopes)


def build_tables(cells_ref, fracs_ref, step, section, weight_refs, slope_refs):
    for component in range(3):
        offsets = cells_ref[step, section, component]
        weights, slopes = cubic_taps(fracs_ref[step, section, component])
        for shift in range(SHIFTS):
            target = shift - 3
            summed = jnp.zeros(offsets.shape, jnp.float32)
            slope_sum = jnp.zeros(offsets.shape, jnp.float32)
            for tap_index in range(4):
                hit = offsets + (tap_index - 1) == target
                summed = summed + jnp.where(hit, weights[tap_index], 0.0)
                if slope_refs is not None:
                    slope_sum = slope_sum + jnp.where(hit, slopes[tap_index], 0.0)
            weight_refs[component][shift] = summed
            if slope_refs is not None:
                slope_refs[component][shift] = slope_sum


def roll_lanes(field, shift):
    shift = shift % field.shape[-1]
    if shift == 0:
        return field
    return pltpu.roll(field, shift, field.ndim - 1)


def sample_block(wrapped_ref, rolled_ref, window_ref, weight_refs, slope_refs, with_value):
    px, py, pz = wrapped_ref.shape
    nx, ny, nz = px - 2 * MARGIN, py - 2 * MARGIN, window_ref.shape[-1]
    field = wrapped_ref[...]
    for sz in range(SHIFTS):
        rolled_ref[...] = roll_lanes(field, 3 - sz)[:, :, :nz]
        for sy in range(SHIFTS):
            window_ref[sy, sz] = rolled_ref[:, sy + 1 : sy + 1 + ny, :]
    table_x, table_y, table_z = weight_refs
    shape = (nx, ny, nz)
    value = jnp.zeros(shape, jnp.float32)
    grad_x = jnp.zeros(shape, jnp.float32)
    grad_y = jnp.zeros(shape, jnp.float32)
    grad_z = jnp.zeros(shape, jnp.float32)
    for sy in range(SHIFTS):
        along_x = jnp.zeros(shape, jnp.float32)
        along_x_slope = jnp.zeros(shape, jnp.float32)
        along_x_zslope = jnp.zeros(shape, jnp.float32)
        for sx in range(SHIFTS):
            column = jnp.zeros(shape, jnp.float32)
            slope_column = jnp.zeros(shape, jnp.float32)
            for sz in range(SHIFTS):
                window = window_ref[sy, sz, sx + 1 : sx + 1 + nx]
                column = column + table_z[sz] * window
                if slope_refs is not None:
                    slope_column = slope_column + slope_refs[2][sz] * window
            along_x = along_x + table_x[sx] * column
            if slope_refs is not None:
                along_x_slope = along_x_slope + slope_refs[0][sx] * column
                along_x_zslope = along_x_zslope + table_x[sx] * slope_column
        weight_y = table_y[sy]
        if with_value:
            value = value + weight_y * along_x
        if slope_refs is not None:
            grad_x = grad_x + weight_y * along_x_slope
            grad_y = grad_y + slope_refs[1][sy] * along_x
            grad_z = grad_z + weight_y * along_x_zslope
    return value, (grad_x, grad_y, grad_z)


def spread_block(field, weight_refs, product_ref, staged_ref, pz):
    table_x, table_y, table_z = weight_refs
    nx, ny, nz = field.shape
    px, py = nx + 2 * MARGIN, ny + 2 * MARGIN
    for sy in range(SHIFTS):
        weighted = table_y[sy] * field
        for sx in range(SHIFTS):
            product_ref[sy, sx] = table_x[sx] * weighted
    total = jnp.zeros((px, py, pz), jnp.float32)
    for sz in range(SHIFTS):
        weight_z = table_z[sz]
        for sy in range(SHIFTS):
            rows = [None] * px
            for sx in range(SHIFTS):
                deposit = weight_z * product_ref[sy, sx]
                for x in range(nx):
                    slot = x + sx + 1
                    rows[slot] = deposit[x] if rows[slot] is None else rows[slot] + deposit[x]
            rows[0] = jnp.zeros((ny, nz), jnp.float32)
            for slot in range(px):
                staged_ref[sy, slot, 8 : 8 + ny, :] = rows[slot]
        summed = jnp.zeros((px, py, nz), jnp.float32)
        for sy in range(SHIFTS):
            summed = summed + staged_ref[sy, :, 7 - sy : 7 - sy + py, :]
        padded = jnp.concatenate([summed, jnp.zeros((px, py, pz - nz), jnp.float32)], axis=2)
        total = total + roll_lanes(padded, sz - 3)
    return total


def table_scratch(shape, count):
    return [pltpu.VMEM((SHIFTS,) + shape, jnp.float32) for _ in range(count)]


def clear_rims(staged_ref):
    staged_ref[...] = jnp.zeros(staged_ref.shape, jnp.float32)


def early_sample_kernel(wrapped_ref, cells_ref, fracs_ref, image_ref, grad_ref,
                        rolled_ref, window_ref, *tables):
    weights, slopes = tables[:3], tables[3:]
    build_tables(cells_ref, fracs_ref, 0, 1, weights, slopes)
    value, grads = sample_block(wrapped_ref, rolled_ref, window_ref, weights, slopes, True)
    image_ref[...] = value
    for component in range(3):
        grad_ref[component] = grads[component]


def late_spread_kernel(cot_ref, cells_ref, fracs_ref, out_ref, product_ref, staged_ref, *tables):
    build_tables(cells_ref, fracs_ref, 1, 1, tables, None)
    clear_rims(staged_ref)
    out_ref[...] = spread_block(cot_ref[...], tables, product_ref, staged_ref, out_ref.shape[-1])


def late_velocity_kernel(wrapped_ref, cot_ref, cells_ref, fracs_ref, out_ref,
                         rolled_ref, window_ref, product_ref, staged_ref, *tables):
    weights, slopes, mid = tables[:3], tables[3:6], tables[6:]
    build_tables(cells_ref, fracs_ref, 1, 1, weights, slopes)
    build_tables(cells_ref, fracs_ref, 1, 0, mid, None)
    _, grads = sample_block(wrapped_ref, rolled_ref, window_ref, weights, slopes, False)
    cot = cot_ref[...]
    clear_rims(staged_ref)
    for component in range(3):
        out_ref[component] = spread_block(cot * grads[component], mid, product_ref, staged_ref,
                                          out_ref.shape[-1])


def early_spread_kernel(adjoint_ref, grad_ref, cells_ref, fracs_ref, out_ref,
                        product_ref, staged_ref, *tables):
    dep, mid = tables[:3], tables[3:]
    build_tables(cells_ref, fracs_ref, 0, 1, dep, None)
    build_tables(cells_ref, fracs_ref, 0, 0, mid, None)
    adjoint = adjoint_ref[...]
    clear_rims(staged_ref)
    pz = out_ref.shape[-1]
    out_ref[0] = spread_block(adjoint, dep, product_ref, staged_ref, pz)
    for component in range(3):
        out_ref[1 + component] = spread_block(adjoint * grad_ref[component], mid, product_ref,
                                              staged_ref, pz)


def vmem_call(kernel, out_shapes, scratch, *args):
    return pl.pallas_call(
        kernel,
        out_shape=out_shapes,
        in_specs=[pl.BlockSpec(memory_space=pltpu.VMEM)] * len(args),
        out_specs=jax.tree.map(lambda _: pl.BlockSpec(memory_space=pltpu.VMEM), out_shapes),
        scratch_shapes=scratch,
        compiler_params=pltpu.CompilerParams(vmem_limit_bytes=48 * 1024 * 1024),
    )(*args)


def shift_from(piece, axis, upward):
    count = lax.axis_size(axis)
    if upward:
        pairs = [(i, (i + 1) % count) for i in range(count)]
    else:
        pairs = [((i + 1) % count, i) for i in range(count)]
    shape = piece.shape
    if shape[-1] < 128 and piece.size % 1024 == 0:
        flat = lax.ppermute(piece.reshape(-1, 128), axis, pairs)
        return flat.reshape(shape)
    return lax.ppermute(piece, axis, pairs)


def widen(block, pz):
    for axis, dim in AXES[:2]:
        size = block.shape[dim]
        head = lax.slice_in_dim(block, 0, MARGIN, axis=dim)
        tail = lax.slice_in_dim(block, size - MARGIN, size, axis=dim)
        block = jnp.concatenate(
            [shift_from(tail, axis, True), block, shift_from(head, axis, False)], axis=dim
        )
    nz = block.shape[2]
    head = block[:, :, :MARGIN]
    tail = block[:, :, nz - MARGIN :]
    gap = jnp.zeros(block.shape[:2] + (pz - nz - 2 * MARGIN,), jnp.float32)
    return jnp.concatenate(
        [block, shift_from(head, "gz", False), gap, shift_from(tail, "gz", True)], axis=2
    )


def place_rim(rim, dim, start, size):
    widths = [(0, 0)] * rim.ndim
    widths[dim] = (start, size - start - rim.shape[dim])
    return jnp.pad(rim, widths)


def fold(wrapped, nz):
    pz = wrapped.shape[3]
    upper = wrapped[..., nz : nz + MARGIN]
    lower = wrapped[..., pz - MARGIN :]
    block = wrapped[..., :nz]
    from_below = shift_from(upper, "gz", True)
    from_above = shift_from(lower, "gz", False)
    block = block + place_rim(from_below, 3, 0, nz)
    block = block + place_rim(from_above, 3, nz - MARGIN, nz)
    for axis, dim in (("gy", 2), ("gx", 1)):
        size = block.shape[dim] - 2 * MARGIN
        low = lax.slice_in_dim(block, 0, MARGIN, axis=dim)
        high = lax.slice_in_dim(block, size + MARGIN, size + 2 * MARGIN, axis=dim)
        block = lax.slice_in_dim(block, MARGIN, size + MARGIN, axis=dim)
        got_low = shift_from(high, axis, True)
        got_high = shift_from(low, axis, False)
        block = block + place_rim(got_low, dim, 0, size)
        block = block + place_rim(got_high, dim, size - MARGIN, size)
    return block


def body(intensity, cotangent, departure_cells, departure_fracs):
    cells = departure_cells
    fracs = departure_fracs
    nx, ny, nz = intensity.shape
    px, py, pz = nx + 2 * MARGIN, ny + 2 * MARGIN, nz + 128
    block = (nx, ny, nz)
    f32 = jnp.float32
    rolled = pltpu.VMEM((px, py, nz), f32)
    windows = pltpu.VMEM((SHIFTS, SHIFTS, px, ny, nz), f32)
    products = pltpu.VMEM((SHIFTS, SHIFTS) + block, f32)
    staged = pltpu.VMEM((SHIFTS, px, ny + 16, nz), f32)

    wrapped = widen(intensity, pz)
    image_mid, grad_raw = vmem_call(
        early_sample_kernel,
        (jax.ShapeDtypeStruct(block, f32), jax.ShapeDtypeStruct((3,) + block, f32)),
        [rolled, windows] + table_scratch(block, 6),
        wrapped, cells, fracs,
    )
    adjoint_padded = vmem_call(
        late_spread_kernel,
        jax.ShapeDtypeStruct((px, py, pz), f32),
        [products, staged] + table_scratch(block, 3),
        cotangent, cells, fracs,
    )
    wrapped_mid = widen(image_mid, pz)
    velocity_padded = vmem_call(
        late_velocity_kernel,
        jax.ShapeDtypeStruct((3, px, py, pz), f32),
        [rolled, windows, products, staged] + table_scratch(block, 9),
        wrapped_mid, cotangent, cells, fracs,
    )
    folded = fold(jnp.concatenate([adjoint_padded[None], velocity_padded]), nz)
    adjoint_mid = folded[0]
    velocity_late = folded[1:]
    early_padded = vmem_call(
        early_spread_kernel,
        jax.ShapeDtypeStruct((4, px, py, pz), f32),
        [products, staged] + table_scratch(block, 6),
        adjoint_mid, grad_raw, cells, fracs,
    )
    folded = fold(early_padded, nz)
    return (folded[0], velocity_late + folded[1:])


def solution(mesh):
    in_specs = (
        P("gx", "gy", "gz"),
        P("gx", "gy", "gz"),
        P(None, None, None, "gx", "gy", "gz"),
        P(None, None, None, "gx", "gy", "gz"),
    )
    out_specs = (P("gx", "gy", "gz"), P(None, "gx", "gy", "gz"))
    return jax.shard_map(body, mesh=mesh, in_specs=in_specs, out_specs=out_specs, check_vma=False)
```

```python
import functools

import jax
import jax.numpy as jnp
from jax import lax
from jax.experimental import pallas as pl
from jax.experimental.pallas import tpu as pltpu
from jax.sharding import PartitionSpec as P

MARGIN = 4
SHIFTS = 8
AXES = (("gx", 0), ("gy", 1), ("gz", 2))


def cubic_taps(fraction):
    fraction_squared = fraction * fraction
    fraction_cubed = fraction_squared * fraction
    weights = [
        0.5 * (2.0 * fraction_squared - fraction_cubed - fraction),
        0.5 * (3.0 * fraction_cubed - 5.0 * fraction_squared + 2.0),
        0.5 * (4.0 * fraction_squared - 3.0 * fraction_cubed + fraction),
        0.5 * (fraction_cubed - fraction_squared),
    ]
    slopes = [
        0.5 * (4.0 * fraction - 3.0 * fraction_squared - 1.0),
        0.5 * (9.0 * fraction_squared - 10.0 * fraction),
        0.5 * (8.0 * fraction - 9.0 * fraction_squared + 1.0),
        0.5 * (3.0 * fraction_squared - 2.0 * fraction),
    ]
    return (weights, slopes)


def build_tables(cells_ref, fracs_ref, step, section, weight_refs, slope_refs):
    for component in range(3):
        offsets = cells_ref[step, section, component]
        weights, slopes = cubic_taps(fracs_ref[step, section, component])
        for shift in range(SHIFTS):
            target = shift - 3
            summed = jnp.zeros(offsets.shape, jnp.float32)
            slope_sum = jnp.zeros(offsets.shape, jnp.float32)
            for tap_index in range(4):
                hit = offsets + (tap_index - 1) == target
                summed = summed + jnp.where(hit, weights[tap_index], 0.0)
                if slope_refs is not None:
                    slope_sum = slope_sum + jnp.where(hit, slopes[tap_index], 0.0)
            weight_refs[component][shift] = summed
            if slope_refs is not None:
                slope_refs[component][shift] = slope_sum


def roll_lanes(field, shift):
    shift = shift % field.shape[-1]
    if shift == 0:
        return field
    return pltpu.roll(field, shift, field.ndim - 1)


def sample_block(wrapped_ref, rolled_ref, window_ref, weight_refs, slope_refs, with_value):
    px, py, pz = wrapped_ref.shape
    nx, ny, nz = px - 2 * MARGIN, py - 2 * MARGIN, window_ref.shape[-1]
    field = wrapped_ref[...]
    for sz in range(SHIFTS):
        rolled_ref[...] = roll_lanes(field, 3 - sz)[:, :, :nz]
        for sy in range(SHIFTS):
            window_ref[sy, sz] = rolled_ref[:, sy + 1 : sy + 1 + ny, :]
    table_x, table_y, table_z = weight_refs
    shape = (nx, ny, nz)

    def along_y(sy, carry):
        value, grad_x, grad_y, grad_z = carry
        along_x = jnp.zeros(shape, jnp.float32)
        along_x_slope = jnp.zeros(shape, jnp.float32)
        along_x_zslope = jnp.zeros(shape, jnp.float32)
        for sx in range(SHIFTS):
            column = jnp.zeros(shape, jnp.float32)
            slope_column = jnp.zeros(shape, jnp.float32)
            for sz in range(SHIFTS):
                window = window_ref[sy, sz, sx + 1 : sx + 1 + nx]
                column = column + table_z[sz] * window
                if slope_refs is not None:
                    slope_column = slope_column + slope_refs[2][sz] * window
            along_x = along_x + table_x[sx] * column
            if slope_refs is not None:
                along_x_slope = along_x_slope + slope_refs[0][sx] * column
                along_x_zslope = along_x_zslope + table_x[sx] * slope_column
        weight_y = table_y[sy]
        if with_value:
            value = value + weight_y * along_x
        if slope_refs is not None:
            grad_x = grad_x + weight_y * along_x_slope
            grad_y = grad_y + slope_refs[1][sy] * along_x
            grad_z = grad_z + weight_y * along_x_zslope
        return value, grad_x, grad_y, grad_z

    zero = jnp.zeros(shape, jnp.float32)
    value, grad_x, grad_y, grad_z = lax.fori_loop(0, SHIFTS, along_y, (zero,) * 4)
    return value, (grad_x, grad_y, grad_z)


def spread_block(field, weight_refs, product_ref, staged_ref, pz):
    table_x, table_y, table_z = weight_refs
    nx, ny, nz = field.shape
    px, py = nx + 2 * MARGIN, ny + 2 * MARGIN
    for sy in range(SHIFTS):
        weighted = table_y[sy] * field
        for sx in range(SHIFTS):
            product_ref[sy, sx] = table_x[sx] * weighted
    def along_z(sz, total):
        weight_z = table_z[sz]
        for sy in range(SHIFTS):
            rows = [None] * px
            for sx in range(SHIFTS):
                deposit = weight_z * product_ref[sy, sx]
                for x in range(nx):
                    slot = x + sx + 1
                    rows[slot] = deposit[x] if rows[slot] is None else rows[slot] + deposit[x]
            rows[0] = jnp.zeros((ny, nz), jnp.float32)
            for slot in range(px):
                staged_ref[sy, slot, 8 : 8 + ny, :] = rows[slot]
        summed = jnp.zeros((px, py, nz), jnp.float32)
        for sy in range(SHIFTS):
            summed = summed + staged_ref[sy, :, 7 - sy : 7 - sy + py, :]
        padded = jnp.concatenate([summed, jnp.zeros((px, py, pz - nz), jnp.float32)], axis=2)
        shift = lax.rem(sz + (pz - 3), pz)
        return total + pltpu.roll(padded, shift, 2)

    total = lax.fori_loop(0, SHIFTS, along_z, jnp.zeros((px, py, pz), jnp.float32))
    return total


def table_scratch(shape, count):
    return [pltpu.VMEM((SHIFTS,) + shape, jnp.float32) for _ in range(count)]


def clear_rims(staged_ref):
    staged_ref[...] = jnp.zeros(staged_ref.shape, jnp.float32)


def early_sample_kernel(wrapped_ref, cells_ref, fracs_ref, image_ref, grad_ref,
                        rolled_ref, window_ref, *tables):
    weights, slopes = tables[:3], tables[3:]
    build_tables(cells_ref, fracs_ref, 0, 1, weights, slopes)
    value, grads = sample_block(wrapped_ref, rolled_ref, window_ref, weights, slopes, True)
    image_ref[...] = value
    for component in range(3):
        grad_ref[component] = grads[component]


def late_spread_kernel(cot_ref, cells_ref, fracs_ref, out_ref, product_ref, staged_ref, *tables):
    build_tables(cells_ref, fracs_ref, 1, 1, tables, None)
    clear_rims(staged_ref)
    out_ref[...] = spread_block(cot_ref[...], tables, product_ref, staged_ref, out_ref.shape[-1])


def late_velocity_kernel(wrapped_ref, cot_ref, cells_ref, fracs_ref, out_ref,
                         rolled_ref, window_ref, product_ref, staged_ref, *tables):
    weights, slopes, mid = tables[:3], tables[3:6], tables[6:]
    build_tables(cells_ref, fracs_ref, 1, 1, weights, slopes)
    build_tables(cells_ref, fracs_ref, 1, 0, mid, None)
    _, grads = sample_block(wrapped_ref, rolled_ref, window_ref, weights, slopes, False)
    cot = cot_ref[...]
    clear_rims(staged_ref)
    for component in range(3):
        out_ref[component] = spread_block(cot * grads[component], mid, product_ref, staged_ref,
                                          out_ref.shape[-1])


def early_spread_kernel(adjoint_ref, grad_ref, cells_ref, fracs_ref, out_ref,
                        product_ref, staged_ref, *tables):
    dep, mid = tables[:3], tables[3:]
    build_tables(cells_ref, fracs_ref, 0, 1, dep, None)
    build_tables(cells_ref, fracs_ref, 0, 0, mid, None)
    adjoint = adjoint_ref[...]
    clear_rims(staged_ref)
    pz = out_ref.shape[-1]
    out_ref[0] = spread_block(adjoint, dep, product_ref, staged_ref, pz)
    for component in range(3):
        out_ref[1 + component] = spread_block(adjoint * grad_ref[component], mid, product_ref,
                                              staged_ref, pz)


def vmem_call(kernel, out_shapes, scratch, *args):
    return pl.pallas_call(
        kernel,
        out_shape=out_shapes,
        in_specs=[pl.BlockSpec(memory_space=pltpu.VMEM)] * len(args),
        out_specs=jax.tree.map(lambda _: pl.BlockSpec(memory_space=pltpu.VMEM), out_shapes),
        scratch_shapes=scratch,
        compiler_params=pltpu.CompilerParams(vmem_limit_bytes=48 * 1024 * 1024),
    )(*args)


def shift_from(piece, axis, upward):
    count = lax.axis_size(axis)
    if upward:
        pairs = [(i, (i + 1) % count) for i in range(count)]
    else:
        pairs = [((i + 1) % count, i) for i in range(count)]
    shape = piece.shape
    if shape[-1] < 128 and piece.size % 1024 == 0:
        flat = lax.ppermute(piece.reshape(-1, 128), axis, pairs)
        return flat.reshape(shape)
    return lax.ppermute(piece, axis, pairs)


def widen(block, pz):
    for axis, dim in AXES[:2]:
        size = block.shape[dim]
        head = lax.slice_in_dim(block, 0, MARGIN, axis=dim)
        tail = lax.slice_in_dim(block, size - MARGIN, size, axis=dim)
        block = jnp.concatenate(
            [shift_from(tail, axis, True), block, shift_from(head, axis, False)], axis=dim
        )
    nz = block.shape[2]
    head = block[:, :, :MARGIN]
    tail = block[:, :, nz - MARGIN :]
    gap = jnp.zeros(block.shape[:2] + (pz - nz - 2 * MARGIN,), jnp.float32)
    return jnp.concatenate(
        [block, shift_from(head, "gz", False), gap, shift_from(tail, "gz", True)], axis=2
    )


def place_rim(rim, dim, start, size):
    widths = [(0, 0)] * rim.ndim
    widths[dim] = (start, size - start - rim.shape[dim])
    return jnp.pad(rim, widths)


def fold(wrapped, nz):
    pz = wrapped.shape[3]
    upper = wrapped[..., nz : nz + MARGIN]
    lower = wrapped[..., pz - MARGIN :]
    block = wrapped[..., :nz]
    from_below = shift_from(upper, "gz", True)
    from_above = shift_from(lower, "gz", False)
    block = block + place_rim(from_below, 3, 0, nz)
    block = block + place_rim(from_above, 3, nz - MARGIN, nz)
    for axis, dim in (("gy", 2), ("gx", 1)):
        size = block.shape[dim] - 2 * MARGIN
        low = lax.slice_in_dim(block, 0, MARGIN, axis=dim)
        high = lax.slice_in_dim(block, size + MARGIN, size + 2 * MARGIN, axis=dim)
        block = lax.slice_in_dim(block, MARGIN, size + MARGIN, axis=dim)
        got_low = shift_from(high, axis, True)
        got_high = shift_from(low, axis, False)
        block = block + place_rim(got_low, dim, 0, size)
        block = block + place_rim(got_high, dim, size - MARGIN, size)
    return block


def body(intensity, cotangent, departure_cells, departure_fracs):
    cells = departure_cells
    fracs = departure_fracs
    nx, ny, nz = intensity.shape
    px, py, pz = nx + 2 * MARGIN, ny + 2 * MARGIN, nz + 128
    block = (nx, ny, nz)
    f32 = jnp.float32
    rolled = pltpu.VMEM((px, py, nz), f32)
    windows = pltpu.VMEM((SHIFTS, SHIFTS, px, ny, nz), f32)
    products = pltpu.VMEM((SHIFTS, SHIFTS) + block, f32)
    staged = pltpu.VMEM((SHIFTS, px, ny + 16, nz), f32)

    wrapped = widen(intensity, pz)
    image_mid, grad_raw = vmem_call(
        early_sample_kernel,
        (jax.ShapeDtypeStruct(block, f32), jax.ShapeDtypeStruct((3,) + block, f32)),
        [rolled, windows] + table_scratch(block, 6),
        wrapped, cells, fracs,
    )
    adjoint_padded = vmem_call(
        late_spread_kernel,
        jax.ShapeDtypeStruct((px, py, pz), f32),
        [products, staged] + table_scratch(block, 3),
        cotangent, cells, fracs,
    )
    wrapped_mid = widen(image_mid, pz)
    velocity_padded = vmem_call(
        late_velocity_kernel,
        jax.ShapeDtypeStruct((3, px, py, pz), f32),
        [rolled, windows, products, staged] + table_scratch(block, 9),
        wrapped_mid, cotangent, cells, fracs,
    )
    folded = fold(jnp.concatenate([adjoint_padded[None], velocity_padded]), nz)
    adjoint_mid = folded[0]
    velocity_late = folded[1:]
    early_padded = vmem_call(
        early_spread_kernel,
        jax.ShapeDtypeStruct((4, px, py, pz), f32),
        [products, staged] + table_scratch(block, 6),
        adjoint_mid, grad_raw, cells, fracs,
    )
    folded = fold(early_padded, nz)
    return (folded[0], velocity_late + folded[1:])


def solution(mesh):
    in_specs = (
        P("gx", "gy", "gz"),
        P("gx", "gy", "gz"),
        P(None, None, None, "gx", "gy", "gz"),
        P(None, None, None, "gx", "gy", "gz"),
    )
    out_specs = (P("gx", "gy", "gz"), P(None, "gx", "gy", "gz"))
    return jax.shard_map(body, mesh=mesh, in_specs=in_specs, out_specs=out_specs, check_vma=False)
```

```python
import functools

import jax
import jax.numpy as jnp
from jax import lax
from jax.experimental import pallas as pl
from jax.experimental.pallas import tpu as pltpu
from jax.sharding import PartitionSpec as P

MARGIN = 4
SHIFTS = 8
AXES = (("gx", 0), ("gy", 1), ("gz", 2))


def cubic_taps(fraction):
    fraction_squared = fraction * fraction
    fraction_cubed = fraction_squared * fraction
    weights = [
        0.5 * (2.0 * fraction_squared - fraction_cubed - fraction),
        0.5 * (3.0 * fraction_cubed - 5.0 * fraction_squared + 2.0),
        0.5 * (4.0 * fraction_squared - 3.0 * fraction_cubed + fraction),
        0.5 * (fraction_cubed - fraction_squared),
    ]
    slopes = [
        0.5 * (4.0 * fraction - 3.0 * fraction_squared - 1.0),
        0.5 * (9.0 * fraction_squared - 10.0 * fraction),
        0.5 * (8.0 * fraction - 9.0 * fraction_squared + 1.0),
        0.5 * (3.0 * fraction_squared - 2.0 * fraction),
    ]
    return (weights, slopes)


def build_tables(cells_ref, fracs_ref, step, section, weight_refs, slope_refs):
    for component in range(3):
        offsets = cells_ref[step, section, component]
        weights, slopes = cubic_taps(fracs_ref[step, section, component])
        for shift in range(SHIFTS):
            target = shift - 3
            summed = jnp.zeros(offsets.shape, jnp.float32)
            slope_sum = jnp.zeros(offsets.shape, jnp.float32)
            for tap_index in range(4):
                hit = offsets + (tap_index - 1) == target
                summed = summed + jnp.where(hit, weights[tap_index], 0.0)
                if slope_refs is not None:
                    slope_sum = slope_sum + jnp.where(hit, slopes[tap_index], 0.0)
            weight_refs[component][shift] = summed
            if slope_refs is not None:
                slope_refs[component][shift] = slope_sum


def roll_lanes(field, shift):
    shift = shift % field.shape[-1]
    if shift == 0:
        return field
    return pltpu.roll(field, shift, field.ndim - 1)


def sample_block(wrapped_ref, rolled_ref, window_ref, weight_refs, slope_refs, with_value):
    px, py, pz = wrapped_ref.shape
    nx, ny, nz = px - 2 * MARGIN, py - 2 * MARGIN, window_ref.shape[-1]
    field = wrapped_ref[...]
    for sz in range(SHIFTS):
        rolled_ref[...] = roll_lanes(field, 3 - sz)[:, :, :nz]
        for sy in range(SHIFTS):
            window_ref[sy, sz] = rolled_ref[:, sy + 1 : sy + 1 + ny, :]
    table_x, table_y, table_z = weight_refs
    shape = (nx, ny, nz)

    def along_y(sy, carry):
        value, grad_x, grad_y, grad_z = carry
        along_x = jnp.zeros(shape, jnp.float32)
        along_x_slope = jnp.zeros(shape, jnp.float32)
        along_x_zslope = jnp.zeros(shape, jnp.float32)
        for sx in range(SHIFTS):
            column = jnp.zeros(shape, jnp.float32)
            slope_column = jnp.zeros(shape, jnp.float32)
            for sz in range(SHIFTS):
                window = window_ref[sy, sz, sx + 1 : sx + 1 + nx]
                column = column + table_z[sz] * window
                if slope_refs is not None:
                    slope_column = slope_column + slope_refs[2][sz] * window
            along_x = along_x + table_x[sx] * column
            if slope_refs is not None:
                along_x_slope = along_x_slope + slope_refs[0][sx] * column
                along_x_zslope = along_x_zslope + table_x[sx] * slope_column
        weight_y = table_y[sy]
        if with_value:
            value = value + weight_y * along_x
        if slope_refs is not None:
            grad_x = grad_x + weight_y * along_x_slope
            grad_y = grad_y + slope_refs[1][sy] * along_x
            grad_z = grad_z + weight_y * along_x_zslope
        return value, grad_x, grad_y, grad_z

    zero = jnp.zeros(shape, jnp.float32)
    value, grad_x, grad_y, grad_z = lax.fori_loop(0, SHIFTS, along_y, (zero,) * 4)
    return value, (grad_x, grad_y, grad_z)


def spread_block(field, weight_refs, product_ref, staged_ref, pz):
    table_x, table_y, table_z = weight_refs
    nx, ny, nz = field.shape
    px, py = nx + 2 * MARGIN, ny + 2 * MARGIN
    for sy in range(SHIFTS):
        weighted = table_y[sy] * field
        for sx in range(SHIFTS):
            product_ref[sy, sx] = table_x[sx] * weighted
    def along_z(sz, total):
        weight_z = table_z[sz]
        for sy in range(SHIFTS):
            rows = [None] * px
            for sx in range(SHIFTS):
                deposit = weight_z * product_ref[sy, sx]
                for x in range(nx):
                    slot = x + sx + 1
                    rows[slot] = deposit[x] if rows[slot] is None else rows[slot] + deposit[x]
            rows[0] = jnp.zeros((ny, nz), jnp.float32)
            for slot in range(px):
                staged_ref[sy, slot, 8 : 8 + ny, :] = rows[slot]
        summed = jnp.zeros((px, py, nz), jnp.float32)
        for sy in range(SHIFTS):
            summed = summed + staged_ref[sy, :, 7 - sy : 7 - sy + py, :]
        padded = jnp.concatenate([summed, jnp.zeros((px, py, pz - nz), jnp.float32)], axis=2)
        shift = lax.rem(sz + (pz - 3), pz)
        return total + pltpu.roll(padded, shift, 2)

    total = lax.fori_loop(0, SHIFTS, along_z, jnp.zeros((px, py, pz), jnp.float32))
    return total


def table_scratch(shape, count):
    return [pltpu.VMEM((SHIFTS,) + shape, jnp.float32) for _ in range(count)]


def clear_rims(staged_ref):
    staged_ref[...] = jnp.zeros(staged_ref.shape, jnp.float32)


def early_sample_kernel(wrapped_ref, cells_ref, fracs_ref, image_ref, grad_ref,
                        rolled_ref, window_ref, *tables):
    weights, slopes = tables[:3], tables[3:]
    build_tables(cells_ref, fracs_ref, 0, 1, weights, slopes)
    value, grads = sample_block(wrapped_ref, rolled_ref, window_ref, weights, slopes, True)
    image_ref[...] = value
    for component in range(3):
        grad_ref[component] = grads[component]


def late_spread_kernel(cot_ref, cells_ref, fracs_ref, out_ref, product_ref, staged_ref, *tables):
    build_tables(cells_ref, fracs_ref, 1, 1, tables, None)
    clear_rims(staged_ref)
    out_ref[...] = spread_block(cot_ref[...], tables, product_ref, staged_ref, out_ref.shape[-1])


def late_velocity_kernel(wrapped_ref, cot_ref, cells_ref, fracs_ref, out_ref,
                         rolled_ref, window_ref, product_ref, staged_ref, *tables):
    weights, slopes, mid = tables[:3], tables[3:6], tables[6:]
    build_tables(cells_ref, fracs_ref, 1, 1, weights, slopes)
    build_tables(cells_ref, fracs_ref, 1, 0, mid, None)
    _, grads = sample_block(wrapped_ref, rolled_ref, window_ref, weights, slopes, False)
    cot = cot_ref[...]
    clear_rims(staged_ref)
    for component in range(3):
        out_ref[component] = spread_block(cot * grads[component], mid, product_ref, staged_ref,
                                          out_ref.shape[-1])


def early_spread_kernel(adjoint_ref, grad_ref, cells_ref, fracs_ref, out_ref,
                        product_ref, staged_ref, *tables):
    dep, mid = tables[:3], tables[3:]
    build_tables(cells_ref, fracs_ref, 0, 1, dep, None)
    build_tables(cells_ref, fracs_ref, 0, 0, mid, None)
    adjoint = adjoint_ref[...]
    clear_rims(staged_ref)
    pz = out_ref.shape[-1]
    out_ref[0] = spread_block(adjoint, dep, product_ref, staged_ref, pz)
    for component in range(3):
        out_ref[1 + component] = spread_block(adjoint * grad_ref[component], mid, product_ref,
                                              staged_ref, pz)


def vmem_call(kernel, out_shapes, scratch, *args):
    return pl.pallas_call(
        kernel,
        out_shape=out_shapes,
        in_specs=[pl.BlockSpec(memory_space=pltpu.VMEM)] * len(args),
        out_specs=jax.tree.map(lambda _: pl.BlockSpec(memory_space=pltpu.VMEM), out_shapes),
        scratch_shapes=scratch,
        compiler_params=pltpu.CompilerParams(vmem_limit_bytes=48 * 1024 * 1024),
    )(*args)


def shift_from(piece, axis, upward):
    count = lax.axis_size(axis)
    if upward:
        pairs = [(i, (i + 1) % count) for i in range(count)]
    else:
        pairs = [((i + 1) % count, i) for i in range(count)]
    shape = piece.shape
    if shape[-1] < 128 and piece.size % 1024 == 0:
        flat = lax.ppermute(piece.reshape(-1, 128), axis, pairs)
        return flat.reshape(shape)
    return lax.ppermute(piece, axis, pairs)


def neighbour_ids():
    here = [lax.axis_index(axis) for axis, _ in AXES]
    ids = []
    for position, (axis, _) in enumerate(AXES):
        count = lax.axis_size(axis)
        for step in (1, count - 1):
            target = list(here)
            target[position] = lax.rem(here[position] + step, count)
            ids.append(tuple(target))
    return ids


def widen_kernel(block_ref, out_ref, recv_x, recv_y, recv_z, wide_x, wide_y, send_sems,
                 recv_sems):
    nx, ny, nz = block_ref.shape
    mesh = pl.DeviceIdType.MESH
    ids = neighbour_ids()
    barrier = pltpu.get_barrier_semaphore()
    for target in ids:
        pl.semaphore_signal(barrier, inc=1, device_id=target, device_id_type=mesh)
    pl.semaphore_wait(barrier, len(ids))

    def exchange(stage, source, landing):
        copies = []
        for side in range(2):
            copy = pltpu.make_async_remote_copy(
                src_ref=source,
                dst_ref=landing.at[side],
                send_sem=send_sems.at[2 * stage + side],
                recv_sem=recv_sems.at[2 * stage + side],
                device_id=ids[2 * stage + side],
                device_id_type=mesh,
            )
            copy.start()
            copies.append(copy)
        for copy in copies:
            copy.wait()

    exchange(0, block_ref, recv_x)
    wide_x[0:MARGIN] = recv_x[0, nx - MARGIN : nx]
    wide_x[MARGIN : MARGIN + nx] = block_ref[...]
    wide_x[MARGIN + nx :] = recv_x[1, 0:MARGIN]
    exchange(1, wide_x, recv_y)
    wide_y[:, 0:ny] = recv_y[0]
    wide_y[:, ny : 2 * ny] = wide_x[...]
    wide_y[:, 2 * ny :] = recv_y[1]
    exchange(2, wide_y, recv_z)
    rows = slice(ny - MARGIN, 2 * ny + MARGIN)
    out_ref[:, :, 0:nz] = wide_y[:, rows, :]
    lane = lax.broadcasted_iota(jnp.int32, out_ref.shape[:2] + (nz,), 2)
    above = recv_z[1, :, rows, :]
    below = recv_z[0, :, rows, :]
    out_ref[:, :, nz:] = jnp.where(
        lane < MARGIN, above, jnp.where(lane >= nz - MARGIN, below, 0.0)
    )


def widen(block, pz):
    nx, ny, nz = block.shape
    px = nx + 2 * MARGIN
    f32 = jnp.float32
    return pl.pallas_call(
        widen_kernel,
        out_shape=jax.ShapeDtypeStruct((px, ny + 2 * MARGIN, pz), f32),
        in_specs=[pl.BlockSpec(memory_space=pltpu.VMEM)],
        out_specs=pl.BlockSpec(memory_space=pltpu.VMEM),
        scratch_shapes=[
            pltpu.VMEM((2, nx, ny, nz), f32),
            pltpu.VMEM((2, px, ny, nz), f32),
            pltpu.VMEM((2, px, 3 * ny, nz), f32),
            pltpu.VMEM((px, ny, nz), f32),
            pltpu.VMEM((px, 3 * ny, nz), f32),
            pltpu.SemaphoreType.DMA((6,)),
            pltpu.SemaphoreType.DMA((6,)),
        ],
        compiler_params=pltpu.CompilerParams(collective_id=0, has_side_effects=True),
    )(block)


def place_rim(rim, dim, start, size):
    widths = [(0, 0)] * rim.ndim
    widths[dim] = (start, size - start - rim.shape[dim])
    return jnp.pad(rim, widths)


def fold(wrapped, nz):
    pz = wrapped.shape[3]
    upper = wrapped[..., nz : nz + MARGIN]
    lower = wrapped[..., pz - MARGIN :]
    block = wrapped[..., :nz]
    from_below = shift_from(upper, "gz", True)
    from_above = shift_from(lower, "gz", False)
    block = block + place_rim(from_below, 3, 0, nz)
    block = block + place_rim(from_above, 3, nz - MARGIN, nz)
    for axis, dim in (("gy", 2), ("gx", 1)):
        size = block.shape[dim] - 2 * MARGIN
        low = lax.slice_in_dim(block, 0, MARGIN, axis=dim)
        high = lax.slice_in_dim(block, size + MARGIN, size + 2 * MARGIN, axis=dim)
        block = lax.slice_in_dim(block, MARGIN, size + MARGIN, axis=dim)
        got_low = shift_from(high, axis, True)
        got_high = shift_from(low, axis, False)
        block = block + place_rim(got_low, dim, 0, size)
        block = block + place_rim(got_high, dim, size - MARGIN, size)
    return block


def body(intensity, cotangent, departure_cells, departure_fracs):
    cells = departure_cells
    fracs = departure_fracs
    nx, ny, nz = intensity.shape
    px, py, pz = nx + 2 * MARGIN, ny + 2 * MARGIN, nz + 128
    block = (nx, ny, nz)
    f32 = jnp.float32
    rolled = pltpu.VMEM((px, py, nz), f32)
    windows = pltpu.VMEM((SHIFTS, SHIFTS, px, ny, nz), f32)
    products = pltpu.VMEM((SHIFTS, SHIFTS) + block, f32)
    staged = pltpu.VMEM((SHIFTS, px, ny + 16, nz), f32)

    wrapped = widen(intensity, pz)
    image_mid, grad_raw = vmem_call(
        early_sample_kernel,
        (jax.ShapeDtypeStruct(block, f32), jax.ShapeDtypeStruct((3,) + block, f32)),
        [rolled, windows] + table_scratch(block, 6),
        wrapped, cells, fracs,
    )
    adjoint_padded = vmem_call(
        late_spread_kernel,
        jax.ShapeDtypeStruct((px, py, pz), f32),
        [products, staged] + table_scratch(block, 3),
        cotangent, cells, fracs,
    )
    wrapped_mid = widen(image_mid, pz)
    velocity_padded = vmem_call(
        late_velocity_kernel,
        jax.ShapeDtypeStruct((3, px, py, pz), f32),
        [rolled, windows, products, staged] + table_scratch(block, 9),
        wrapped_mid, cotangent, cells, fracs,
    )
    folded = fold(jnp.concatenate([adjoint_padded[None], velocity_padded]), nz)
    adjoint_mid = folded[0]
    velocity_late = folded[1:]
    early_padded = vmem_call(
        early_spread_kernel,
        jax.ShapeDtypeStruct((4, px, py, pz), f32),
        [products, staged] + table_scratch(block, 6),
        adjoint_mid, grad_raw, cells, fracs,
    )
    folded = fold(early_padded, nz)
    return (folded[0], velocity_late + folded[1:])


def solution(mesh):
    in_specs = (
        P("gx", "gy", "gz"),
        P("gx", "gy", "gz"),
        P(None, None, None, "gx", "gy", "gz"),
        P(None, None, None, "gx", "gy", "gz"),
    )
    out_specs = (P("gx", "gy", "gz"), P(None, "gx", "gy", "gz"))
    return jax.shard_map(body, mesh=mesh, in_specs=in_specs, out_specs=out_specs, check_vma=False)
```

```python
import functools

import jax
import jax.numpy as jnp
from jax import lax
from jax.experimental import pallas as pl
from jax.experimental.pallas import tpu as pltpu
from jax.sharding import PartitionSpec as P

MARGIN = 4
SHIFTS = 8
AXES = (("gx", 0), ("gy", 1), ("gz", 2))


def cubic_taps(fraction):
    fraction_squared = fraction * fraction
    fraction_cubed = fraction_squared * fraction
    weights = [
        0.5 * (2.0 * fraction_squared - fraction_cubed - fraction),
        0.5 * (3.0 * fraction_cubed - 5.0 * fraction_squared + 2.0),
        0.5 * (4.0 * fraction_squared - 3.0 * fraction_cubed + fraction),
        0.5 * (fraction_cubed - fraction_squared),
    ]
    slopes = [
        0.5 * (4.0 * fraction - 3.0 * fraction_squared - 1.0),
        0.5 * (9.0 * fraction_squared - 10.0 * fraction),
        0.5 * (8.0 * fraction - 9.0 * fraction_squared + 1.0),
        0.5 * (3.0 * fraction_squared - 2.0 * fraction),
    ]
    return (weights, slopes)


def build_tables(cells_ref, fracs_ref, step, section, weight_refs, slope_refs):
    for component in range(3):
        offsets = cells_ref[step, section, component]
        weights, slopes = cubic_taps(fracs_ref[step, section, component])
        for shift in range(SHIFTS):
            target = shift - 3
            summed = jnp.zeros(offsets.shape, jnp.float32)
            slope_sum = jnp.zeros(offsets.shape, jnp.float32)
            for tap_index in range(4):
                hit = offsets + (tap_index - 1) == target
                summed = summed + jnp.where(hit, weights[tap_index], 0.0)
                if slope_refs is not None:
                    slope_sum = slope_sum + jnp.where(hit, slopes[tap_index], 0.0)
            weight_refs[component][shift] = summed
            if slope_refs is not None:
                slope_refs[component][shift] = slope_sum


def roll_lanes(field, shift):
    shift = shift % field.shape[-1]
    if shift == 0:
        return field
    return pltpu.roll(field, shift, field.ndim - 1)


def sample_block(wrapped_ref, rolled_ref, window_ref, weight_refs, slope_refs, with_value):
    px, py, pz = wrapped_ref.shape
    nx, ny, nz = px - 2 * MARGIN, py - 2 * MARGIN, window_ref.shape[-1]
    field = wrapped_ref[...]
    for sz in range(SHIFTS):
        rolled_ref[...] = roll_lanes(field, 3 - sz)[:, :, :nz]
        for sy in range(SHIFTS):
            window_ref[sy, sz] = rolled_ref[:, sy + 1 : sy + 1 + ny, :]
    table_x, table_y, table_z = weight_refs
    shape = (nx, ny, nz)

    def along_y(sy, carry):
        value, grad_x, grad_y, grad_z = carry
        along_x = jnp.zeros(shape, jnp.float32)
        along_x_slope = jnp.zeros(shape, jnp.float32)
        along_x_zslope = jnp.zeros(shape, jnp.float32)
        for sx in range(SHIFTS):
            column = jnp.zeros(shape, jnp.float32)
            slope_column = jnp.zeros(shape, jnp.float32)
            for sz in range(SHIFTS):
                window = window_ref[sy, sz, sx + 1 : sx + 1 + nx]
                column = column + table_z[sz] * window
                if slope_refs is not None:
                    slope_column = slope_column + slope_refs[2][sz] * window
            along_x = along_x + table_x[sx] * column
            if slope_refs is not None:
                along_x_slope = along_x_slope + slope_refs[0][sx] * column
                along_x_zslope = along_x_zslope + table_x[sx] * slope_column
        weight_y = table_y[sy]
        if with_value:
            value = value + weight_y * along_x
        if slope_refs is not None:
            grad_x = grad_x + weight_y * along_x_slope
            grad_y = grad_y + slope_refs[1][sy] * along_x
            grad_z = grad_z + weight_y * along_x_zslope
        return value, grad_x, grad_y, grad_z

    zero = jnp.zeros(shape, jnp.float32)
    value, grad_x, grad_y, grad_z = lax.fori_loop(0, SHIFTS, along_y, (zero,) * 4)
    return value, (grad_x, grad_y, grad_z)


def spread_block(field, weight_refs, product_ref, staged_ref, pz):
    table_x, table_y, table_z = weight_refs
    nx, ny, nz = field.shape
    px, py = nx + 2 * MARGIN, ny + 2 * MARGIN
    for sy in range(SHIFTS):
        weighted = table_y[sy] * field
        for sx in range(SHIFTS):
            product_ref[sy, sx] = table_x[sx] * weighted
    def along_z(sz, total):
        weight_z = table_z[sz]
        for sy in range(SHIFTS):
            rows = [None] * px
            for sx in range(SHIFTS):
                deposit = weight_z * product_ref[sy, sx]
                for x in range(nx):
                    slot = x + sx + 1
                    rows[slot] = deposit[x] if rows[slot] is None else rows[slot] + deposit[x]
            rows[0] = jnp.zeros((ny, nz), jnp.float32)
            for slot in range(px):
                staged_ref[sy, slot, 8 : 8 + ny, :] = rows[slot]
        summed = jnp.zeros((px, py, nz), jnp.float32)
        for sy in range(SHIFTS):
            summed = summed + staged_ref[sy, :, 7 - sy : 7 - sy + py, :]
        padded = jnp.concatenate([summed, jnp.zeros((px, py, pz - nz), jnp.float32)], axis=2)
        shift = lax.rem(sz + (pz - 3), pz)
        return total + pltpu.roll(padded, shift, 2)

    total = lax.fori_loop(0, SHIFTS, along_z, jnp.zeros((px, py, pz), jnp.float32))
    return total


def table_scratch(shape, count):
    return [pltpu.VMEM((SHIFTS,) + shape, jnp.float32) for _ in range(count)]


def clear_rims(staged_ref):
    staged_ref[...] = jnp.zeros(staged_ref.shape, jnp.float32)


def early_sample_kernel(wrapped_ref, cells_ref, fracs_ref, image_ref, grad_ref,
                        rolled_ref, window_ref, *tables):
    weights, slopes = tables[:3], tables[3:]
    build_tables(cells_ref, fracs_ref, 0, 1, weights, slopes)
    value, grads = sample_block(wrapped_ref, rolled_ref, window_ref, weights, slopes, True)
    image_ref[...] = value
    for component in range(3):
        grad_ref[component] = grads[component]


def late_spread_kernel(cot_ref, cells_ref, fracs_ref, out_ref, product_ref, staged_ref, *tables):
    build_tables(cells_ref, fracs_ref, 1, 1, tables, None)
    clear_rims(staged_ref)
    out_ref[...] = spread_block(cot_ref[...], tables, product_ref, staged_ref, out_ref.shape[-1])


def late_velocity_kernel(wrapped_ref, cot_ref, cells_ref, fracs_ref, out_ref,
                         rolled_ref, window_ref, product_ref, staged_ref, *tables):
    weights, slopes, mid = tables[:3], tables[3:6], tables[6:]
    build_tables(cells_ref, fracs_ref, 1, 1, weights, slopes)
    build_tables(cells_ref, fracs_ref, 1, 0, mid, None)
    _, grads = sample_block(wrapped_ref, rolled_ref, window_ref, weights, slopes, False)
    cot = cot_ref[...]
    clear_rims(staged_ref)
    for component in range(3):
        out_ref[component] = spread_block(cot * grads[component], mid, product_ref, staged_ref,
                                          out_ref.shape[-1])


def early_spread_kernel(adjoint_ref, grad_ref, cells_ref, fracs_ref, out_ref,
                        product_ref, staged_ref, *tables):
    dep, mid = tables[:3], tables[3:]
    build_tables(cells_ref, fracs_ref, 0, 1, dep, None)
    build_tables(cells_ref, fracs_ref, 0, 0, mid, None)
    adjoint = adjoint_ref[...]
    clear_rims(staged_ref)
    pz = out_ref.shape[-1]
    out_ref[0] = spread_block(adjoint, dep, product_ref, staged_ref, pz)
    for component in range(3):
        out_ref[1 + component] = spread_block(adjoint * grad_ref[component], mid, product_ref,
                                              staged_ref, pz)


def vmem_call(kernel, out_shapes, scratch, *args):
    return pl.pallas_call(
        kernel,
        out_shape=out_shapes,
        in_specs=[pl.BlockSpec(memory_space=pltpu.VMEM)] * len(args),
        out_specs=jax.tree.map(lambda _: pl.BlockSpec(memory_space=pltpu.VMEM), out_shapes),
        scratch_shapes=scratch,
        compiler_params=pltpu.CompilerParams(vmem_limit_bytes=48 * 1024 * 1024),
    )(*args)


def shift_from(piece, axis, upward):
    count = lax.axis_size(axis)
    if upward:
        pairs = [(i, (i + 1) % count) for i in range(count)]
    else:
        pairs = [((i + 1) % count, i) for i in range(count)]
    shape = piece.shape
    if shape[-1] < 128 and piece.size % 1024 == 0:
        flat = lax.ppermute(piece.reshape(-1, 128), axis, pairs)
        return flat.reshape(shape)
    return lax.ppermute(piece, axis, pairs)


def offsets_26():
    return [
        (a, b, c)
        for a in (-1, 0, 1)
        for b in (-1, 0, 1)
        for c in (-1, 0, 1)
        if (a, b, c) != (0, 0, 0)
    ]


def slot_of(offset):
    return (offset[0] + 1) * 9 + (offset[1] + 1) * 3 + (offset[2] + 1)


def device_at(offset):
    target = []
    for (axis, _), step in zip(AXES, offset):
        count = lax.axis_size(axis)
        target.append(lax.rem(lax.axis_index(axis) + (step + count), count))
    return tuple(target)


def widen_kernel(block_ref, out_ref, landed, planes, send_sems, recv_sems):
    nx, ny, nz = block_ref.shape
    mesh = pl.DeviceIdType.MESH
    offsets = offsets_26()
    barrier = pltpu.get_barrier_semaphore()
    for offset in offsets:
        pl.semaphore_signal(barrier, inc=1, device_id=device_at(offset), device_id_type=mesh)
    pl.semaphore_wait(barrier, len(offsets))
    copies = []
    for offset in offsets:
        back = slot_of(tuple(-step for step in offset))
        copy = pltpu.make_async_remote_copy(
            src_ref=block_ref,
            dst_ref=landed.at[back],
            send_sem=send_sems.at[slot_of(offset)],
            recv_sem=recv_sems.at[back],
            device_id=device_at(offset),
            device_id_type=mesh,
        )
        copy.start()
        copies.append(copy)
    for copy in copies:
        copy.wait()
    row_ranges = {-1: (nx - MARGIN, nx, 0), 0: (0, nx, MARGIN), 1: (0, MARGIN, MARGIN + nx)}
    for c in (-1, 0, 1):
        for b in (-1, 0, 1):
            for a in (-1, 0, 1):
                first, last, at = row_ranges[a]
                if (a, b, c) == (0, 0, 0):
                    piece = block_ref[first:last]
                else:
                    piece = landed[slot_of((a, b, c)), first:last]
                planes[c + 1, at : at + last - first, (b + 1) * ny : (b + 2) * ny, :] = piece
    rows = slice(ny - MARGIN, 2 * ny + MARGIN)
    out_ref[:, :, 0:nz] = planes[1, :, rows, :]
    lane = lax.broadcasted_iota(jnp.int32, out_ref.shape[:2] + (nz,), 2)
    above = planes[2, :, rows, :]
    below = planes[0, :, rows, :]
    out_ref[:, :, nz:] = jnp.where(
        lane < MARGIN, above, jnp.where(lane >= nz - MARGIN, below, 0.0)
    )


def widen(block, pz):
    nx, ny, nz = block.shape
    px = nx + 2 * MARGIN
    f32 = jnp.float32
    return pl.pallas_call(
        widen_kernel,
        out_shape=jax.ShapeDtypeStruct((px, ny + 2 * MARGIN, pz), f32),
        in_specs=[pl.BlockSpec(memory_space=pltpu.VMEM)],
        out_specs=pl.BlockSpec(memory_space=pltpu.VMEM),
        scratch_shapes=[
            pltpu.VMEM((27, nx, ny, nz), f32),
            pltpu.VMEM((3, px, 3 * ny, nz), f32),
            pltpu.SemaphoreType.DMA((27,)),
            pltpu.SemaphoreType.DMA((27,)),
        ],
        compiler_params=pltpu.CompilerParams(collective_id=0, has_side_effects=True),
    )(block)


def place_rim(rim, dim, start, size):
    widths = [(0, 0)] * rim.ndim
    widths[dim] = (start, size - start - rim.shape[dim])
    return jnp.pad(rim, widths)


def fold(wrapped, nz):
    pz = wrapped.shape[3]
    upper = wrapped[..., nz : nz + MARGIN]
    lower = wrapped[..., pz - MARGIN :]
    block = wrapped[..., :nz]
    from_below = shift_from(upper, "gz", True)
    from_above = shift_from(lower, "gz", False)
    block = block + place_rim(from_below, 3, 0, nz)
    block = block + place_rim(from_above, 3, nz - MARGIN, nz)
    for axis, dim in (("gy", 2), ("gx", 1)):
        size = block.shape[dim] - 2 * MARGIN
        low = lax.slice_in_dim(block, 0, MARGIN, axis=dim)
        high = lax.slice_in_dim(block, size + MARGIN, size + 2 * MARGIN, axis=dim)
        block = lax.slice_in_dim(block, MARGIN, size + MARGIN, axis=dim)
        got_low = shift_from(high, axis, True)
        got_high = shift_from(low, axis, False)
        block = block + place_rim(got_low, dim, 0, size)
        block = block + place_rim(got_high, dim, size - MARGIN, size)
    return block


def body(intensity, cotangent, departure_cells, departure_fracs):
    cells = departure_cells
    fracs = departure_fracs
    nx, ny, nz = intensity.shape
    px, py, pz = nx + 2 * MARGIN, ny + 2 * MARGIN, nz + 128
    block = (nx, ny, nz)
    f32 = jnp.float32
    rolled = pltpu.VMEM((px, py, nz), f32)
    windows = pltpu.VMEM((SHIFTS, SHIFTS, px, ny, nz), f32)
    products = pltpu.VMEM((SHIFTS, SHIFTS) + block, f32)
    staged = pltpu.VMEM((SHIFTS, px, ny + 16, nz), f32)

    wrapped = widen(intensity, pz)
    image_mid, grad_raw = vmem_call(
        early_sample_kernel,
        (jax.ShapeDtypeStruct(block, f32), jax.ShapeDtypeStruct((3,) + block, f32)),
        [rolled, windows] + table_scratch(block, 6),
        wrapped, cells, fracs,
    )
    adjoint_padded = vmem_call(
        late_spread_kernel,
        jax.ShapeDtypeStruct((px, py, pz), f32),
        [products, staged] + table_scratch(block, 3),
        cotangent, cells, fracs,
    )
    wrapped_mid = widen(image_mid, pz)
    velocity_padded = vmem_call(
        late_velocity_kernel,
        jax.ShapeDtypeStruct((3, px, py, pz), f32),
        [rolled, windows, products, staged] + table_scratch(block, 9),
        wrapped_mid, cotangent, cells, fracs,
    )
    folded = fold(jnp.concatenate([adjoint_padded[None], velocity_padded]), nz)
    adjoint_mid = folded[0]
    velocity_late = folded[1:]
    early_padded = vmem_call(
        early_spread_kernel,
        jax.ShapeDtypeStruct((4, px, py, pz), f32),
        [products, staged] + table_scratch(block, 6),
        adjoint_mid, grad_raw, cells, fracs,
    )
    folded = fold(early_padded, nz)
    return (folded[0], velocity_late + folded[1:])


def solution(mesh):
    in_specs = (
        P("gx", "gy", "gz"),
        P("gx", "gy", "gz"),
        P(None, None, None, "gx", "gy", "gz"),
        P(None, None, None, "gx", "gy", "gz"),
    )
    out_specs = (P("gx", "gy", "gz"), P(None, "gx", "gy", "gz"))
    return jax.shard_map(body, mesh=mesh, in_specs=in_specs, out_specs=out_specs, check_vma=False)
```

```python
import functools

import jax
import jax.numpy as jnp
from jax import lax
from jax.experimental import pallas as pl
from jax.experimental.pallas import tpu as pltpu
from jax.sharding import PartitionSpec as P

MARGIN = 4
SHIFTS = 8
AXES = (("gx", 0), ("gy", 1), ("gz", 2))


def cubic_taps(fraction):
    fraction_squared = fraction * fraction
    fraction_cubed = fraction_squared * fraction
    weights = [
        0.5 * (2.0 * fraction_squared - fraction_cubed - fraction),
        0.5 * (3.0 * fraction_cubed - 5.0 * fraction_squared + 2.0),
        0.5 * (4.0 * fraction_squared - 3.0 * fraction_cubed + fraction),
        0.5 * (fraction_cubed - fraction_squared),
    ]
    slopes = [
        0.5 * (4.0 * fraction - 3.0 * fraction_squared - 1.0),
        0.5 * (9.0 * fraction_squared - 10.0 * fraction),
        0.5 * (8.0 * fraction - 9.0 * fraction_squared + 1.0),
        0.5 * (3.0 * fraction_squared - 2.0 * fraction),
    ]
    return (weights, slopes)


def build_tables(cells_ref, fracs_ref, step, section, weight_refs, slope_refs):
    for component in range(3):
        offsets = cells_ref[step, section, component]
        weights, slopes = cubic_taps(fracs_ref[step, section, component])
        for shift in range(SHIFTS):
            target = shift - 3
            summed = jnp.zeros(offsets.shape, jnp.float32)
            slope_sum = jnp.zeros(offsets.shape, jnp.float32)
            for tap_index in range(4):
                hit = offsets + (tap_index - 1) == target
                summed = summed + jnp.where(hit, weights[tap_index], 0.0)
                if slope_refs is not None:
                    slope_sum = slope_sum + jnp.where(hit, slopes[tap_index], 0.0)
            weight_refs[component][shift] = summed
            if slope_refs is not None:
                slope_refs[component][shift] = slope_sum


def roll_lanes(field, shift):
    shift = shift % field.shape[-1]
    if shift == 0:
        return field
    return pltpu.roll(field, shift, field.ndim - 1)


def sample_block(wrapped_ref, rolled_ref, window_ref, weight_refs, slope_refs, with_value):
    px, py, pz = wrapped_ref.shape
    nx, ny, nz = px - 2 * MARGIN, py - 2 * MARGIN, window_ref.shape[-1]
    field = wrapped_ref[...]
    for sz in range(SHIFTS):
        rolled_ref[...] = roll_lanes(field, 3 - sz)[:, :, :nz]
        for sy in range(SHIFTS):
            window_ref[sy, sz] = rolled_ref[:, sy + 1 : sy + 1 + ny, :]
    table_x, table_y, table_z = weight_refs
    shape = (nx, ny, nz)

    def along_y(sy, carry):
        value, grad_x, grad_y, grad_z = carry
        along_x = jnp.zeros(shape, jnp.float32)
        along_x_slope = jnp.zeros(shape, jnp.float32)
        along_x_zslope = jnp.zeros(shape, jnp.float32)
        for sx in range(SHIFTS):
            column = jnp.zeros(shape, jnp.float32)
            slope_column = jnp.zeros(shape, jnp.float32)
            for sz in range(SHIFTS):
                window = window_ref[sy, sz, sx + 1 : sx + 1 + nx]
                column = column + table_z[sz] * window
                if slope_refs is not None:
                    slope_column = slope_column + slope_refs[2][sz] * window
            along_x = along_x + table_x[sx] * column
            if slope_refs is not None:
                along_x_slope = along_x_slope + slope_refs[0][sx] * column
                along_x_zslope = along_x_zslope + table_x[sx] * slope_column
        weight_y = table_y[sy]
        if with_value:
            value = value + weight_y * along_x
        if slope_refs is not None:
            grad_x = grad_x + weight_y * along_x_slope
            grad_y = grad_y + slope_refs[1][sy] * along_x
            grad_z = grad_z + weight_y * along_x_zslope
        return value, grad_x, grad_y, grad_z

    zero = jnp.zeros(shape, jnp.float32)
    value, grad_x, grad_y, grad_z = lax.fori_loop(0, SHIFTS, along_y, (zero,) * 4)
    return value, (grad_x, grad_y, grad_z)


def spread_block(field, weight_refs, product_ref, staged_ref, pz):
    table_x, table_y, table_z = weight_refs
    nx, ny, nz = field.shape
    px, py = nx + 2 * MARGIN, ny + 2 * MARGIN
    for sy in range(SHIFTS):
        weighted = table_y[sy] * field
        for sx in range(SHIFTS):
            product_ref[sy, sx] = table_x[sx] * weighted
    def along_z(sz, total):
        weight_z = table_z[sz]
        for sy in range(SHIFTS):
            rows = [None] * px
            for sx in range(SHIFTS):
                deposit = weight_z * product_ref[sy, sx]
                for x in range(nx):
                    slot = x + sx + 1
                    rows[slot] = deposit[x] if rows[slot] is None else rows[slot] + deposit[x]
            rows[0] = jnp.zeros((ny, nz), jnp.float32)
            for slot in range(px):
                staged_ref[sy, slot, 8 : 8 + ny, :] = rows[slot]
        summed = jnp.zeros((px, py, nz), jnp.float32)
        for sy in range(SHIFTS):
            summed = summed + staged_ref[sy, :, 7 - sy : 7 - sy + py, :]
        padded = jnp.concatenate([summed, jnp.zeros((px, py, pz - nz), jnp.float32)], axis=2)
        shift = lax.rem(sz + (pz - 3), pz)
        return total + pltpu.roll(padded, shift, 2)

    total = lax.fori_loop(0, SHIFTS, along_z, jnp.zeros((px, py, pz), jnp.float32))
    return total


def table_scratch(shape, count):
    return [pltpu.VMEM((SHIFTS,) + shape, jnp.float32) for _ in range(count)]


def clear_rims(staged_ref):
    staged_ref[...] = jnp.zeros(staged_ref.shape, jnp.float32)


def early_sample_kernel(wrapped_ref, cells_ref, fracs_ref, image_ref, grad_ref,
                        rolled_ref, window_ref, *tables):
    weights, slopes = tables[:3], tables[3:]
    build_tables(cells_ref, fracs_ref, 0, 1, weights, slopes)
    value, grads = sample_block(wrapped_ref, rolled_ref, window_ref, weights, slopes, True)
    image_ref[...] = value
    for component in range(3):
        grad_ref[component] = grads[component]


def late_spread_kernel(cot_ref, cells_ref, fracs_ref, out_ref, product_ref, staged_ref, *tables):
    build_tables(cells_ref, fracs_ref, 1, 1, tables, None)
    clear_rims(staged_ref)
    out_ref[...] = spread_block(cot_ref[...], tables, product_ref, staged_ref, out_ref.shape[-1])


def late_velocity_kernel(wrapped_ref, cot_ref, cells_ref, fracs_ref, out_ref,
                         rolled_ref, window_ref, product_ref, staged_ref, *tables):
    weights, slopes, mid = tables[:3], tables[3:6], tables[6:]
    build_tables(cells_ref, fracs_ref, 1, 1, weights, slopes)
    build_tables(cells_ref, fracs_ref, 1, 0, mid, None)
    _, grads = sample_block(wrapped_ref, rolled_ref, window_ref, weights, slopes, False)
    cot = cot_ref[...]
    clear_rims(staged_ref)
    for component in range(3):
        out_ref[component] = spread_block(cot * grads[component], mid, product_ref, staged_ref,
                                          out_ref.shape[-1])


def early_spread_kernel(adjoint_ref, grad_ref, cells_ref, fracs_ref, out_ref,
                        product_ref, staged_ref, *tables):
    dep, mid = tables[:3], tables[3:]
    build_tables(cells_ref, fracs_ref, 0, 1, dep, None)
    build_tables(cells_ref, fracs_ref, 0, 0, mid, None)
    adjoint = adjoint_ref[...]
    clear_rims(staged_ref)
    pz = out_ref.shape[-1]
    out_ref[0] = spread_block(adjoint, dep, product_ref, staged_ref, pz)
    for component in range(3):
        out_ref[1 + component] = spread_block(adjoint * grad_ref[component], mid, product_ref,
                                              staged_ref, pz)


def vmem_call(kernel, out_shapes, scratch, *args):
    return pl.pallas_call(
        kernel,
        out_shape=out_shapes,
        in_specs=[pl.BlockSpec(memory_space=pltpu.VMEM)] * len(args),
        out_specs=jax.tree.map(lambda _: pl.BlockSpec(memory_space=pltpu.VMEM), out_shapes),
        scratch_shapes=scratch,
        compiler_params=pltpu.CompilerParams(vmem_limit_bytes=48 * 1024 * 1024),
        cost_estimate=pl.CostEstimate(
            flops=40_000_000, transcendentals=0, bytes_accessed=2_000_000
        ),
    )(*args)


def shift_from(piece, axis, upward):
    count = lax.axis_size(axis)
    if upward:
        pairs = [(i, (i + 1) % count) for i in range(count)]
    else:
        pairs = [((i + 1) % count, i) for i in range(count)]
    shape = piece.shape
    if shape[-1] < 128 and piece.size % 1024 == 0:
        flat = lax.ppermute(piece.reshape(-1, 128), axis, pairs)
        return flat.reshape(shape)
    return lax.ppermute(piece, axis, pairs)


def widen(block, pz):
    for axis, dim in AXES[:2]:
        size = block.shape[dim]
        head = lax.slice_in_dim(block, 0, MARGIN, axis=dim)
        tail = lax.slice_in_dim(block, size - MARGIN, size, axis=dim)
        block = jnp.concatenate(
            [shift_from(tail, axis, True), block, shift_from(head, axis, False)], axis=dim
        )
    nz = block.shape[2]
    head = block[:, :, :MARGIN]
    tail = block[:, :, nz - MARGIN :]
    gap = jnp.zeros(block.shape[:2] + (pz - nz - 2 * MARGIN,), jnp.float32)
    return jnp.concatenate(
        [block, shift_from(head, "gz", False), gap, shift_from(tail, "gz", True)], axis=2
    )


def place_rim(rim, dim, start, size):
    widths = [(0, 0)] * rim.ndim
    widths[dim] = (start, size - start - rim.shape[dim])
    return jnp.pad(rim, widths)


def fold(wrapped, nz):
    pz = wrapped.shape[3]
    upper = wrapped[..., nz : nz + MARGIN]
    lower = wrapped[..., pz - MARGIN :]
    block = wrapped[..., :nz]
    from_below = shift_from(upper, "gz", True)
    from_above = shift_from(lower, "gz", False)
    block = block + place_rim(from_below, 3, 0, nz)
    block = block + place_rim(from_above, 3, nz - MARGIN, nz)
    for axis, dim in (("gy", 2), ("gx", 1)):
        size = block.shape[dim] - 2 * MARGIN
        low = lax.slice_in_dim(block, 0, MARGIN, axis=dim)
        high = lax.slice_in_dim(block, size + MARGIN, size + 2 * MARGIN, axis=dim)
        block = lax.slice_in_dim(block, MARGIN, size + MARGIN, axis=dim)
        got_low = shift_from(high, axis, True)
        got_high = shift_from(low, axis, False)
        block = block + place_rim(got_low, dim, 0, size)
        block = block + place_rim(got_high, dim, size - MARGIN, size)
    return block


def body(intensity, cotangent, departure_cells, departure_fracs):
    cells = departure_cells
    fracs = departure_fracs
    nx, ny, nz = intensity.shape
    px, py, pz = nx + 2 * MARGIN, ny + 2 * MARGIN, nz + 128
    block = (nx, ny, nz)
    f32 = jnp.float32
    rolled = pltpu.VMEM((px, py, nz), f32)
    windows = pltpu.VMEM((SHIFTS, SHIFTS, px, ny, nz), f32)
    products = pltpu.VMEM((SHIFTS, SHIFTS) + block, f32)
    staged = pltpu.VMEM((SHIFTS, px, ny + 16, nz), f32)

    wrapped = widen(intensity, pz)
    image_mid, grad_raw = vmem_call(
        early_sample_kernel,
        (jax.ShapeDtypeStruct(block, f32), jax.ShapeDtypeStruct((3,) + block, f32)),
        [rolled, windows] + table_scratch(block, 6),
        wrapped, cells, fracs,
    )
    adjoint_padded = vmem_call(
        late_spread_kernel,
        jax.ShapeDtypeStruct((px, py, pz), f32),
        [products, staged] + table_scratch(block, 3),
        cotangent, cells, fracs,
    )
    adjoint_mid = fold(adjoint_padded[None], nz)[0]
    early_padded = vmem_call(
        early_spread_kernel,
        jax.ShapeDtypeStruct((4, px, py, pz), f32),
        [products, staged] + table_scratch(block, 6),
        adjoint_mid, grad_raw, cells, fracs,
    )
    wrapped_mid = widen(image_mid, pz)
    velocity_padded = vmem_call(
        late_velocity_kernel,
        jax.ShapeDtypeStruct((3, px, py, pz), f32),
        [rolled, windows, products, staged] + table_scratch(block, 9),
        wrapped_mid, cotangent, cells, fracs,
    )
    deposits = jnp.concatenate([early_padded[:1], early_padded[1:] + velocity_padded])
    folded = fold(deposits, nz)
    return (folded[0], folded[1:])


def solution(mesh):
    in_specs = (
        P("gx", "gy", "gz"),
        P("gx", "gy", "gz"),
        P(None, None, None, "gx", "gy", "gz"),
        P(None, None, None, "gx", "gy", "gz"),
    )
    out_specs = (P("gx", "gy", "gz"), P(None, "gx", "gy", "gz"))
    return jax.shard_map(body, mesh=mesh, in_specs=in_specs, out_specs=out_specs, check_vma=False)
```

```python
import functools

import jax
import jax.numpy as jnp
from jax import lax
from jax.experimental import pallas as pl
from jax.experimental.pallas import tpu as pltpu
from jax.sharding import PartitionSpec as P

MARGIN = 4
SHIFTS = 8
AXES = (("gx", 0), ("gy", 1), ("gz", 2))


def cubic_taps(fraction):
    fraction_squared = fraction * fraction
    fraction_cubed = fraction_squared * fraction
    weights = [
        0.5 * (2.0 * fraction_squared - fraction_cubed - fraction),
        0.5 * (3.0 * fraction_cubed - 5.0 * fraction_squared + 2.0),
        0.5 * (4.0 * fraction_squared - 3.0 * fraction_cubed + fraction),
        0.5 * (fraction_cubed - fraction_squared),
    ]
    slopes = [
        0.5 * (4.0 * fraction - 3.0 * fraction_squared - 1.0),
        0.5 * (9.0 * fraction_squared - 10.0 * fraction),
        0.5 * (8.0 * fraction - 9.0 * fraction_squared + 1.0),
        0.5 * (3.0 * fraction_squared - 2.0 * fraction),
    ]
    return (weights, slopes)


def build_tables(cells_ref, fracs_ref, step, section, weight_refs, slope_refs):
    for component in range(3):
        offsets = cells_ref[step, section, component]
        weights, slopes = cubic_taps(fracs_ref[step, section, component])
        for shift in range(SHIFTS):
            target = shift - 3
            summed = jnp.zeros(offsets.shape, jnp.float32)
            slope_sum = jnp.zeros(offsets.shape, jnp.float32)
            for tap_index in range(4):
                hit = offsets + (tap_index - 1) == target
                summed = summed + jnp.where(hit, weights[tap_index], 0.0)
                if slope_refs is not None:
                    slope_sum = slope_sum + jnp.where(hit, slopes[tap_index], 0.0)
            weight_refs[component][shift] = summed
            if slope_refs is not None:
                slope_refs[component][shift] = slope_sum


def roll_lanes(field, shift):
    shift = shift % field.shape[-1]
    if shift == 0:
        return field
    return pltpu.roll(field, shift, field.ndim - 1)


def sample_block(wrapped_ref, rolled_ref, window_ref, weight_refs, slope_refs, with_value):
    px, py, pz = wrapped_ref.shape
    nx, ny, nz = px - 2 * MARGIN, py - 2 * MARGIN, window_ref.shape[-1]
    field = wrapped_ref[...]
    for sz in range(SHIFTS):
        rolled_ref[...] = roll_lanes(field, 3 - sz)[:, :, :nz]
        for sy in range(SHIFTS):
            window_ref[sy, sz] = rolled_ref[:, sy + 1 : sy + 1 + ny, :]
    table_x, table_y, table_z = weight_refs
    shape = (nx, ny, nz)

    def along_y(sy, carry):
        value, grad_x, grad_y, grad_z = carry
        along_x = jnp.zeros(shape, jnp.float32)
        along_x_slope = jnp.zeros(shape, jnp.float32)
        along_x_zslope = jnp.zeros(shape, jnp.float32)
        for sx in range(SHIFTS):
            column = jnp.zeros(shape, jnp.float32)
            slope_column = jnp.zeros(shape, jnp.float32)
            for sz in range(SHIFTS):
                window = window_ref[sy, sz, sx + 1 : sx + 1 + nx]
                column = column + table_z[sz] * window
                if slope_refs is not None:
                    slope_column = slope_column + slope_refs[2][sz] * window
            along_x = along_x + table_x[sx] * column
            if slope_refs is not None:
                along_x_slope = along_x_slope + slope_refs[0][sx] * column
                along_x_zslope = along_x_zslope + table_x[sx] * slope_column
        weight_y = table_y[sy]
        if with_value:
            value = value + weight_y * along_x
        if slope_refs is not None:
            grad_x = grad_x + weight_y * along_x_slope
            grad_y = grad_y + slope_refs[1][sy] * along_x
            grad_z = grad_z + weight_y * along_x_zslope
        return value, grad_x, grad_y, grad_z

    zero = jnp.zeros(shape, jnp.float32)
    value, grad_x, grad_y, grad_z = lax.fori_loop(0, SHIFTS, along_y, (zero,) * 4)
    return value, (grad_x, grad_y, grad_z)


def spread_block(field, weight_refs, product_ref, staged_ref, summed_ref, pz):
    table_x, table_y, table_z = weight_refs
    nx, ny, nz = field.shape
    px, py = nx + 2 * MARGIN, ny + 2 * MARGIN
    for sy in range(SHIFTS):
        weighted = table_y[sy] * field
        for sx in range(SHIFTS):
            product_ref[sy, sx] = table_x[sx] * weighted
    def along_z(sz, carry):
        weight_z = table_z[sz]
        for sy in range(SHIFTS):
            rows = [None] * px
            for sx in range(SHIFTS):
                deposit = weight_z * product_ref[sy, sx]
                for x in range(nx):
                    slot = x + sx + 1
                    rows[slot] = deposit[x] if rows[slot] is None else rows[slot] + deposit[x]
            rows[0] = jnp.zeros((ny, nz), jnp.float32)
            for slot in range(px):
                staged_ref[sy, slot, 8 : 8 + ny, :] = rows[slot]
        summed = jnp.zeros((px, py, nz), jnp.float32)
        for sy in range(SHIFTS):
            summed = summed + staged_ref[sy, :, 7 - sy : 7 - sy + py, :]
        summed_ref[sz] = summed
        return carry

    lax.fori_loop(0, SHIFTS, along_z, 0)
    total = jnp.zeros((px, py, pz), jnp.float32)
    gap = jnp.zeros((px, py, pz - nz), jnp.float32)
    for sz in range(SHIFTS):
        padded = jnp.concatenate([summed_ref[sz], gap], axis=2)
        total = total + roll_lanes(padded, sz - 3)
    return total


def table_scratch(shape, count):
    return [pltpu.VMEM((SHIFTS,) + shape, jnp.float32) for _ in range(count)]


def clear_rims(staged_ref):
    staged_ref[...] = jnp.zeros(staged_ref.shape, jnp.float32)


def early_sample_kernel(wrapped_ref, cells_ref, fracs_ref, image_ref, grad_ref,
                        rolled_ref, window_ref, *tables):
    weights, slopes = tables[:3], tables[3:]
    build_tables(cells_ref, fracs_ref, 0, 1, weights, slopes)
    value, grads = sample_block(wrapped_ref, rolled_ref, window_ref, weights, slopes, True)
    image_ref[...] = value
    for component in range(3):
        grad_ref[component] = grads[component]


def late_spread_kernel(cot_ref, cells_ref, fracs_ref, out_ref, product_ref, staged_ref, summed_ref, *tables):
    build_tables(cells_ref, fracs_ref, 1, 1, tables, None)
    clear_rims(staged_ref)
    out_ref[...] = spread_block(cot_ref[...], tables, product_ref, staged_ref, summed_ref,
                                out_ref.shape[-1])


def late_velocity_kernel(wrapped_ref, cot_ref, cells_ref, fracs_ref, out_ref,
                         rolled_ref, window_ref, product_ref, staged_ref, summed_ref, *tables):
    weights, slopes, mid = tables[:3], tables[3:6], tables[6:]
    build_tables(cells_ref, fracs_ref, 1, 1, weights, slopes)
    build_tables(cells_ref, fracs_ref, 1, 0, mid, None)
    _, grads = sample_block(wrapped_ref, rolled_ref, window_ref, weights, slopes, False)
    cot = cot_ref[...]
    clear_rims(staged_ref)
    for component in range(3):
        out_ref[component] = spread_block(cot * grads[component], mid, product_ref, staged_ref, summed_ref,
                                          out_ref.shape[-1])


def early_spread_kernel(adjoint_ref, grad_ref, cells_ref, fracs_ref, out_ref,
                        product_ref, staged_ref, summed_ref, *tables):
    dep, mid = tables[:3], tables[3:]
    build_tables(cells_ref, fracs_ref, 0, 1, dep, None)
    build_tables(cells_ref, fracs_ref, 0, 0, mid, None)
    adjoint = adjoint_ref[...]
    clear_rims(staged_ref)
    pz = out_ref.shape[-1]
    out_ref[0] = spread_block(adjoint, dep, product_ref, staged_ref, summed_ref, pz)
    for component in range(3):
        out_ref[1 + component] = spread_block(adjoint * grad_ref[component], mid, product_ref,
                                              staged_ref, summed_ref, pz)


def vmem_call(kernel, out_shapes, scratch, *args):
    return pl.pallas_call(
        kernel,
        out_shape=out_shapes,
        in_specs=[pl.BlockSpec(memory_space=pltpu.VMEM)] * len(args),
        out_specs=jax.tree.map(lambda _: pl.BlockSpec(memory_space=pltpu.VMEM), out_shapes),
        scratch_shapes=scratch,
        compiler_params=pltpu.CompilerParams(vmem_limit_bytes=48 * 1024 * 1024),
        cost_estimate=pl.CostEstimate(
            flops=40_000_000, transcendentals=0, bytes_accessed=2_000_000
        ),
    )(*args)


def shift_from(piece, axis, upward):
    count = lax.axis_size(axis)
    if upward:
        pairs = [(i, (i + 1) % count) for i in range(count)]
    else:
        pairs = [((i + 1) % count, i) for i in range(count)]
    shape = piece.shape
    if shape[-1] < 128 and piece.size % 1024 == 0:
        flat = lax.ppermute(piece.reshape(-1, 128), axis, pairs)
        return flat.reshape(shape)
    return lax.ppermute(piece, axis, pairs)


def widen(block, pz):
    for axis, dim in AXES[:2]:
        size = block.shape[dim]
        head = lax.slice_in_dim(block, 0, MARGIN, axis=dim)
        tail = lax.slice_in_dim(block, size - MARGIN, size, axis=dim)
        block = jnp.concatenate(
            [shift_from(tail, axis, True), block, shift_from(head, axis, False)], axis=dim
        )
    nz = block.shape[2]
    head = block[:, :, :MARGIN]
    tail = block[:, :, nz - MARGIN :]
    gap = jnp.zeros(block.shape[:2] + (pz - nz - 2 * MARGIN,), jnp.float32)
    return jnp.concatenate(
        [block, shift_from(head, "gz", False), gap, shift_from(tail, "gz", True)], axis=2
    )


def place_rim(rim, dim, start, size):
    widths = [(0, 0)] * rim.ndim
    widths[dim] = (start, size - start - rim.shape[dim])
    return jnp.pad(rim, widths)


def fold(wrapped, nz):
    pz = wrapped.shape[3]
    upper = wrapped[..., nz : nz + MARGIN]
    lower = wrapped[..., pz - MARGIN :]
    block = wrapped[..., :nz]
    from_below = shift_from(upper, "gz", True)
    from_above = shift_from(lower, "gz", False)
    block = block + place_rim(from_below, 3, 0, nz)
    block = block + place_rim(from_above, 3, nz - MARGIN, nz)
    for axis, dim in (("gy", 2), ("gx", 1)):
        size = block.shape[dim] - 2 * MARGIN
        low = lax.slice_in_dim(block, 0, MARGIN, axis=dim)
        high = lax.slice_in_dim(block, size + MARGIN, size + 2 * MARGIN, axis=dim)
        block = lax.slice_in_dim(block, MARGIN, size + MARGIN, axis=dim)
        got_low = shift_from(high, axis, True)
        got_high = shift_from(low, axis, False)
        block = block + place_rim(got_low, dim, 0, size)
        block = block + place_rim(got_high, dim, size - MARGIN, size)
    return block


def body(intensity, cotangent, departure_cells, departure_fracs):
    cells = departure_cells
    fracs = departure_fracs
    nx, ny, nz = intensity.shape
    px, py, pz = nx + 2 * MARGIN, ny + 2 * MARGIN, nz + 128
    block = (nx, ny, nz)
    f32 = jnp.float32
    rolled = pltpu.VMEM((px, py, nz), f32)
    windows = pltpu.VMEM((SHIFTS, SHIFTS, px, ny, nz), f32)
    products = pltpu.VMEM((SHIFTS, SHIFTS) + block, f32)
    staged = pltpu.VMEM((SHIFTS, px, ny + 16, nz), f32)
    summed = pltpu.VMEM((SHIFTS, px, py, nz), f32)

    wrapped = widen(intensity, pz)
    image_mid, grad_raw = vmem_call(
        early_sample_kernel,
        (jax.ShapeDtypeStruct(block, f32), jax.ShapeDtypeStruct((3,) + block, f32)),
        [rolled, windows] + table_scratch(block, 6),
        wrapped, cells, fracs,
    )
    adjoint_padded = vmem_call(
        late_spread_kernel,
        jax.ShapeDtypeStruct((px, py, pz), f32),
        [products, staged, summed] + table_scratch(block, 3),
        cotangent, cells, fracs,
    )
    adjoint_mid = fold(adjoint_padded[None], nz)[0]
    early_padded = vmem_call(
        early_spread_kernel,
        jax.ShapeDtypeStruct((4, px, py, pz), f32),
        [products, staged, summed] + table_scratch(block, 6),
        adjoint_mid, grad_raw, cells, fracs,
    )
    wrapped_mid = widen(image_mid, pz)
    velocity_padded = vmem_call(
        late_velocity_kernel,
        jax.ShapeDtypeStruct((3, px, py, pz), f32),
        [rolled, windows, products, staged, summed] + table_scratch(block, 9),
        wrapped_mid, cotangent, cells, fracs,
    )
    deposits = jnp.concatenate([early_padded[:1], early_padded[1:] + velocity_padded])
    folded = fold(deposits, nz)
    return (folded[0], folded[1:])


def solution(mesh):
    in_specs = (
        P("gx", "gy", "gz"),
        P("gx", "gy", "gz"),
        P(None, None, None, "gx", "gy", "gz"),
        P(None, None, None, "gx", "gy", "gz"),
    )
    out_specs = (P("gx", "gy", "gz"), P(None, "gx", "gy", "gz"))
    return jax.shard_map(body, mesh=mesh, in_specs=in_specs, out_specs=out_specs, check_vma=False)
```

```python
import functools

import jax
import jax.numpy as jnp
from jax import lax
from jax.experimental import pallas as pl
from jax.experimental.pallas import tpu as pltpu
from jax.sharding import PartitionSpec as P

MARGIN = 4
SHIFTS = 8
AXES = (("gx", 0), ("gy", 1), ("gz", 2))


def cubic_taps(fraction):
    fraction_squared = fraction * fraction
    fraction_cubed = fraction_squared * fraction
    weights = [
        0.5 * (2.0 * fraction_squared - fraction_cubed - fraction),
        0.5 * (3.0 * fraction_cubed - 5.0 * fraction_squared + 2.0),
        0.5 * (4.0 * fraction_squared - 3.0 * fraction_cubed + fraction),
        0.5 * (fraction_cubed - fraction_squared),
    ]
    slopes = [
        0.5 * (4.0 * fraction - 3.0 * fraction_squared - 1.0),
        0.5 * (9.0 * fraction_squared - 10.0 * fraction),
        0.5 * (8.0 * fraction - 9.0 * fraction_squared + 1.0),
        0.5 * (3.0 * fraction_squared - 2.0 * fraction),
    ]
    return (weights, slopes)


def build_tables(cells_ref, fracs_ref, step, section, weight_refs, slope_refs):
    for component in range(3):
        offsets = cells_ref[step, section, component]
        weights, slopes = cubic_taps(fracs_ref[step, section, component])
        for shift in range(SHIFTS):
            target = shift - 3
            summed = jnp.zeros(offsets.shape, jnp.float32)
            slope_sum = jnp.zeros(offsets.shape, jnp.float32)
            for tap_index in range(4):
                hit = offsets + (tap_index - 1) == target
                summed = summed + jnp.where(hit, weights[tap_index], 0.0)
                if slope_refs is not None:
                    slope_sum = slope_sum + jnp.where(hit, slopes[tap_index], 0.0)
            weight_refs[component][shift] = summed
            if slope_refs is not None:
                slope_refs[component][shift] = slope_sum


def roll_lanes(field, shift):
    shift = shift % field.shape[-1]
    if shift == 0:
        return field
    return pltpu.roll(field, shift, field.ndim - 1)


def sample_block(wrapped_ref, rolled_ref, window_ref, weight_refs, slope_refs, with_value):
    px, py, pz = wrapped_ref.shape
    nx, ny, nz = px - 2 * MARGIN, py - 2 * MARGIN, window_ref.shape[-1]
    field = wrapped_ref[...]
    for sz in range(SHIFTS):
        rolled_ref[...] = roll_lanes(field, 3 - sz)[:, :, :nz]
        for sy in range(SHIFTS):
            window_ref[sy, sz] = rolled_ref[:, sy + 1 : sy + 1 + ny, :]
    table_x, table_y, table_z = weight_refs
    shape = (nx, ny, nz)

    def along_y(sy, carry):
        value, grad_x, grad_y, grad_z = carry
        along_x = jnp.zeros(shape, jnp.float32)
        along_x_slope = jnp.zeros(shape, jnp.float32)
        along_x_zslope = jnp.zeros(shape, jnp.float32)
        for sx in range(SHIFTS):
            column = jnp.zeros(shape, jnp.float32)
            slope_column = jnp.zeros(shape, jnp.float32)
            for sz in range(SHIFTS):
                window = window_ref[sy, sz, sx + 1 : sx + 1 + nx]
                column = column + table_z[sz] * window
                if slope_refs is not None:
                    slope_column = slope_column + slope_refs[2][sz] * window
            along_x = along_x + table_x[sx] * column
            if slope_refs is not None:
                along_x_slope = along_x_slope + slope_refs[0][sx] * column
                along_x_zslope = along_x_zslope + table_x[sx] * slope_column
        weight_y = table_y[sy]
        if with_value:
            value = value + weight_y * along_x
        if slope_refs is not None:
            grad_x = grad_x + weight_y * along_x_slope
            grad_y = grad_y + slope_refs[1][sy] * along_x
            grad_z = grad_z + weight_y * along_x_zslope
        return value, grad_x, grad_y, grad_z

    zero = jnp.zeros(shape, jnp.float32)
    value, grad_x, grad_y, grad_z = lax.fori_loop(0, SHIFTS, along_y, (zero,) * 4)
    return value, (grad_x, grad_y, grad_z)


def spread_block(field, weight_refs, product_ref, staged_ref, summed_ref, pz):
    table_x, table_y, table_z = weight_refs
    nx, ny, nz = field.shape
    px, py = nx + 2 * MARGIN, ny + 2 * MARGIN
    for sy in range(SHIFTS):
        weighted = table_y[sy] * field
        for sx in range(SHIFTS):
            product_ref[sy, sx] = table_x[sx] * weighted
    def along_z(sz, carry):
        weight_z = table_z[sz]
        for sy in range(SHIFTS):
            rows = [None] * px
            for sx in range(SHIFTS):
                deposit = weight_z * product_ref[sy, sx]
                for x in range(nx):
                    slot = x + sx + 1
                    rows[slot] = deposit[x] if rows[slot] is None else rows[slot] + deposit[x]
            rows[0] = jnp.zeros((ny, nz), jnp.float32)
            for slot in range(px):
                staged_ref[sy, slot, 8 : 8 + ny, :] = rows[slot]
        summed = jnp.zeros((px, py, nz), jnp.float32)
        for sy in range(SHIFTS):
            summed = summed + staged_ref[sy, :, 7 - sy : 7 - sy + py, :]
        summed_ref[sz] = summed
        return carry

    lax.fori_loop(0, SHIFTS, along_z, 0)
    total = jnp.zeros((px, py, pz), jnp.float32)
    gap = jnp.zeros((px, py, pz - nz), jnp.float32)
    for sz in range(SHIFTS):
        padded = jnp.concatenate([summed_ref[sz], gap], axis=2)
        total = total + roll_lanes(padded, sz - 3)
    return total


def table_scratch(shape, count):
    return [pltpu.VMEM((SHIFTS,) + shape, jnp.float32) for _ in range(count)]


def clear_rims(staged_ref):
    staged_ref[...] = jnp.zeros(staged_ref.shape, jnp.float32)


def early_sample_kernel(wrapped_ref, cells_ref, fracs_ref, image_ref, grad_ref,
                        rolled_ref, window_ref, *tables):
    weights, slopes = tables[:3], tables[3:]
    build_tables(cells_ref, fracs_ref, 0, 1, weights, slopes)
    value, grads = sample_block(wrapped_ref, rolled_ref, window_ref, weights, slopes, True)
    image_ref[...] = value
    for component in range(3):
        grad_ref[component] = grads[component]


def late_spread_kernel(cot_ref, cells_ref, fracs_ref, out_ref, product_ref, staged_ref, summed_ref, *tables):
    build_tables(cells_ref, fracs_ref, 1, 1, tables, None)
    clear_rims(staged_ref)
    out_ref[...] = spread_block(cot_ref[...], tables, product_ref, staged_ref, summed_ref,
                                out_ref.shape[-1])


def late_velocity_kernel(wrapped_ref, cot_ref, cells_ref, fracs_ref, out_ref,
                         rolled_ref, window_ref, product_ref, staged_ref, summed_ref, *tables):
    weights, slopes, mid = tables[:3], tables[3:6], tables[6:]
    build_tables(cells_ref, fracs_ref, 1, 1, weights, slopes)
    build_tables(cells_ref, fracs_ref, 1, 0, mid, None)
    _, grads = sample_block(wrapped_ref, rolled_ref, window_ref, weights, slopes, False)
    cot = cot_ref[...]
    clear_rims(staged_ref)
    for component in range(3):
        out_ref[component] = spread_block(cot * grads[component], mid, product_ref, staged_ref, summed_ref,
                                          out_ref.shape[-1])


def early_spread_kernel(adjoint_ref, grad_ref, cells_ref, fracs_ref, out_ref,
                        product_ref, staged_ref, summed_ref, *tables):
    dep, mid = tables[:3], tables[3:]
    build_tables(cells_ref, fracs_ref, 0, 1, dep, None)
    build_tables(cells_ref, fracs_ref, 0, 0, mid, None)
    adjoint = adjoint_ref[...]
    clear_rims(staged_ref)
    pz = out_ref.shape[-1]
    out_ref[0] = spread_block(adjoint, dep, product_ref, staged_ref, summed_ref, pz)
    for component in range(3):
        out_ref[1 + component] = spread_block(adjoint * grad_ref[component], mid, product_ref,
                                              staged_ref, summed_ref, pz)


def vmem_call(kernel, out_shapes, scratch, *args):
    return pl.pallas_call(
        kernel,
        out_shape=out_shapes,
        in_specs=[pl.BlockSpec(memory_space=pltpu.VMEM)] * len(args),
        out_specs=jax.tree.map(lambda _: pl.BlockSpec(memory_space=pltpu.VMEM), out_shapes),
        scratch_shapes=scratch,
        compiler_params=pltpu.CompilerParams(vmem_limit_bytes=48 * 1024 * 1024),
        cost_estimate=pl.CostEstimate(
            flops=40_000_000, transcendentals=0, bytes_accessed=2_000_000
        ),
    )(*args)


def shift_from(piece, axis, upward):
    count = lax.axis_size(axis)
    if upward:
        pairs = [(i, (i + 1) % count) for i in range(count)]
    else:
        pairs = [((i + 1) % count, i) for i in range(count)]
    shape = piece.shape
    if shape[-1] < 128 and piece.size % 1024 == 0:
        flat = lax.ppermute(piece.reshape(-1, 128), axis, pairs)
        return flat.reshape(shape)
    return lax.ppermute(piece, axis, pairs)


def widen(block, pz):
    for axis, dim in AXES[:2]:
        size = block.shape[dim]
        head = lax.slice_in_dim(block, 0, MARGIN, axis=dim)
        tail = lax.slice_in_dim(block, size - MARGIN, size, axis=dim)
        block = jnp.concatenate(
            [shift_from(tail, axis, True), block, shift_from(head, axis, False)], axis=dim
        )
    nz = block.shape[2]
    head = block[:, :, :MARGIN]
    tail = block[:, :, nz - MARGIN :]
    gap = jnp.zeros(block.shape[:2] + (pz - nz - 2 * MARGIN,), jnp.float32)
    return jnp.concatenate(
        [block, shift_from(head, "gz", False), gap, shift_from(tail, "gz", True)], axis=2
    )


def place_rim(rim, dim, start, size):
    widths = [(0, 0)] * rim.ndim
    widths[dim] = (start, size - start - rim.shape[dim])
    return jnp.pad(rim, widths)


def fold(wrapped, nz):
    pz = wrapped.shape[3]
    upper = wrapped[..., nz : nz + MARGIN]
    lower = wrapped[..., pz - MARGIN :]
    block = wrapped[..., :nz]
    from_below = shift_from(upper, "gz", True)
    from_above = shift_from(lower, "gz", False)
    block = block + place_rim(from_below, 3, 0, nz)
    block = block + place_rim(from_above, 3, nz - MARGIN, nz)
    for axis, dim in (("gy", 2), ("gx", 1)):
        size = block.shape[dim] - 2 * MARGIN
        low = lax.slice_in_dim(block, 0, MARGIN, axis=dim)
        high = lax.slice_in_dim(block, size + MARGIN, size + 2 * MARGIN, axis=dim)
        block = lax.slice_in_dim(block, MARGIN, size + MARGIN, axis=dim)
        got_low = shift_from(high, axis, True)
        got_high = shift_from(low, axis, False)
        block = block + place_rim(got_low, dim, 0, size)
        block = block + place_rim(got_high, dim, size - MARGIN, size)
    return block


def joint_exchange(block, deposit, pz):
    nz = block.shape[2]

    def trade(axis, up_pieces, down_pieces):
        results = []
        for pieces, upward in ((up_pieces, True), (down_pieces, False)):
            flat = jnp.concatenate([piece.reshape(-1, 128) for piece in pieces])
            got = lax.ppermute(flat, axis, [
                ((i, (i + 1) % lax.axis_size(axis)) if upward
                 else ((i + 1) % lax.axis_size(axis), i))
                for i in range(lax.axis_size(axis))
            ])
            parts, start = [], 0
            for piece in pieces:
                rows = piece.size // 128
                parts.append(got[start : start + rows].reshape(piece.shape))
                start += rows
            results.append(parts)
        return results

    for axis, dim in AXES[:2]:
        size = block.shape[dim]
        head = lax.slice_in_dim(block, 0, MARGIN, axis=dim)
        tail = lax.slice_in_dim(block, size - MARGIN, size, axis=dim)
        low = lax.slice_in_dim(deposit, 0, MARGIN, axis=dim)
        high = lax.slice_in_dim(deposit, size + MARGIN, size + 2 * MARGIN, axis=dim)
        (below, got_low), (above, got_high) = trade(axis, [tail, high], [head, low])
        block = jnp.concatenate([below, block, above], axis=dim)
        deposit = lax.slice_in_dim(deposit, MARGIN, size + MARGIN, axis=dim)
        deposit = deposit + place_rim(got_low, dim, 0, size)
        deposit = deposit + place_rim(got_high, dim, size - MARGIN, size)
    head = block[:, :, :MARGIN]
    tail = block[:, :, nz - MARGIN :]
    upper = deposit[..., nz : nz + MARGIN]
    lower = deposit[..., pz - MARGIN :]
    (below, from_below), (above, from_above) = trade("gz", [tail, upper], [head, lower])
    gap = jnp.zeros(block.shape[:2] + (pz - nz - 2 * MARGIN,), jnp.float32)
    wrapped = jnp.concatenate([block, above, gap, below], axis=2)
    folded = deposit[..., :nz]
    folded = folded + place_rim(from_below, 2, 0, nz)
    folded = folded + place_rim(from_above, 2, nz - MARGIN, nz)
    return wrapped, folded


def body(intensity, cotangent, departure_cells, departure_fracs):
    cells = departure_cells
    fracs = departure_fracs
    nx, ny, nz = intensity.shape
    px, py, pz = nx + 2 * MARGIN, ny + 2 * MARGIN, nz + 128
    block = (nx, ny, nz)
    f32 = jnp.float32
    rolled = pltpu.VMEM((px, py, nz), f32)
    windows = pltpu.VMEM((SHIFTS, SHIFTS, px, ny, nz), f32)
    products = pltpu.VMEM((SHIFTS, SHIFTS) + block, f32)
    staged = pltpu.VMEM((SHIFTS, px, ny + 16, nz), f32)
    summed = pltpu.VMEM((SHIFTS, px, py, nz), f32)

    adjoint_padded = vmem_call(
        late_spread_kernel,
        jax.ShapeDtypeStruct((px, py, pz), f32),
        [products, staged, summed] + table_scratch(block, 3),
        cotangent, cells, fracs,
    )
    wrapped, adjoint_mid = joint_exchange(intensity, adjoint_padded, pz)
    image_mid, grad_raw = vmem_call(
        early_sample_kernel,
        (jax.ShapeDtypeStruct(block, f32), jax.ShapeDtypeStruct((3,) + block, f32)),
        [rolled, windows] + table_scratch(block, 6),
        wrapped, cells, fracs,
    )
    early_padded = vmem_call(
        early_spread_kernel,
        jax.ShapeDtypeStruct((4, px, py, pz), f32),
        [products, staged, summed] + table_scratch(block, 6),
        adjoint_mid, grad_raw, cells, fracs,
    )
    wrapped_mid = widen(image_mid, pz)
    velocity_padded = vmem_call(
        late_velocity_kernel,
        jax.ShapeDtypeStruct((3, px, py, pz), f32),
        [rolled, windows, products, staged, summed] + table_scratch(block, 9),
        wrapped_mid, cotangent, cells, fracs,
    )
    deposits = jnp.concatenate([early_padded[:1], early_padded[1:] + velocity_padded])
    folded = fold(deposits, nz)
    return (folded[0], folded[1:])


def solution(mesh):
    in_specs = (
        P("gx", "gy", "gz"),
        P("gx", "gy", "gz"),
        P(None, None, None, "gx", "gy", "gz"),
        P(None, None, None, "gx", "gy", "gz"),
    )
    out_specs = (P("gx", "gy", "gz"), P(None, "gx", "gy", "gz"))
    return jax.shard_map(body, mesh=mesh, in_specs=in_specs, out_specs=out_specs, check_vma=False)
```

```python
import functools

import jax
import jax.numpy as jnp
from jax import lax
from jax.experimental import pallas as pl
from jax.experimental.pallas import tpu as pltpu
from jax.sharding import PartitionSpec as P

MARGIN = 4
SHIFTS = 8
AXES = (("gx", 0), ("gy", 1), ("gz", 2))


def cubic_taps(fraction):
    fraction_squared = fraction * fraction
    fraction_cubed = fraction_squared * fraction
    weights = [
        0.5 * (2.0 * fraction_squared - fraction_cubed - fraction),
        0.5 * (3.0 * fraction_cubed - 5.0 * fraction_squared + 2.0),
        0.5 * (4.0 * fraction_squared - 3.0 * fraction_cubed + fraction),
        0.5 * (fraction_cubed - fraction_squared),
    ]
    slopes = [
        0.5 * (4.0 * fraction - 3.0 * fraction_squared - 1.0),
        0.5 * (9.0 * fraction_squared - 10.0 * fraction),
        0.5 * (8.0 * fraction - 9.0 * fraction_squared + 1.0),
        0.5 * (3.0 * fraction_squared - 2.0 * fraction),
    ]
    return (weights, slopes)


def build_tables(cells_ref, fracs_ref, step, section, weight_refs, slope_refs):
    for component in range(3):
        offsets = cells_ref[step, section, component]
        weights, slopes = cubic_taps(fracs_ref[step, section, component])
        for shift in range(SHIFTS):
            target = shift - 3
            summed = jnp.zeros(offsets.shape, jnp.float32)
            slope_sum = jnp.zeros(offsets.shape, jnp.float32)
            for tap_index in range(4):
                hit = offsets + (tap_index - 1) == target
                summed = summed + jnp.where(hit, weights[tap_index], 0.0)
                if slope_refs is not None:
                    slope_sum = slope_sum + jnp.where(hit, slopes[tap_index], 0.0)
            weight_refs[component][shift] = summed
            if slope_refs is not None:
                slope_refs[component][shift] = slope_sum


def roll_lanes(field, shift):
    shift = shift % field.shape[-1]
    if shift == 0:
        return field
    return pltpu.roll(field, shift, field.ndim - 1)


def sample_block(wrapped_ref, rolled_ref, window_ref, weight_refs, slope_refs, with_value):
    px, py, pz = wrapped_ref.shape
    nx, ny, nz = px - 2 * MARGIN, py - 2 * MARGIN, window_ref.shape[-1]
    field = wrapped_ref[...]
    for sz in range(SHIFTS):
        rolled_ref[...] = roll_lanes(field, 3 - sz)[:, :, :nz]
        for sy in range(SHIFTS):
            window_ref[sy, sz] = rolled_ref[:, sy + 1 : sy + 1 + ny, :]
    table_x, table_y, table_z = weight_refs
    shape = (nx, ny, nz)

    def along_y(sy, carry):
        value, grad_x, grad_y, grad_z = carry
        along_x = jnp.zeros(shape, jnp.float32)
        along_x_slope = jnp.zeros(shape, jnp.float32)
        along_x_zslope = jnp.zeros(shape, jnp.float32)
        for sx in range(SHIFTS):
            column = jnp.zeros(shape, jnp.float32)
            slope_column = jnp.zeros(shape, jnp.float32)
            for sz in range(SHIFTS):
                window = window_ref[sy, sz, sx + 1 : sx + 1 + nx]
                column = column + table_z[sz] * window
                if slope_refs is not None:
                    slope_column = slope_column + slope_refs[2][sz] * window
            along_x = along_x + table_x[sx] * column
            if slope_refs is not None:
                along_x_slope = along_x_slope + slope_refs[0][sx] * column
                along_x_zslope = along_x_zslope + table_x[sx] * slope_column
        weight_y = table_y[sy]
        if with_value:
            value = value + weight_y * along_x
        if slope_refs is not None:
            grad_x = grad_x + weight_y * along_x_slope
            grad_y = grad_y + slope_refs[1][sy] * along_x
            grad_z = grad_z + weight_y * along_x_zslope
        return value, grad_x, grad_y, grad_z

    zero = jnp.zeros(shape, jnp.float32)
    value, grad_x, grad_y, grad_z = lax.fori_loop(0, SHIFTS, along_y, (zero,) * 4)
    return value, (grad_x, grad_y, grad_z)


def spread_block(field, weight_refs, product_ref, staged_ref, summed_ref, pz):
    table_x, table_y, table_z = weight_refs
    nx, ny, nz = field.shape
    px, py = nx + 2 * MARGIN, ny + 2 * MARGIN
    for sy in range(SHIFTS):
        weighted = table_y[sy] * field
        for sx in range(SHIFTS):
            product_ref[sy, sx] = table_x[sx] * weighted
    def along_z(sz, carry):
        weight_z = table_z[sz]
        for sy in range(SHIFTS):
            rows = [None] * px
            for sx in range(SHIFTS):
                deposit = weight_z * product_ref[sy, sx]
                for x in range(nx):
                    slot = x + sx + 1
                    rows[slot] = deposit[x] if rows[slot] is None else rows[slot] + deposit[x]
            rows[0] = jnp.zeros((ny, nz), jnp.float32)
            for slot in range(px):
                staged_ref[sy, slot, 8 : 8 + ny, :] = rows[slot]
        summed = jnp.zeros((px, py, nz), jnp.float32)
        for sy in range(SHIFTS):
            summed = summed + staged_ref[sy, :, 7 - sy : 7 - sy + py, :]
        summed_ref[sz] = summed
        return carry

    lax.fori_loop(0, SHIFTS, along_z, 0)
    total = jnp.zeros((px, py, pz), jnp.float32)
    gap = jnp.zeros((px, py, pz - nz), jnp.float32)
    for sz in range(SHIFTS):
        padded = jnp.concatenate([summed_ref[sz], gap], axis=2)
        total = total + roll_lanes(padded, sz - 3)
    return total


def table_scratch(shape, count):
    return [pltpu.VMEM((SHIFTS,) + shape, jnp.float32) for _ in range(count)]


def clear_rims(staged_ref):
    staged_ref[...] = jnp.zeros(staged_ref.shape, jnp.float32)


def early_sample_kernel(wrapped_ref, cells_ref, fracs_ref, image_ref, grad_ref,
                        rolled_ref, window_ref, *tables):
    weights, slopes = tables[:3], tables[3:]
    build_tables(cells_ref, fracs_ref, 0, 1, weights, slopes)
    value, grads = sample_block(wrapped_ref, rolled_ref, window_ref, weights, slopes, True)
    image_ref[...] = value
    for component in range(3):
        grad_ref[component] = grads[component]


def late_spread_kernel(cot_ref, cells_ref, fracs_ref, out_ref, product_ref, staged_ref, summed_ref, *tables):
    build_tables(cells_ref, fracs_ref, 1, 1, tables, None)
    clear_rims(staged_ref)
    out_ref[...] = spread_block(cot_ref[...], tables, product_ref, staged_ref, summed_ref,
                                out_ref.shape[-1])


def late_velocity_kernel(wrapped_ref, cot_ref, cells_ref, fracs_ref, out_ref,
                         rolled_ref, window_ref, product_ref, staged_ref, summed_ref, *tables):
    weights, slopes, mid = tables[:3], tables[3:6], tables[6:]
    build_tables(cells_ref, fracs_ref, 1, 1, weights, slopes)
    build_tables(cells_ref, fracs_ref, 1, 0, mid, None)
    _, grads = sample_block(wrapped_ref, rolled_ref, window_ref, weights, slopes, False)
    cot = cot_ref[...]
    clear_rims(staged_ref)
    for component in range(3):
        out_ref[component] = spread_block(cot * grads[component], mid, product_ref, staged_ref, summed_ref,
                                          out_ref.shape[-1])


def early_spread_kernel(adjoint_ref, grad_ref, cells_ref, fracs_ref, out_ref,
                        product_ref, staged_ref, summed_ref, *tables):
    dep, mid = tables[:3], tables[3:]
    build_tables(cells_ref, fracs_ref, 0, 1, dep, None)
    build_tables(cells_ref, fracs_ref, 0, 0, mid, None)
    adjoint = adjoint_ref[...]
    clear_rims(staged_ref)
    pz = out_ref.shape[-1]
    out_ref[0] = spread_block(adjoint, dep, product_ref, staged_ref, summed_ref, pz)
    for component in range(3):
        out_ref[1 + component] = spread_block(adjoint * grad_ref[component], mid, product_ref,
                                              staged_ref, summed_ref, pz)


def vmem_call(kernel, out_shapes, scratch, *args):
    return pl.pallas_call(
        kernel,
        out_shape=out_shapes,
        in_specs=[pl.BlockSpec(memory_space=pltpu.VMEM)] * len(args),
        out_specs=jax.tree.map(lambda _: pl.BlockSpec(memory_space=pltpu.VMEM), out_shapes),
        scratch_shapes=scratch,
        compiler_params=pltpu.CompilerParams(vmem_limit_bytes=48 * 1024 * 1024),
        cost_estimate=pl.CostEstimate(
            flops=4_000_000_000, transcendentals=0, bytes_accessed=2_000_000
        ),
    )(*args)


def shift_from(piece, axis, upward):
    count = lax.axis_size(axis)
    if upward:
        pairs = [(i, (i + 1) % count) for i in range(count)]
    else:
        pairs = [((i + 1) % count, i) for i in range(count)]
    shape = piece.shape
    if shape[-1] < 128 and piece.size % 1024 == 0:
        flat = lax.ppermute(piece.reshape(-1, 128), axis, pairs)
        return flat.reshape(shape)
    return lax.ppermute(piece, axis, pairs)


def widen(block, pz):
    for axis, dim in AXES[:2]:
        size = block.shape[dim]
        head = lax.slice_in_dim(block, 0, MARGIN, axis=dim)
        tail = lax.slice_in_dim(block, size - MARGIN, size, axis=dim)
        block = jnp.concatenate(
            [shift_from(tail, axis, True), block, shift_from(head, axis, False)], axis=dim
        )
    nz = block.shape[2]
    head = block[:, :, :MARGIN]
    tail = block[:, :, nz - MARGIN :]
    gap = jnp.zeros(block.shape[:2] + (pz - nz - 2 * MARGIN,), jnp.float32)
    return jnp.concatenate(
        [block, shift_from(head, "gz", False), gap, shift_from(tail, "gz", True)], axis=2
    )


def place_rim(rim, dim, start, size):
    widths = [(0, 0)] * rim.ndim
    widths[dim] = (start, size - start - rim.shape[dim])
    return jnp.pad(rim, widths)


def fold(wrapped, nz):
    pz = wrapped.shape[3]
    upper = wrapped[..., nz : nz + MARGIN]
    lower = wrapped[..., pz - MARGIN :]
    block = wrapped[..., :nz]
    from_below = shift_from(upper, "gz", True)
    from_above = shift_from(lower, "gz", False)
    block = block + place_rim(from_below, 3, 0, nz)
    block = block + place_rim(from_above, 3, nz - MARGIN, nz)
    for axis, dim in (("gy", 2), ("gx", 1)):
        size = block.shape[dim] - 2 * MARGIN
        low = lax.slice_in_dim(block, 0, MARGIN, axis=dim)
        high = lax.slice_in_dim(block, size + MARGIN, size + 2 * MARGIN, axis=dim)
        block = lax.slice_in_dim(block, MARGIN, size + MARGIN, axis=dim)
        got_low = shift_from(high, axis, True)
        got_high = shift_from(low, axis, False)
        block = block + place_rim(got_low, dim, 0, size)
        block = block + place_rim(got_high, dim, size - MARGIN, size)
    return block


def joint_exchange(block, deposit, pz):
    nz = block.shape[2]

    def trade(axis, up_pieces, down_pieces):
        results = []
        for pieces, upward in ((up_pieces, True), (down_pieces, False)):
            flat = jnp.concatenate([piece.reshape(-1, 128) for piece in pieces])
            got = lax.ppermute(flat, axis, [
                ((i, (i + 1) % lax.axis_size(axis)) if upward
                 else ((i + 1) % lax.axis_size(axis), i))
                for i in range(lax.axis_size(axis))
            ])
            parts, start = [], 0
            for piece in pieces:
                rows = piece.size // 128
                parts.append(got[start : start + rows].reshape(piece.shape))
                start += rows
            results.append(parts)
        return results

    for axis, dim in AXES[:2]:
        size = block.shape[dim]
        head = lax.slice_in_dim(block, 0, MARGIN, axis=dim)
        tail = lax.slice_in_dim(block, size - MARGIN, size, axis=dim)
        low = lax.slice_in_dim(deposit, 0, MARGIN, axis=dim)
        high = lax.slice_in_dim(deposit, size + MARGIN, size + 2 * MARGIN, axis=dim)
        (below, got_low), (above, got_high) = trade(axis, [tail, high], [head, low])
        block = jnp.concatenate([below, block, above], axis=dim)
        deposit = lax.slice_in_dim(deposit, MARGIN, size + MARGIN, axis=dim)
        deposit = deposit + place_rim(got_low, dim, 0, size)
        deposit = deposit + place_rim(got_high, dim, size - MARGIN, size)
    head = block[:, :, :MARGIN]
    tail = block[:, :, nz - MARGIN :]
    upper = deposit[..., nz : nz + MARGIN]
    lower = deposit[..., pz - MARGIN :]
    (below, from_below), (above, from_above) = trade("gz", [tail, upper], [head, lower])
    gap = jnp.zeros(block.shape[:2] + (pz - nz - 2 * MARGIN,), jnp.float32)
    wrapped = jnp.concatenate([block, above, gap, below], axis=2)
    folded = deposit[..., :nz]
    folded = folded + place_rim(from_below, 2, 0, nz)
    folded = folded + place_rim(from_above, 2, nz - MARGIN, nz)
    return wrapped, folded


def body(intensity, cotangent, departure_cells, departure_fracs):
    cells = departure_cells
    fracs = departure_fracs
    nx, ny, nz = intensity.shape
    px, py, pz = nx + 2 * MARGIN, ny + 2 * MARGIN, nz + 128
    block = (nx, ny, nz)
    f32 = jnp.float32
    rolled = pltpu.VMEM((px, py, nz), f32)
    windows = pltpu.VMEM((SHIFTS, SHIFTS, px, ny, nz), f32)
    products = pltpu.VMEM((SHIFTS, SHIFTS) + block, f32)
    staged = pltpu.VMEM((SHIFTS, px, ny + 16, nz), f32)
    summed = pltpu.VMEM((SHIFTS, px, py, nz), f32)

    adjoint_padded = vmem_call(
        late_spread_kernel,
        jax.ShapeDtypeStruct((px, py, pz), f32),
        [products, staged, summed] + table_scratch(block, 3),
        cotangent, cells, fracs,
    )
    wrapped, adjoint_mid = joint_exchange(intensity, adjoint_padded, pz)
    image_mid, grad_raw = vmem_call(
        early_sample_kernel,
        (jax.ShapeDtypeStruct(block, f32), jax.ShapeDtypeStruct((3,) + block, f32)),
        [rolled, windows] + table_scratch(block, 6),
        wrapped, cells, fracs,
    )
    early_padded = vmem_call(
        early_spread_kernel,
        jax.ShapeDtypeStruct((4, px, py, pz), f32),
        [products, staged, summed] + table_scratch(block, 6),
        adjoint_mid, grad_raw, cells, fracs,
    )
    wrapped_mid = widen(image_mid, pz)
    velocity_padded = vmem_call(
        late_velocity_kernel,
        jax.ShapeDtypeStruct((3, px, py, pz), f32),
        [rolled, windows, products, staged, summed] + table_scratch(block, 9),
        wrapped_mid, cotangent, cells, fracs,
    )
    deposits = jnp.concatenate([early_padded[:1], early_padded[1:] + velocity_padded])
    folded = fold(deposits, nz)
    return (folded[0], folded[1:])


def solution(mesh):
    in_specs = (
        P("gx", "gy", "gz"),
        P("gx", "gy", "gz"),
        P(None, None, None, "gx", "gy", "gz"),
        P(None, None, None, "gx", "gy", "gz"),
    )
    out_specs = (P("gx", "gy", "gz"), P(None, "gx", "gy", "gz"))
    return jax.shard_map(body, mesh=mesh, in_specs=in_specs, out_specs=out_specs, check_vma=False)
```

```python
import functools

import jax
import jax.numpy as jnp
from jax import lax
from jax.experimental import pallas as pl
from jax.experimental.pallas import tpu as pltpu
from jax.sharding import PartitionSpec as P

MARGIN = 4
SHIFTS = 8
AXES = (("gx", 0), ("gy", 1), ("gz", 2))


def cubic_taps(fraction):
    fraction_squared = fraction * fraction
    fraction_cubed = fraction_squared * fraction
    weights = [
        0.5 * (2.0 * fraction_squared - fraction_cubed - fraction),
        0.5 * (3.0 * fraction_cubed - 5.0 * fraction_squared + 2.0),
        0.5 * (4.0 * fraction_squared - 3.0 * fraction_cubed + fraction),
        0.5 * (fraction_cubed - fraction_squared),
    ]
    slopes = [
        0.5 * (4.0 * fraction - 3.0 * fraction_squared - 1.0),
        0.5 * (9.0 * fraction_squared - 10.0 * fraction),
        0.5 * (8.0 * fraction - 9.0 * fraction_squared + 1.0),
        0.5 * (3.0 * fraction_squared - 2.0 * fraction),
    ]
    return (weights, slopes)


def build_tables(cells_ref, fracs_ref, step, section, weight_refs, slope_refs):
    for component in range(3):
        offsets = cells_ref[step, section, component]
        weights, slopes = cubic_taps(fracs_ref[step, section, component])
        for shift in range(SHIFTS):
            target = shift - 3
            summed = jnp.zeros(offsets.shape, jnp.float32)
            slope_sum = jnp.zeros(offsets.shape, jnp.float32)
            for tap_index in range(4):
                hit = offsets + (tap_index - 1) == target
                summed = summed + jnp.where(hit, weights[tap_index], 0.0)
                if slope_refs is not None:
                    slope_sum = slope_sum + jnp.where(hit, slopes[tap_index], 0.0)
            weight_refs[component][shift] = summed
            if slope_refs is not None:
                slope_refs[component][shift] = slope_sum


def roll_lanes(field, shift):
    shift = shift % field.shape[-1]
    if shift == 0:
        return field
    return pltpu.roll(field, shift, field.ndim - 1)


def sample_block(wrapped_ref, rolled_ref, window_ref, weight_refs, slope_refs, with_value):
    px, py, pz = wrapped_ref.shape
    nx, ny, nz = px - 2 * MARGIN, py - 2 * MARGIN, window_ref.shape[-1]
    field = wrapped_ref[...]
    for sz in range(SHIFTS):
        rolled_ref[...] = roll_lanes(field, 3 - sz)[:, :, :nz]
        for sy in range(SHIFTS):
            window_ref[sy, sz] = rolled_ref[:, sy + 1 : sy + 1 + ny, :]
    table_x, table_y, table_z = weight_refs
    shape = (nx, ny, nz)

    def along_y(sy, carry):
        value, grad_x, grad_y, grad_z = carry
        along_x = jnp.zeros(shape, jnp.float32)
        along_x_slope = jnp.zeros(shape, jnp.float32)
        along_x_zslope = jnp.zeros(shape, jnp.float32)
        for sx in range(SHIFTS):
            column = jnp.zeros(shape, jnp.float32)
            slope_column = jnp.zeros(shape, jnp.float32)
            for sz in range(SHIFTS):
                window = window_ref[sy, sz, sx + 1 : sx + 1 + nx]
                column = column + table_z[sz] * window
                if slope_refs is not None:
                    slope_column = slope_column + slope_refs[2][sz] * window
            along_x = along_x + table_x[sx] * column
            if slope_refs is not None:
                along_x_slope = along_x_slope + slope_refs[0][sx] * column
                along_x_zslope = along_x_zslope + table_x[sx] * slope_column
        weight_y = table_y[sy]
        if with_value:
            value = value + weight_y * along_x
        if slope_refs is not None:
            grad_x = grad_x + weight_y * along_x_slope
            grad_y = grad_y + slope_refs[1][sy] * along_x
            grad_z = grad_z + weight_y * along_x_zslope
        return value, grad_x, grad_y, grad_z

    zero = jnp.zeros(shape, jnp.float32)
    value, grad_x, grad_y, grad_z = lax.fori_loop(0, SHIFTS, along_y, (zero,) * 4)
    return value, (grad_x, grad_y, grad_z)


def spread_block(field, weight_refs, product_ref, staged_ref, summed_ref, pz):
    table_x, table_y, table_z = weight_refs
    nx, ny, nz = field.shape
    px, py = nx + 2 * MARGIN, ny + 2 * MARGIN
    for sy in range(SHIFTS):
        weighted = table_y[sy] * field
        for sx in range(SHIFTS):
            product_ref[sy, sx] = table_x[sx] * weighted
    def along_z(sz, carry):
        weight_z = table_z[sz]
        for sy in range(SHIFTS):
            rows = [None] * px
            for sx in range(SHIFTS):
                deposit = weight_z * product_ref[sy, sx]
                for x in range(nx):
                    slot = x + sx + 1
                    rows[slot] = deposit[x] if rows[slot] is None else rows[slot] + deposit[x]
            rows[0] = jnp.zeros((ny, nz), jnp.float32)
            for slot in range(px):
                staged_ref[sy, slot, 8 : 8 + ny, :] = rows[slot]
        summed = jnp.zeros((px, py, nz), jnp.float32)
        for sy in range(SHIFTS):
            summed = summed + staged_ref[sy, :, 7 - sy : 7 - sy + py, :]
        summed_ref[sz] = summed
        return carry

    lax.fori_loop(0, SHIFTS, along_z, 0)
    total = jnp.zeros((px, py, pz), jnp.float32)
    gap = jnp.zeros((px, py, pz - nz), jnp.float32)
    for sz in range(SHIFTS):
        padded = jnp.concatenate([summed_ref[sz], gap], axis=2)
        total = total + roll_lanes(padded, sz - 3)
    return total


def table_scratch(shape, count):
    return [pltpu.VMEM((SHIFTS,) + shape, jnp.float32) for _ in range(count)]


def clear_rims(staged_ref):
    staged_ref[...] = jnp.zeros(staged_ref.shape, jnp.float32)


def early_sample_kernel(wrapped_ref, cells_ref, fracs_ref, image_ref, grad_ref,
                        rolled_ref, window_ref, *tables):
    weights, slopes = tables[:3], tables[3:]
    build_tables(cells_ref, fracs_ref, 0, 1, weights, slopes)
    value, grads = sample_block(wrapped_ref, rolled_ref, window_ref, weights, slopes, True)
    image_ref[...] = value
    for component in range(3):
        grad_ref[component] = grads[component]


def late_spread_kernel(cot_ref, cells_ref, fracs_ref, out_ref, product_ref, staged_ref, summed_ref, *tables):
    build_tables(cells_ref, fracs_ref, 1, 1, tables, None)
    clear_rims(staged_ref)
    out_ref[...] = spread_block(cot_ref[...], tables, product_ref, staged_ref, summed_ref,
                                out_ref.shape[-1])


def late_velocity_kernel(wrapped_ref, cot_ref, cells_ref, fracs_ref, out_ref,
                         rolled_ref, window_ref, product_ref, staged_ref, summed_ref, *tables):
    weights, slopes, mid = tables[:3], tables[3:6], tables[6:]
    build_tables(cells_ref, fracs_ref, 1, 1, weights, slopes)
    build_tables(cells_ref, fracs_ref, 1, 0, mid, None)
    _, grads = sample_block(wrapped_ref, rolled_ref, window_ref, weights, slopes, False)
    cot = cot_ref[...]
    clear_rims(staged_ref)
    for component in range(3):
        out_ref[component] = spread_block(cot * grads[component], mid, product_ref, staged_ref, summed_ref,
                                          out_ref.shape[-1])


def early_spread_kernel(adjoint_ref, grad_ref, cells_ref, fracs_ref, out_ref,
                        product_ref, staged_ref, summed_ref, *tables):
    dep, mid = tables[:3], tables[3:]
    build_tables(cells_ref, fracs_ref, 0, 1, dep, None)
    build_tables(cells_ref, fracs_ref, 0, 0, mid, None)
    adjoint = adjoint_ref[...]
    clear_rims(staged_ref)
    pz = out_ref.shape[-1]
    out_ref[0] = spread_block(adjoint, dep, product_ref, staged_ref, summed_ref, pz)
    for component in range(3):
        out_ref[1 + component] = spread_block(adjoint * grad_ref[component], mid, product_ref,
                                              staged_ref, summed_ref, pz)


def vmem_call(kernel, out_shapes, scratch, *args):
    return pl.pallas_call(
        kernel,
        out_shape=out_shapes,
        in_specs=[pl.BlockSpec(memory_space=pltpu.VMEM)] * len(args),
        out_specs=jax.tree.map(lambda _: pl.BlockSpec(memory_space=pltpu.VMEM), out_shapes),
        scratch_shapes=scratch,
        compiler_params=pltpu.CompilerParams(vmem_limit_bytes=48 * 1024 * 1024),
        cost_estimate=pl.CostEstimate(
            flops=4_000_000_000, transcendentals=0, bytes_accessed=2_000_000
        ),
    )(*args)


def shift_from(piece, axis, upward):
    count = lax.axis_size(axis)
    if upward:
        pairs = [(i, (i + 1) % count) for i in range(count)]
    else:
        pairs = [((i + 1) % count, i) for i in range(count)]
    shape = piece.shape
    if shape[-1] < 128 and piece.size % 1024 == 0:
        flat = lax.ppermute(piece.reshape(-1, 128), axis, pairs)
        return flat.reshape(shape)
    return lax.ppermute(piece, axis, pairs)


def widen(block, pz):
    for axis, dim in AXES[:2]:
        size = block.shape[dim]
        head = lax.slice_in_dim(block, 0, MARGIN, axis=dim)
        tail = lax.slice_in_dim(block, size - MARGIN, size, axis=dim)
        block = jnp.concatenate(
            [shift_from(tail, axis, True), block, shift_from(head, axis, False)], axis=dim
        )
    nz = block.shape[2]
    head = block[:, :, :MARGIN]
    tail = block[:, :, nz - MARGIN :]
    gap = jnp.zeros(block.shape[:2] + (pz - nz - 2 * MARGIN,), jnp.float32)
    return jnp.concatenate(
        [block, shift_from(head, "gz", False), gap, shift_from(tail, "gz", True)], axis=2
    )


def place_rim(rim, dim, start, size):
    widths = [(0, 0)] * rim.ndim
    widths[dim] = (start, size - start - rim.shape[dim])
    return jnp.pad(rim, widths)


def fold(wrapped, nz):
    pz = wrapped.shape[3]
    upper = wrapped[..., nz : nz + MARGIN]
    lower = wrapped[..., pz - MARGIN :]
    block = wrapped[..., :nz]
    from_below = shift_from(upper, "gz", True)
    from_above = shift_from(lower, "gz", False)
    block = block + place_rim(from_below, 3, 0, nz)
    block = block + place_rim(from_above, 3, nz - MARGIN, nz)
    for axis, dim in (("gy", 2), ("gx", 1)):
        size = block.shape[dim] - 2 * MARGIN
        low = lax.slice_in_dim(block, 0, MARGIN, axis=dim)
        high = lax.slice_in_dim(block, size + MARGIN, size + 2 * MARGIN, axis=dim)
        block = lax.slice_in_dim(block, MARGIN, size + MARGIN, axis=dim)
        got_low = shift_from(high, axis, True)
        got_high = shift_from(low, axis, False)
        block = block + place_rim(got_low, dim, 0, size)
        block = block + place_rim(got_high, dim, size - MARGIN, size)
    return block


def body(intensity, cotangent, departure_cells, departure_fracs):
    cells = departure_cells
    fracs = departure_fracs
    nx, ny, nz = intensity.shape
    px, py, pz = nx + 2 * MARGIN, ny + 2 * MARGIN, nz + 128
    block = (nx, ny, nz)
    f32 = jnp.float32
    rolled = pltpu.VMEM((px, py, nz), f32)
    windows = pltpu.VMEM((SHIFTS, SHIFTS, px, ny, nz), f32)
    products = pltpu.VMEM((SHIFTS, SHIFTS) + block, f32)
    staged = pltpu.VMEM((SHIFTS, px, ny + 16, nz), f32)
    summed = pltpu.VMEM((SHIFTS, px, py, nz), f32)

    wrapped = widen(intensity, pz)
    image_mid, grad_raw = vmem_call(
        early_sample_kernel,
        (jax.ShapeDtypeStruct(block, f32), jax.ShapeDtypeStruct((3,) + block, f32)),
        [rolled, windows] + table_scratch(block, 6),
        wrapped, cells, fracs,
    )
    adjoint_padded = vmem_call(
        late_spread_kernel,
        jax.ShapeDtypeStruct((px, py, pz), f32),
        [products, staged, summed] + table_scratch(block, 3),
        cotangent, cells, fracs,
    )
    adjoint_mid = fold(adjoint_padded[None], nz)[0]
    early_padded = vmem_call(
        early_spread_kernel,
        jax.ShapeDtypeStruct((4, px, py, pz), f32),
        [products, staged, summed] + table_scratch(block, 6),
        adjoint_mid, grad_raw, cells, fracs,
    )
    wrapped_mid = widen(image_mid, pz)
    velocity_padded = vmem_call(
        late_velocity_kernel,
        jax.ShapeDtypeStruct((3, px, py, pz), f32),
        [rolled, windows, products, staged, summed] + table_scratch(block, 9),
        wrapped_mid, cotangent, cells, fracs,
    )
    deposits = jnp.concatenate([early_padded[:1], early_padded[1:] + velocity_padded])
    folded = fold(deposits, nz)
    return (folded[0], folded[1:])


def solution(mesh):
    in_specs = (
        P("gx", "gy", "gz"),
        P("gx", "gy", "gz"),
        P(None, None, None, "gx", "gy", "gz"),
        P(None, None, None, "gx", "gy", "gz"),
    )
    out_specs = (P("gx", "gy", "gz"), P(None, "gx", "gy", "gz"))
    return jax.shard_map(body, mesh=mesh, in_specs=in_specs, out_specs=out_specs, check_vma=False)
```

```python
import functools

import jax
import jax.numpy as jnp
from jax import lax
from jax.experimental import pallas as pl
from jax.experimental.pallas import tpu as pltpu
from jax.sharding import PartitionSpec as P

MARGIN = 4
SHIFTS = 8
AXES = (("gx", 0), ("gy", 1), ("gz", 2))


def cubic_taps(fraction):
    fraction_squared = fraction * fraction
    fraction_cubed = fraction_squared * fraction
    weights = [
        0.5 * (2.0 * fraction_squared - fraction_cubed - fraction),
        0.5 * (3.0 * fraction_cubed - 5.0 * fraction_squared + 2.0),
        0.5 * (4.0 * fraction_squared - 3.0 * fraction_cubed + fraction),
        0.5 * (fraction_cubed - fraction_squared),
    ]
    slopes = [
        0.5 * (4.0 * fraction - 3.0 * fraction_squared - 1.0),
        0.5 * (9.0 * fraction_squared - 10.0 * fraction),
        0.5 * (8.0 * fraction - 9.0 * fraction_squared + 1.0),
        0.5 * (3.0 * fraction_squared - 2.0 * fraction),
    ]
    return (weights, slopes)


def build_tables(cells_ref, fracs_ref, step, section, weight_refs, slope_refs):
    for component in range(3):
        offsets = cells_ref[step, section, component]
        weights, slopes = cubic_taps(fracs_ref[step, section, component])
        for shift in range(SHIFTS):
            target = shift - 3
            summed = jnp.zeros(offsets.shape, jnp.float32)
            slope_sum = jnp.zeros(offsets.shape, jnp.float32)
            for tap_index in range(4):
                hit = offsets + (tap_index - 1) == target
                summed = summed + jnp.where(hit, weights[tap_index], 0.0)
                if slope_refs is not None:
                    slope_sum = slope_sum + jnp.where(hit, slopes[tap_index], 0.0)
            weight_refs[component][shift] = summed
            if slope_refs is not None:
                slope_refs[component][shift] = slope_sum


def roll_lanes(field, shift):
    shift = shift % field.shape[-1]
    if shift == 0:
        return field
    return pltpu.roll(field, shift, field.ndim - 1)


def sample_block(wrapped_ref, rolled_ref, window_ref, weight_refs, slope_refs, with_value):
    px, py, pz = wrapped_ref.shape
    nx, ny, nz = px - 2 * MARGIN, py - 2 * MARGIN, window_ref.shape[-1]
    field = wrapped_ref[...]
    for sz in range(SHIFTS):
        rolled_ref[...] = roll_lanes(field, 3 - sz)[:, :, :nz]
        for sy in range(SHIFTS):
            window_ref[sy, sz] = rolled_ref[:, sy + 1 : sy + 1 + ny, :]
    table_x, table_y, table_z = weight_refs
    shape = (nx, ny, nz)

    def along_y(sy, carry):
        value, grad_x, grad_y, grad_z = carry
        along_x = jnp.zeros(shape, jnp.float32)
        along_x_slope = jnp.zeros(shape, jnp.float32)
        along_x_zslope = jnp.zeros(shape, jnp.float32)
        for sx in range(SHIFTS):
            column = jnp.zeros(shape, jnp.float32)
            slope_column = jnp.zeros(shape, jnp.float32)
            for sz in range(SHIFTS):
                window = window_ref[sy, sz, sx + 1 : sx + 1 + nx]
                column = column + table_z[sz] * window
                if slope_refs is not None:
                    slope_column = slope_column + slope_refs[2][sz] * window
            along_x = along_x + table_x[sx] * column
            if slope_refs is not None:
                along_x_slope = along_x_slope + slope_refs[0][sx] * column
                along_x_zslope = along_x_zslope + table_x[sx] * slope_column
        weight_y = table_y[sy]
        if with_value:
            value = value + weight_y * along_x
        if slope_refs is not None:
            grad_x = grad_x + weight_y * along_x_slope
            grad_y = grad_y + slope_refs[1][sy] * along_x
            grad_z = grad_z + weight_y * along_x_zslope
        return value, grad_x, grad_y, grad_z

    zero = jnp.zeros(shape, jnp.float32)
    value, grad_x, grad_y, grad_z = lax.fori_loop(0, SHIFTS, along_y, (zero,) * 4, unroll=2)
    return value, (grad_x, grad_y, grad_z)


def spread_block(field, weight_refs, product_ref, staged_ref, summed_ref, pz):
    table_x, table_y, table_z = weight_refs
    nx, ny, nz = field.shape
    px, py = nx + 2 * MARGIN, ny + 2 * MARGIN
    for sy in range(SHIFTS):
        weighted = table_y[sy] * field
        for sx in range(SHIFTS):
            product_ref[sy, sx] = table_x[sx] * weighted
    def along_z(sz, carry):
        weight_z = table_z[sz]
        for sy in range(SHIFTS):
            rows = [None] * px
            for sx in range(SHIFTS):
                deposit = weight_z * product_ref[sy, sx]
                for x in range(nx):
                    slot = x + sx + 1
                    rows[slot] = deposit[x] if rows[slot] is None else rows[slot] + deposit[x]
            rows[0] = jnp.zeros((ny, nz), jnp.float32)
            for slot in range(px):
                staged_ref[sy, slot, 8 : 8 + ny, :] = rows[slot]
        summed = jnp.zeros((px, py, nz), jnp.float32)
        for sy in range(SHIFTS):
            summed = summed + staged_ref[sy, :, 7 - sy : 7 - sy + py, :]
        summed_ref[sz] = summed
        return carry

    lax.fori_loop(0, SHIFTS, along_z, 0, unroll=2)
    total = jnp.zeros((px, py, pz), jnp.float32)
    gap = jnp.zeros((px, py, pz - nz), jnp.float32)
    for sz in range(SHIFTS):
        padded = jnp.concatenate([summed_ref[sz], gap], axis=2)
        total = total + roll_lanes(padded, sz - 3)
    return total


def table_scratch(shape, count):
    return [pltpu.VMEM((SHIFTS,) + shape, jnp.float32) for _ in range(count)]


def clear_rims(staged_ref):
    staged_ref[...] = jnp.zeros(staged_ref.shape, jnp.float32)


def early_sample_kernel(wrapped_ref, cells_ref, fracs_ref, image_ref, grad_ref,
                        rolled_ref, window_ref, *tables):
    weights, slopes = tables[:3], tables[3:]
    build_tables(cells_ref, fracs_ref, 0, 1, weights, slopes)
    value, grads = sample_block(wrapped_ref, rolled_ref, window_ref, weights, slopes, True)
    image_ref[...] = value
    for component in range(3):
        grad_ref[component] = grads[component]


def late_spread_kernel(cot_ref, cells_ref, fracs_ref, out_ref, product_ref, staged_ref, summed_ref, *tables):
    build_tables(cells_ref, fracs_ref, 1, 1, tables, None)
    clear_rims(staged_ref)
    out_ref[...] = spread_block(cot_ref[...], tables, product_ref, staged_ref, summed_ref,
                                out_ref.shape[-1])


def late_velocity_kernel(wrapped_ref, cot_ref, cells_ref, fracs_ref, out_ref,
                         rolled_ref, window_ref, product_ref, staged_ref, summed_ref, *tables):
    weights, slopes, mid = tables[:3], tables[3:6], tables[6:]
    build_tables(cells_ref, fracs_ref, 1, 1, weights, slopes)
    build_tables(cells_ref, fracs_ref, 1, 0, mid, None)
    _, grads = sample_block(wrapped_ref, rolled_ref, window_ref, weights, slopes, False)
    cot = cot_ref[...]
    clear_rims(staged_ref)
    for component in range(3):
        out_ref[component] = spread_block(cot * grads[component], mid, product_ref, staged_ref, summed_ref,
                                          out_ref.shape[-1])


def early_spread_kernel(adjoint_ref, grad_ref, cells_ref, fracs_ref, out_ref,
                        product_ref, staged_ref, summed_ref, *tables):
    dep, mid = tables[:3], tables[3:]
    build_tables(cells_ref, fracs_ref, 0, 1, dep, None)
    build_tables(cells_ref, fracs_ref, 0, 0, mid, None)
    adjoint = adjoint_ref[...]
    clear_rims(staged_ref)
    pz = out_ref.shape[-1]
    out_ref[0] = spread_block(adjoint, dep, product_ref, staged_ref, summed_ref, pz)
    for component in range(3):
        out_ref[1 + component] = spread_block(adjoint * grad_ref[component], mid, product_ref,
                                              staged_ref, summed_ref, pz)


def vmem_call(kernel, out_shapes, scratch, *args):
    return pl.pallas_call(
        kernel,
        out_shape=out_shapes,
        in_specs=[pl.BlockSpec(memory_space=pltpu.VMEM)] * len(args),
        out_specs=jax.tree.map(lambda _: pl.BlockSpec(memory_space=pltpu.VMEM), out_shapes),
        scratch_shapes=scratch,
        compiler_params=pltpu.CompilerParams(vmem_limit_bytes=48 * 1024 * 1024),
        cost_estimate=pl.CostEstimate(
            flops=40_000_000, transcendentals=0, bytes_accessed=2_000_000
        ),
    )(*args)


def shift_from(piece, axis, upward):
    count = lax.axis_size(axis)
    if upward:
        pairs = [(i, (i + 1) % count) for i in range(count)]
    else:
        pairs = [((i + 1) % count, i) for i in range(count)]
    shape = piece.shape
    if shape[-1] < 128 and piece.size % 1024 == 0:
        flat = lax.ppermute(piece.reshape(-1, 128), axis, pairs)
        return flat.reshape(shape)
    return lax.ppermute(piece, axis, pairs)


def widen(block, pz):
    for axis, dim in AXES[:2]:
        size = block.shape[dim]
        head = lax.slice_in_dim(block, 0, MARGIN, axis=dim)
        tail = lax.slice_in_dim(block, size - MARGIN, size, axis=dim)
        block = jnp.concatenate(
            [shift_from(tail, axis, True), block, shift_from(head, axis, False)], axis=dim
        )
    nz = block.shape[2]
    head = block[:, :, :MARGIN]
    tail = block[:, :, nz - MARGIN :]
    gap = jnp.zeros(block.shape[:2] + (pz - nz - 2 * MARGIN,), jnp.float32)
    return jnp.concatenate(
        [block, shift_from(head, "gz", False), gap, shift_from(tail, "gz", True)], axis=2
    )


def place_rim(rim, dim, start, size):
    widths = [(0, 0)] * rim.ndim
    widths[dim] = (start, size - start - rim.shape[dim])
    return jnp.pad(rim, widths)


def fold(wrapped, nz):
    pz = wrapped.shape[3]
    upper = wrapped[..., nz : nz + MARGIN]
    lower = wrapped[..., pz - MARGIN :]
    block = wrapped[..., :nz]
    from_below = shift_from(upper, "gz", True)
    from_above = shift_from(lower, "gz", False)
    block = block + place_rim(from_below, 3, 0, nz)
    block = block + place_rim(from_above, 3, nz - MARGIN, nz)
    for axis, dim in (("gy", 2), ("gx", 1)):
        size = block.shape[dim] - 2 * MARGIN
        low = lax.slice_in_dim(block, 0, MARGIN, axis=dim)
        high = lax.slice_in_dim(block, size + MARGIN, size + 2 * MARGIN, axis=dim)
        block = lax.slice_in_dim(block, MARGIN, size + MARGIN, axis=dim)
        got_low = shift_from(high, axis, True)
        got_high = shift_from(low, axis, False)
        block = block + place_rim(got_low, dim, 0, size)
        block = block + place_rim(got_high, dim, size - MARGIN, size)
    return block


def body(intensity, cotangent, departure_cells, departure_fracs):
    cells = departure_cells
    fracs = departure_fracs
    nx, ny, nz = intensity.shape
    px, py, pz = nx + 2 * MARGIN, ny + 2 * MARGIN, nz + 128
    block = (nx, ny, nz)
    f32 = jnp.float32
    rolled = pltpu.VMEM((px, py, nz), f32)
    windows = pltpu.VMEM((SHIFTS, SHIFTS, px, ny, nz), f32)
    products = pltpu.VMEM((SHIFTS, SHIFTS) + block, f32)
    staged = pltpu.VMEM((SHIFTS, px, ny + 16, nz), f32)
    summed = pltpu.VMEM((SHIFTS, px, py, nz), f32)

    wrapped = widen(intensity, pz)
    image_mid, grad_raw = vmem_call(
        early_sample_kernel,
        (jax.ShapeDtypeStruct(block, f32), jax.ShapeDtypeStruct((3,) + block, f32)),
        [rolled, windows] + table_scratch(block, 6),
        wrapped, cells, fracs,
    )
    adjoint_padded = vmem_call(
        late_spread_kernel,
        jax.ShapeDtypeStruct((px, py, pz), f32),
        [products, staged, summed] + table_scratch(block, 3),
        cotangent, cells, fracs,
    )
    adjoint_mid = fold(adjoint_padded[None], nz)[0]
    early_padded = vmem_call(
        early_spread_kernel,
        jax.ShapeDtypeStruct((4, px, py, pz), f32),
        [products, staged, summed] + table_scratch(block, 6),
        adjoint_mid, grad_raw, cells, fracs,
    )
    wrapped_mid = widen(image_mid, pz)
    velocity_padded = vmem_call(
        late_velocity_kernel,
        jax.ShapeDtypeStruct((3, px, py, pz), f32),
        [rolled, windows, products, staged, summed] + table_scratch(block, 9),
        wrapped_mid, cotangent, cells, fracs,
    )
    deposits = jnp.concatenate([early_padded[:1], early_padded[1:] + velocity_padded])
    folded = fold(deposits, nz)
    return (folded[0], folded[1:])


def solution(mesh):
    in_specs = (
        P("gx", "gy", "gz"),
        P("gx", "gy", "gz"),
        P(None, None, None, "gx", "gy", "gz"),
        P(None, None, None, "gx", "gy", "gz"),
    )
    out_specs = (P("gx", "gy", "gz"), P(None, "gx", "gy", "gz"))
    return jax.shard_map(body, mesh=mesh, in_specs=in_specs, out_specs=out_specs, check_vma=False)
```

```python
import functools

import jax
import jax.numpy as jnp
from jax import lax
from jax.experimental import pallas as pl
from jax.experimental.pallas import tpu as pltpu
from jax.sharding import PartitionSpec as P

MARGIN = 4
SHIFTS = 8
AXES = (("gx", 0), ("gy", 1), ("gz", 2))


def cubic_taps(fraction):
    fraction_squared = fraction * fraction
    fraction_cubed = fraction_squared * fraction
    weights = [
        0.5 * (2.0 * fraction_squared - fraction_cubed - fraction),
        0.5 * (3.0 * fraction_cubed - 5.0 * fraction_squared + 2.0),
        0.5 * (4.0 * fraction_squared - 3.0 * fraction_cubed + fraction),
        0.5 * (fraction_cubed - fraction_squared),
    ]
    slopes = [
        0.5 * (4.0 * fraction - 3.0 * fraction_squared - 1.0),
        0.5 * (9.0 * fraction_squared - 10.0 * fraction),
        0.5 * (8.0 * fraction - 9.0 * fraction_squared + 1.0),
        0.5 * (3.0 * fraction_squared - 2.0 * fraction),
    ]
    return (weights, slopes)


def build_tables(cells_ref, fracs_ref, step, section, weight_refs, slope_refs):
    for component in range(3):
        offsets = cells_ref[step, section, component]
        weights, slopes = cubic_taps(fracs_ref[step, section, component])
        for shift in range(SHIFTS):
            target = shift - 3
            summed = jnp.zeros(offsets.shape, jnp.float32)
            slope_sum = jnp.zeros(offsets.shape, jnp.float32)
            for tap_index in range(4):
                hit = offsets + (tap_index - 1) == target
                summed = summed + jnp.where(hit, weights[tap_index], 0.0)
                if slope_refs is not None:
                    slope_sum = slope_sum + jnp.where(hit, slopes[tap_index], 0.0)
            weight_refs[component][shift] = summed
            if slope_refs is not None:
                slope_refs[component][shift] = slope_sum


def roll_lanes(field, shift):
    shift = shift % field.shape[-1]
    if shift == 0:
        return field
    return pltpu.roll(field, shift, field.ndim - 1)


def sample_block(wrapped_ref, rolled_ref, window_ref, weight_refs, slope_refs, with_value):
    px, py, pz = wrapped_ref.shape
    nx, ny, nz = px - 2 * MARGIN, py - 2 * MARGIN, window_ref.shape[-1]
    field = wrapped_ref[...]
    for sz in range(SHIFTS):
        rolled_ref[...] = roll_lanes(field, 3 - sz)[:, :, :nz]
        for sy in range(SHIFTS):
            window_ref[sy, sz] = rolled_ref[:, sy + 1 : sy + 1 + ny, :]
    table_x, table_y, table_z = weight_refs
    shape = (nx, ny, nz)

    def along_y(sy, carry):
        value, grad_x, grad_y, grad_z = carry
        along_x = jnp.zeros(shape, jnp.float32)
        along_x_slope = jnp.zeros(shape, jnp.float32)
        along_x_zslope = jnp.zeros(shape, jnp.float32)
        for sx in range(SHIFTS):
            column = jnp.zeros(shape, jnp.float32)
            slope_column = jnp.zeros(shape, jnp.float32)
            for sz in range(SHIFTS):
                window = window_ref[sy, sz, sx + 1 : sx + 1 + nx]
                column = column + table_z[sz] * window
                if slope_refs is not None:
                    slope_column = slope_column + slope_refs[2][sz] * window
            along_x = along_x + table_x[sx] * column
            if slope_refs is not None:
                along_x_slope = along_x_slope + slope_refs[0][sx] * column
                along_x_zslope = along_x_zslope + table_x[sx] * slope_column
        weight_y = table_y[sy]
        if with_value:
            value = value + weight_y * along_x
        if slope_refs is not None:
            grad_x = grad_x + weight_y * along_x_slope
            grad_y = grad_y + slope_refs[1][sy] * along_x
            grad_z = grad_z + weight_y * along_x_zslope
        return value, grad_x, grad_y, grad_z

    zero = jnp.zeros(shape, jnp.float32)
    value, grad_x, grad_y, grad_z = lax.fori_loop(0, SHIFTS, along_y, (zero,) * 4)
    return value, (grad_x, grad_y, grad_z)


def spread_block(field, weight_refs, product_ref, staged_ref, summed_ref, pz):
    table_x, table_y, table_z = weight_refs
    nx, ny, nz = field.shape
    px, py = nx + 2 * MARGIN, ny + 2 * MARGIN
    for sy in range(SHIFTS):
        weighted = table_y[sy] * field
        for sx in range(SHIFTS):
            product_ref[sy, sx] = table_x[sx] * weighted
    def along_z(sz, carry):
        weight_z = table_z[sz]
        for sy in range(SHIFTS):
            rows = [None] * px
            for sx in range(SHIFTS):
                deposit = weight_z * product_ref[sy, sx]
                for x in range(nx):
                    slot = x + sx + 1
                    rows[slot] = deposit[x] if rows[slot] is None else rows[slot] + deposit[x]
            rows[0] = jnp.zeros((ny, nz), jnp.float32)
            for slot in range(px):
                staged_ref[sy, slot, 8 : 8 + ny, :] = rows[slot]
        summed = jnp.zeros((px, py, nz), jnp.float32)
        for sy in range(SHIFTS):
            summed = summed + staged_ref[sy, :, 7 - sy : 7 - sy + py, :]
        summed_ref[sz] = summed
        return carry

    lax.fori_loop(0, SHIFTS, along_z, 0)
    total = jnp.zeros((px, py, pz), jnp.float32)
    gap = jnp.zeros((px, py, pz - nz), jnp.float32)
    for sz in range(SHIFTS):
        padded = jnp.concatenate([summed_ref[sz], gap], axis=2)
        total = total + roll_lanes(padded, sz - 3)
    return total


def table_scratch(shape, count):
    return [pltpu.VMEM((SHIFTS,) + shape, jnp.float32) for _ in range(count)]


def clear_rims(staged_ref):
    staged_ref[...] = jnp.zeros(staged_ref.shape, jnp.float32)


def early_sample_kernel(wrapped_ref, cells_ref, fracs_ref, image_ref, rolled_ref, window_ref,
                        *tables):
    build_tables(cells_ref, fracs_ref, 0, 1, tables, None)
    value, _ = sample_block(wrapped_ref, rolled_ref, window_ref, tables, None, True)
    image_ref[...] = value


def late_spread_kernel(cot_ref, cells_ref, fracs_ref, out_ref, product_ref, staged_ref, summed_ref, *tables):
    build_tables(cells_ref, fracs_ref, 1, 1, tables, None)
    clear_rims(staged_ref)
    out_ref[...] = spread_block(cot_ref[...], tables, product_ref, staged_ref, summed_ref,
                                out_ref.shape[-1])


def late_velocity_kernel(wrapped_ref, cot_ref, cells_ref, fracs_ref, out_ref,
                         rolled_ref, window_ref, product_ref, staged_ref, summed_ref, *tables):
    weights, slopes, mid = tables[:3], tables[3:6], tables[6:]
    build_tables(cells_ref, fracs_ref, 1, 1, weights, slopes)
    build_tables(cells_ref, fracs_ref, 1, 0, mid, None)
    _, grads = sample_block(wrapped_ref, rolled_ref, window_ref, weights, slopes, False)
    cot = cot_ref[...]
    clear_rims(staged_ref)
    for component in range(3):
        out_ref[component] = spread_block(cot * grads[component], mid, product_ref, staged_ref, summed_ref,
                                          out_ref.shape[-1])


def early_spread_kernel(adjoint_ref, wrapped_ref, cells_ref, fracs_ref, out_ref, rolled_ref,
                        window_ref, product_ref, staged_ref, summed_ref, *tables):
    dep, slopes, mid = tables[:3], tables[3:6], tables[6:]
    build_tables(cells_ref, fracs_ref, 0, 1, dep, slopes)
    build_tables(cells_ref, fracs_ref, 0, 0, mid, None)
    _, grads = sample_block(wrapped_ref, rolled_ref, window_ref, dep, slopes, False)
    adjoint = adjoint_ref[...]
    clear_rims(staged_ref)
    pz = out_ref.shape[-1]
    out_ref[0] = spread_block(adjoint, dep, product_ref, staged_ref, summed_ref, pz)
    for component in range(3):
        out_ref[1 + component] = spread_block(adjoint * grads[component], mid, product_ref,
                                              staged_ref, summed_ref, pz)


def vmem_call(kernel, out_shapes, scratch, *args):
    return pl.pallas_call(
        kernel,
        out_shape=out_shapes,
        in_specs=[pl.BlockSpec(memory_space=pltpu.VMEM)] * len(args),
        out_specs=jax.tree.map(lambda _: pl.BlockSpec(memory_space=pltpu.VMEM), out_shapes),
        scratch_shapes=scratch,
        compiler_params=pltpu.CompilerParams(vmem_limit_bytes=48 * 1024 * 1024),
        cost_estimate=pl.CostEstimate(
            flops=40_000_000, transcendentals=0, bytes_accessed=2_000_000
        ),
    )(*args)


def shift_from(piece, axis, upward):
    count = lax.axis_size(axis)
    if upward:
        pairs = [(i, (i + 1) % count) for i in range(count)]
    else:
        pairs = [((i + 1) % count, i) for i in range(count)]
    shape = piece.shape
    if shape[-1] < 128 and piece.size % 1024 == 0:
        flat = lax.ppermute(piece.reshape(-1, 128), axis, pairs)
        return flat.reshape(shape)
    return lax.ppermute(piece, axis, pairs)


def widen(block, pz):
    for axis, dim in AXES[:2]:
        size = block.shape[dim]
        head = lax.slice_in_dim(block, 0, MARGIN, axis=dim)
        tail = lax.slice_in_dim(block, size - MARGIN, size, axis=dim)
        block = jnp.concatenate(
            [shift_from(tail, axis, True), block, shift_from(head, axis, False)], axis=dim
        )
    nz = block.shape[2]
    head = block[:, :, :MARGIN]
    tail = block[:, :, nz - MARGIN :]
    gap = jnp.zeros(block.shape[:2] + (pz - nz - 2 * MARGIN,), jnp.float32)
    return jnp.concatenate(
        [block, shift_from(head, "gz", False), gap, shift_from(tail, "gz", True)], axis=2
    )


def place_rim(rim, dim, start, size):
    widths = [(0, 0)] * rim.ndim
    widths[dim] = (start, size - start - rim.shape[dim])
    return jnp.pad(rim, widths)


def fold(wrapped, nz):
    pz = wrapped.shape[3]
    upper = wrapped[..., nz : nz + MARGIN]
    lower = wrapped[..., pz - MARGIN :]
    block = wrapped[..., :nz]
    from_below = shift_from(upper, "gz", True)
    from_above = shift_from(lower, "gz", False)
    block = block + place_rim(from_below, 3, 0, nz)
    block = block + place_rim(from_above, 3, nz - MARGIN, nz)
    for axis, dim in (("gy", 2), ("gx", 1)):
        size = block.shape[dim] - 2 * MARGIN
        low = lax.slice_in_dim(block, 0, MARGIN, axis=dim)
        high = lax.slice_in_dim(block, size + MARGIN, size + 2 * MARGIN, axis=dim)
        block = lax.slice_in_dim(block, MARGIN, size + MARGIN, axis=dim)
        got_low = shift_from(high, axis, True)
        got_high = shift_from(low, axis, False)
        block = block + place_rim(got_low, dim, 0, size)
        block = block + place_rim(got_high, dim, size - MARGIN, size)
    return block


def body(intensity, cotangent, departure_cells, departure_fracs):
    cells = departure_cells
    fracs = departure_fracs
    nx, ny, nz = intensity.shape
    px, py, pz = nx + 2 * MARGIN, ny + 2 * MARGIN, nz + 128
    block = (nx, ny, nz)
    f32 = jnp.float32
    rolled = pltpu.VMEM((px, py, nz), f32)
    windows = pltpu.VMEM((SHIFTS, SHIFTS, px, ny, nz), f32)
    products = pltpu.VMEM((SHIFTS, SHIFTS) + block, f32)
    staged = pltpu.VMEM((SHIFTS, px, ny + 16, nz), f32)
    summed = pltpu.VMEM((SHIFTS, px, py, nz), f32)

    wrapped = widen(intensity, pz)
    image_mid = vmem_call(
        early_sample_kernel,
        jax.ShapeDtypeStruct(block, f32),
        [rolled, windows] + table_scratch(block, 3),
        wrapped, cells, fracs,
    )
    adjoint_padded = vmem_call(
        late_spread_kernel,
        jax.ShapeDtypeStruct((px, py, pz), f32),
        [products, staged, summed] + table_scratch(block, 3),
        cotangent, cells, fracs,
    )
    adjoint_mid = fold(adjoint_padded[None], nz)[0]
    early_padded = vmem_call(
        early_spread_kernel,
        jax.ShapeDtypeStruct((4, px, py, pz), f32),
        [rolled, windows, products, staged, summed] + table_scratch(block, 9),
        adjoint_mid, wrapped, cells, fracs,
    )
    wrapped_mid = widen(image_mid, pz)
    velocity_padded = vmem_call(
        late_velocity_kernel,
        jax.ShapeDtypeStruct((3, px, py, pz), f32),
        [rolled, windows, products, staged, summed] + table_scratch(block, 9),
        wrapped_mid, cotangent, cells, fracs,
    )
    deposits = jnp.concatenate([early_padded[:1], early_padded[1:] + velocity_padded])
    folded = fold(deposits, nz)
    return (folded[0], folded[1:])


def solution(mesh):
    in_specs = (
        P("gx", "gy", "gz"),
        P("gx", "gy", "gz"),
        P(None, None, None, "gx", "gy", "gz"),
        P(None, None, None, "gx", "gy", "gz"),
    )
    out_specs = (P("gx", "gy", "gz"), P(None, "gx", "gy", "gz"))
    return jax.shard_map(body, mesh=mesh, in_specs=in_specs, out_specs=out_specs, check_vma=False)
```

```python
import functools

import jax
import jax.numpy as jnp
from jax import lax
from jax.experimental import pallas as pl
from jax.experimental.pallas import tpu as pltpu
from jax.sharding import PartitionSpec as P

MARGIN = 4
SHIFTS = 8
AXES = (("gx", 0), ("gy", 1), ("gz", 2))


def cubic_taps(fraction):
    fraction_squared = fraction * fraction
    fraction_cubed = fraction_squared * fraction
    weights = [
        0.5 * (2.0 * fraction_squared - fraction_cubed - fraction),
        0.5 * (3.0 * fraction_cubed - 5.0 * fraction_squared + 2.0),
        0.5 * (4.0 * fraction_squared - 3.0 * fraction_cubed + fraction),
        0.5 * (fraction_cubed - fraction_squared),
    ]
    slopes = [
        0.5 * (4.0 * fraction - 3.0 * fraction_squared - 1.0),
        0.5 * (9.0 * fraction_squared - 10.0 * fraction),
        0.5 * (8.0 * fraction - 9.0 * fraction_squared + 1.0),
        0.5 * (3.0 * fraction_squared - 2.0 * fraction),
    ]
    return (weights, slopes)


def build_tables(cells_ref, fracs_ref, step, section, weight_refs, slope_refs):
    for component in range(3):
        offsets = cells_ref[step, section, component]
        weights, slopes = cubic_taps(fracs_ref[step, section, component])
        for shift in range(SHIFTS):
            target = shift - 3
            summed = jnp.zeros(offsets.shape, jnp.float32)
            slope_sum = jnp.zeros(offsets.shape, jnp.float32)
            for tap_index in range(4):
                hit = offsets + (tap_index - 1) == target
                summed = summed + jnp.where(hit, weights[tap_index], 0.0)
                if slope_refs is not None:
                    slope_sum = slope_sum + jnp.where(hit, slopes[tap_index], 0.0)
            weight_refs[component][shift] = summed
            if slope_refs is not None:
                slope_refs[component][shift] = slope_sum


def roll_lanes(field, shift):
    shift = shift % field.shape[-1]
    if shift == 0:
        return field
    return pltpu.roll(field, shift, field.ndim - 1)


def sample_block(wrapped_ref, rolled_ref, window_ref, weight_refs, slope_refs, with_value):
    px, py, pz = wrapped_ref.shape
    nx, ny, nz = px - 2 * MARGIN, py - 2 * MARGIN, window_ref.shape[-1]
    field = wrapped_ref[...]
    for sz in range(SHIFTS):
        rolled_ref[...] = roll_lanes(field, 3 - sz)[:, :, :nz]
        for sy in range(SHIFTS):
            window_ref[sy, sz] = rolled_ref[:, sy + 1 : sy + 1 + ny, :]
    table_x, table_y, table_z = weight_refs
    shape = (nx, ny, nz)

    def along_y(sy, carry):
        value, grad_x, grad_y, grad_z = carry
        along_x = jnp.zeros(shape, jnp.float32)
        along_x_slope = jnp.zeros(shape, jnp.float32)
        along_x_zslope = jnp.zeros(shape, jnp.float32)
        for sx in range(SHIFTS):
            column = jnp.zeros(shape, jnp.float32)
            slope_column = jnp.zeros(shape, jnp.float32)
            for sz in range(SHIFTS):
                window = window_ref[sy, sz, sx + 1 : sx + 1 + nx]
                column = column + table_z[sz] * window
                if slope_refs is not None:
                    slope_column = slope_column + slope_refs[2][sz] * window
            along_x = along_x + table_x[sx] * column
            if slope_refs is not None:
                along_x_slope = along_x_slope + slope_refs[0][sx] * column
                along_x_zslope = along_x_zslope + table_x[sx] * slope_column
        weight_y = table_y[sy]
        if with_value:
            value = value + weight_y * along_x
        if slope_refs is not None:
            grad_x = grad_x + weight_y * along_x_slope
            grad_y = grad_y + slope_refs[1][sy] * along_x
            grad_z = grad_z + weight_y * along_x_zslope
        return value, grad_x, grad_y, grad_z

    zero = jnp.zeros(shape, jnp.float32)
    value, grad_x, grad_y, grad_z = lax.fori_loop(0, SHIFTS, along_y, (zero,) * 4)
    return value, (grad_x, grad_y, grad_z)


def spread_block(field, weight_refs, product_ref, staged_ref, summed_ref, pz):
    table_x, table_y, table_z = weight_refs
    nx, ny, nz = field.shape
    px, py = nx + 2 * MARGIN, ny + 2 * MARGIN
    for sy in range(SHIFTS):
        weighted = table_y[sy] * field
        for sx in range(SHIFTS):
            product_ref[sy, sx] = table_x[sx] * weighted
    def along_z(sz, carry):
        weight_z = table_z[sz]
        for sy in range(SHIFTS):
            rows = [None] * px
            for sx in range(SHIFTS):
                deposit = weight_z * product_ref[sy, sx]
                for x in range(nx):
                    slot = x + sx + 1
                    rows[slot] = deposit[x] if rows[slot] is None else rows[slot] + deposit[x]
            rows[0] = jnp.zeros((ny, nz), jnp.float32)
            for slot in range(px):
                staged_ref[sy, slot, 8 : 8 + ny, :] = rows[slot]
        summed = jnp.zeros((px, py, nz), jnp.float32)
        for sy in range(SHIFTS):
            summed = summed + staged_ref[sy, :, 7 - sy : 7 - sy + py, :]
        summed_ref[sz] = summed
        return carry

    lax.fori_loop(0, SHIFTS, along_z, 0)
    total = jnp.zeros((px, py, pz), jnp.float32)
    gap = jnp.zeros((px, py, pz - nz), jnp.float32)
    for sz in range(SHIFTS):
        padded = jnp.concatenate([summed_ref[sz], gap], axis=2)
        total = total + roll_lanes(padded, sz - 3)
    return total


def table_scratch(shape, count):
    return [pltpu.VMEM((SHIFTS,) + shape, jnp.float32) for _ in range(count)]


def clear_rims(staged_ref):
    staged_ref[...] = jnp.zeros(staged_ref.shape, jnp.float32)


def early_sample_kernel(wrapped_ref, cells_ref, fracs_ref, image_ref, grad_ref,
                        rolled_ref, window_ref, *tables):
    weights, slopes = tables[:3], tables[3:]
    build_tables(cells_ref, fracs_ref, 0, 1, weights, slopes)
    value, grads = sample_block(wrapped_ref, rolled_ref, window_ref, weights, slopes, True)
    image_ref[...] = value
    for component in range(3):
        grad_ref[component] = grads[component]


def late_spread_kernel(cot_ref, cells_ref, fracs_ref, out_ref, product_ref, staged_ref, summed_ref, *tables):
    build_tables(cells_ref, fracs_ref, 1, 1, tables, None)
    clear_rims(staged_ref)
    out_ref[...] = spread_block(cot_ref[...], tables, product_ref, staged_ref, summed_ref,
                                out_ref.shape[-1])


def late_velocity_kernel(wrapped_ref, cot_ref, early_ref, cells_ref, fracs_ref, out_ref,
                         rolled_ref, window_ref, product_ref, staged_ref, summed_ref, *tables):
    weights, slopes, mid = tables[:3], tables[3:6], tables[6:]
    build_tables(cells_ref, fracs_ref, 1, 1, weights, slopes)
    build_tables(cells_ref, fracs_ref, 1, 0, mid, None)
    _, grads = sample_block(wrapped_ref, rolled_ref, window_ref, weights, slopes, False)
    cot = cot_ref[...]
    clear_rims(staged_ref)
    out_ref[0] = early_ref[0]
    for component in range(3):
        out_ref[1 + component] = early_ref[1 + component] + spread_block(
            cot * grads[component], mid, product_ref, staged_ref, summed_ref, out_ref.shape[-1])


def early_spread_kernel(adjoint_ref, grad_ref, cells_ref, fracs_ref, out_ref,
                        product_ref, staged_ref, summed_ref, *tables):
    dep, mid = tables[:3], tables[3:]
    build_tables(cells_ref, fracs_ref, 0, 1, dep, None)
    build_tables(cells_ref, fracs_ref, 0, 0, mid, None)
    adjoint = adjoint_ref[...]
    clear_rims(staged_ref)
    pz = out_ref.shape[-1]
    out_ref[0] = spread_block(adjoint, dep, product_ref, staged_ref, summed_ref, pz)
    for component in range(3):
        out_ref[1 + component] = spread_block(adjoint * grad_ref[component], mid, product_ref,
                                              staged_ref, summed_ref, pz)


def vmem_call(kernel, out_shapes, scratch, *args):
    return pl.pallas_call(
        kernel,
        out_shape=out_shapes,
        in_specs=[pl.BlockSpec(memory_space=pltpu.VMEM)] * len(args),
        out_specs=jax.tree.map(lambda _: pl.BlockSpec(memory_space=pltpu.VMEM), out_shapes),
        scratch_shapes=scratch,
        compiler_params=pltpu.CompilerParams(vmem_limit_bytes=48 * 1024 * 1024),
        cost_estimate=pl.CostEstimate(
            flops=40_000_000, transcendentals=0, bytes_accessed=2_000_000
        ),
    )(*args)


def shift_from(piece, axis, upward):
    count = lax.axis_size(axis)
    if upward:
        pairs = [(i, (i + 1) % count) for i in range(count)]
    else:
        pairs = [((i + 1) % count, i) for i in range(count)]
    shape = piece.shape
    if shape[-1] < 128 and piece.size % 1024 == 0:
        flat = lax.ppermute(piece.reshape(-1, 128), axis, pairs)
        return flat.reshape(shape)
    return lax.ppermute(piece, axis, pairs)


def widen(block, pz):
    for axis, dim in AXES[:2]:
        size = block.shape[dim]
        head = lax.slice_in_dim(block, 0, MARGIN, axis=dim)
        tail = lax.slice_in_dim(block, size - MARGIN, size, axis=dim)
        block = jnp.concatenate(
            [shift_from(tail, axis, True), block, shift_from(head, axis, False)], axis=dim
        )
    nz = block.shape[2]
    head = block[:, :, :MARGIN]
    tail = block[:, :, nz - MARGIN :]
    gap = jnp.zeros(block.shape[:2] + (pz - nz - 2 * MARGIN,), jnp.float32)
    return jnp.concatenate(
        [block, shift_from(head, "gz", False), gap, shift_from(tail, "gz", True)], axis=2
    )


def place_rim(rim, dim, start, size):
    widths = [(0, 0)] * rim.ndim
    widths[dim] = (start, size - start - rim.shape[dim])
    return jnp.pad(rim, widths)


def fold(wrapped, nz):
    pz = wrapped.shape[3]
    upper = wrapped[..., nz : nz + MARGIN]
    lower = wrapped[..., pz - MARGIN :]
    block = wrapped[..., :nz]
    from_below = shift_from(upper, "gz", True)
    from_above = shift_from(lower, "gz", False)
    block = block + place_rim(from_below, 3, 0, nz)
    block = block + place_rim(from_above, 3, nz - MARGIN, nz)
    for axis, dim in (("gy", 2), ("gx", 1)):
        size = block.shape[dim] - 2 * MARGIN
        low = lax.slice_in_dim(block, 0, MARGIN, axis=dim)
        high = lax.slice_in_dim(block, size + MARGIN, size + 2 * MARGIN, axis=dim)
        block = lax.slice_in_dim(block, MARGIN, size + MARGIN, axis=dim)
        got_low = shift_from(high, axis, True)
        got_high = shift_from(low, axis, False)
        block = block + place_rim(got_low, dim, 0, size)
        block = block + place_rim(got_high, dim, size - MARGIN, size)
    return block


def body(intensity, cotangent, departure_cells, departure_fracs):
    cells = departure_cells
    fracs = departure_fracs
    nx, ny, nz = intensity.shape
    px, py, pz = nx + 2 * MARGIN, ny + 2 * MARGIN, nz + 128
    block = (nx, ny, nz)
    f32 = jnp.float32
    rolled = pltpu.VMEM((px, py, nz), f32)
    windows = pltpu.VMEM((SHIFTS, SHIFTS, px, ny, nz), f32)
    products = pltpu.VMEM((SHIFTS, SHIFTS) + block, f32)
    staged = pltpu.VMEM((SHIFTS, px, ny + 16, nz), f32)
    summed = pltpu.VMEM((SHIFTS, px, py, nz), f32)

    wrapped = widen(intensity, pz)
    image_mid, grad_raw = vmem_call(
        early_sample_kernel,
        (jax.ShapeDtypeStruct(block, f32), jax.ShapeDtypeStruct((3,) + block, f32)),
        [rolled, windows] + table_scratch(block, 6),
        wrapped, cells, fracs,
    )
    adjoint_padded = vmem_call(
        late_spread_kernel,
        jax.ShapeDtypeStruct((px, py, pz), f32),
        [products, staged, summed] + table_scratch(block, 3),
        cotangent, cells, fracs,
    )
    adjoint_mid = fold(adjoint_padded[None], nz)[0]
    early_padded = vmem_call(
        early_spread_kernel,
        jax.ShapeDtypeStruct((4, px, py, pz), f32),
        [products, staged, summed] + table_scratch(block, 6),
        adjoint_mid, grad_raw, cells, fracs,
    )
    wrapped_mid = widen(image_mid, pz)
    velocity_padded = vmem_call(
        late_velocity_kernel,
        jax.ShapeDtypeStruct((4, px, py, pz), f32),
        [rolled, windows, products, staged, summed] + table_scratch(block, 9),
        wrapped_mid, cotangent, early_padded, cells, fracs,
    )
    folded = fold(velocity_padded, nz)
    return (folded[0], folded[1:])


def solution(mesh):
    in_specs = (
        P("gx", "gy", "gz"),
        P("gx", "gy", "gz"),
        P(None, None, None, "gx", "gy", "gz"),
        P(None, None, None, "gx", "gy", "gz"),
    )
    out_specs = (P("gx", "gy", "gz"), P(None, "gx", "gy", "gz"))
    return jax.shard_map(body, mesh=mesh, in_specs=in_specs, out_specs=out_specs, check_vma=False)
```
